256 devices in a mesh: inner: 16 (over x, y), outer: 16 (over z, core).
Axes of the slice: x: 4, y: 4, z: 8, core: 2. Of those that a mesh axis runs over, the one named last changes fastest.
Arguments:
- jac: float32 [4096, 256, 256], P(('outer', 'inner')), may hold values from -0.5 to 1
- obs: float32 [4096, 256], P(('outer', 'inner')), may hold values from -6 to 6
- gain_filter: float32 [256], replicated, may hold values from 0 to 0.1
- gain_smooth: float32 [256, 256], replicated, may hold values from -0.5 to 1
- init_mean: float32 [256], replicated, may hold values from -6 to 6
Outputs:
- filtered: float32 [4096, 256], P(('outer', 'inner'))
- smoothed: float32 [4096, 256], P(('outer', 'inner'))
The draws below stay inside these ranges and needn't reach their ends.
All inputs are finite; a program needn't handle non-finite values.
Results may differ from the reference program's by a relative error of at most 0.0003.
Values sent between devices are 32-bit elements; how exact they have to be, the bound alone decides.
No kernel may reach another device: no remote copies, remote signals or barrier semaphores. Data moves between devices by JAX's collectives and lax.ppermute only.
A program may use at most 64 MiB of HBM per device.

```python
import math
import jax
import jax.numpy as jnp
from jax import lax

N = 256
TSTEPS = 4096


def channel_rates(seed_key, share):
    keys = jax.random.split(jax.random.fold_in(seed_key, 7), 5)
    slow_mask = jax.random.uniform(keys[0], (N,), jnp.float32) < share
    slow_decay = jax.random.uniform(keys[1], (N,), jnp.float32, 0.1, 1.0) / TSTEPS
    fast_decay = jnp.exp(jax.random.uniform(keys[2], (N,), jnp.float32, math.log(0.01), math.log(0.05)))
    slow_gain = jax.random.uniform(keys[3], (N,), jnp.float32, 0.05, 0.5) / TSTEPS
    fast_gain = jnp.exp(jax.random.uniform(keys[4], (N,), jnp.float32, math.log(0.01), math.log(0.1)))
    return (jnp.where(slow_mask, slow_decay, fast_decay), jnp.where(slow_mask, slow_gain, fast_gain))


def draw_jac(key, part):
    share = 0.5
    decay, unused_gain = channel_rates(key, share)
    keys = jax.random.split(jax.random.fold_in(key, 11), 3)
    rough = jnp.exp(jax.random.uniform(keys[0], (TSTEPS, N), jnp.float32, math.log(0.5), math.log(2.0)))
    spots = jax.random.randint(keys[1], (4,), 0, TSTEPS)
    hits = jnp.any(jnp.arange(TSTEPS)[:, None] == spots[None, :], axis=1)
    diagonal = (1.0 - decay[None, :] * rough) * jnp.where(hits, 0.75, 1.0)[:, None]
    noise = jax.random.normal(keys[2], (TSTEPS, N, N), jnp.float32) * (0.015 / math.sqrt(2.0 * N))
    skewed = noise - jnp.swapaxes(noise, 1, 2)
    result = skewed + diagonal[:, :, None] * jnp.eye(N, dtype=jnp.float32)[None]
    return result.astype(jnp.float32)


def draw_gain_filter(key, part):
    share = 0.5
    unused_decay, gains = channel_rates(key, share)
    return gains.astype(jnp.float32)


def draw_gain_smooth(key, part):
    share = 0.5
    decay, unused_gain = channel_rates(key, share)
    keys = jax.random.split(jax.random.fold_in(key, 17), 2)
    rough = jnp.exp(jax.random.uniform(keys[0], (N,), jnp.float32, math.log(0.5), math.log(2.0)))
    noise = jax.random.normal(keys[1], (N, N), jnp.float32) * (0.01 / math.sqrt(2.0 * N))
    skewed = noise - noise.T
    result = skewed + jnp.diag(1.0 - decay * rough)
    return result.astype(jnp.float32)


def level_of(rng, dims, pieces, least, top_value):
    factor_of = 1.0
    for position, parts in pieces:
        heights = jax.random.uniform(jax.random.fold_in(jax.random.fold_in(rng, 6), position), (parts,), jnp.float32, least / len(pieces), top_value / len(pieces))
        factor_of = factor_of * jnp.repeat(jnp.exp(heights), dims[position] // parts).reshape((-1,) + (1,) * (len(dims) - 1 - position))
    return factor_of


def scatter_about(own_key, shape, deviation, bound, pieces=(), held_as=jnp.bfloat16):
    entries = deviation * jax.random.normal(own_key, shape, jnp.float32)
    if pieces:
        entries = entries * level_of(own_key, shape, pieces, -0.22, 0.18)
    return jnp.clip(entries, -bound, bound).astype(held_as)


def setup_inputs(seed: int = 0) -> dict:
    seeds = jax.random.split(jax.random.key(seed), 6)
    return {
        "jac": draw_jac(jax.random.fold_in(seeds[5], 71), 0),
        "obs": scatter_about(seeds[1], (TSTEPS, N), 1.0, 6.0, ((0, 256),), jnp.float32),
        "gain_filter": draw_gain_filter(jax.random.fold_in(seeds[5], 71), 0),
        "gain_smooth": draw_gain_smooth(jax.random.fold_in(seeds[5], 71), 0),
        "init_mean": scatter_about(seeds[4], (N,), 1.0, 6.0, (), jnp.float32),
    }


def reference(jac, obs, gain_filter, gain_smooth, init_mean):
    highest = lax.Precision.HIGHEST

    def forward(state, inputs):
        step_matrix, measured = inputs
        predicted = jnp.dot(step_matrix, state, precision=highest)
        updated = predicted + gain_filter * (measured - predicted)
        return updated, (predicted, updated)

    _, (predicted_all, filtered_all) = lax.scan(forward, init_mean, (jac, obs))

    def backward(state, correction):
        renewed = jnp.dot(gain_smooth, state, precision=highest) + correction
        return renewed, renewed

    _, back_states = lax.scan(backward, jnp.zeros((N,), jnp.float32), filtered_all - predicted_all, reverse=True)
    return filtered_all, predicted_all + back_states
```

```python
import functools

import jax
import jax.numpy as jnp
from jax import lax
from jax.experimental import pallas as pl
from jax.experimental.pallas import tpu as pltpu
from jax.sharding import PartitionSpec as P

HIGHEST = lax.Precision.HIGHEST
F32 = jnp.float32
VMEM = pl.BlockSpec(memory_space=pltpu.VMEM)
SMEM = pl.BlockSpec(memory_space=pltpu.SMEM)
ANY = pl.BlockSpec(memory_space=pl.ANY)
PAD = 8


def dot_nn(a, b):
    return lax.dot_general(
        a, b, (((1,), (0,)), ((), ())), precision=HIGHEST, preferred_element_type=F32
    )


def dot_nt(a, b):
    return lax.dot_general(
        a, b, (((1,), (1,)), ((), ())), precision=HIGHEST, preferred_element_type=F32
    )


def kernel_call(body, out_shape, in_specs, args, name, scratch=(), flops=0, size=0):
    many = isinstance(out_shape, list)
    shapes = [jax.ShapeDtypeStruct(s, F32) for s in (out_shape if many else [out_shape])]
    out = pl.pallas_call(
        body,
        out_shape=shapes,
        in_specs=in_specs,
        out_specs=[VMEM] * len(shapes),
        scratch_shapes=list(scratch),
        cost_estimate=pl.CostEstimate(flops=flops, bytes_accessed=size, transcendentals=0),
        compiler_params=pltpu.CompilerParams(vmem_limit_bytes=40 << 20),
        name=name,
    )(*args)
    return out if many else out[0]


def local_map_body(jac_hbm, obs, gain, out, buf, chain, sems):
    steps, n, _ = buf.shape
    lanes = 4
    depth = steps // lanes
    order = [c * depth + i for i in range(depth) for c in range(lanes)]
    for t in order:
        pltpu.make_async_copy(jac_hbm.at[t], buf.at[t], sems.at[t]).start()
    g = gain[...]
    retain = 1.0 - g
    for i in range(depth):
        for c in range(lanes):
            t = c * depth + i
            pltpu.make_async_copy(jac_hbm.at[t], buf.at[t], sems.at[t]).wait()
            offset = jnp.broadcast_to(g * obs[t : t + 1, :], (PAD, n))
            if i == 0:
                chain[c, :n] = buf[t].T * retain
                chain[c, n:] = offset
            else:
                moved = dot_nt(chain[c], buf[t]) * retain
                chain[c, :n] = moved[:n]
                chain[c, n:] = moved[n:] + offset
    width = 1
    while width < lanes:
        for c in range(0, lanes, 2 * width):
            moved = dot_nn(chain[c], chain[c + width, :n])
            dest = out if 2 * width == lanes else chain.at[c]
            later = chain[c + width, n:]
            dest[:n] = moved[:n]
            dest[n:] = moved[n:] + later
        width *= 2


def local_map(jac, obs, gain):
    steps, n, _ = jac.shape
    return kernel_call(
        local_map_body,
        (n + PAD, n),
        [ANY, VMEM, VMEM],
        (jac, obs, gain),
        "local_map",
        scratch=[
            pltpu.VMEM((steps, n, n), F32),
            pltpu.VMEM((4, n + PAD, n), F32),
            pltpu.SemaphoreType.DMA((steps,)),
        ],
        flops=12 * steps * n**3,
        size=4 * steps * n * n,
    )


def join(earlier, later, out):
    n = out.shape[1]
    moved = dot_nn(earlier[...], later[:n])
    out[:n] = moved[:n]
    out[n:] = moved[n:] + later[n:]


def total_body(upper, own, other, out):
    @pl.when(upper[0] == 1)
    def _():
        join(other, own, out)

    @pl.when(upper[0] == 0)
    def _():
        join(own, other, out)


def before_body(upper, before, other, out):
    @pl.when(upper[0] == 1)
    def _():
        join(other, before, out)

    @pl.when(upper[0] == 0)
    def _():
        out[...] = before[...]


def pair_call(body, upper, a, b, name):
    n = a.shape[1]
    return kernel_call(
        body, a.shape, [SMEM, VMEM, VMEM], (upper, a, b), name, flops=12 * n**3, size=12 * n * n
    )


def hop_body(take, x, received, group_map, x_out, y_out):
    n = x.shape[1]
    taken = jnp.where(take[0] == 1, received[...], x[...])
    x_out[...] = taken
    y_out[...] = dot_nn(taken, group_map[:n]) + group_map[n:]


def hop(take, x, received, group_map):
    n = x.shape[1]
    return kernel_call(
        hop_body,
        [(PAD, n), (PAD, n)],
        [SMEM, VMEM, VMEM, VMEM],
        (take, x, received, group_map),
        "hop",
        flops=96 * n * n,
        size=4 * n * n,
    )


def scan_body(take, x, received, before, jac_hbm, obs, gain, smooth, pred, filt, out, buf, sems):
    steps, n, _ = buf.shape
    for t in range(steps):
        pltpu.make_async_copy(jac_hbm.at[t], buf.at[t], sems.at[t]).start()
    g = gain[...]
    state = jnp.where(take[0] == 1, received[...], x[...])
    state = dot_nn(state, before[:n]) + before[n:]
    for t in range(steps):
        pltpu.make_async_copy(jac_hbm.at[t], buf.at[t], sems.at[t]).wait()
        predicted = dot_nt(state, buf[t])
        state = predicted + g * (obs[t : t + 1, :] - predicted)
        pred[t : t + 1, :] = predicted[:1]
        filt[t : t + 1, :] = state[:1]
    back = jnp.zeros_like(state)
    gs = smooth[...]
    for t in reversed(range(steps)):
        back = dot_nt(back, gs) + (filt[t : t + 1, :] - pred[t : t + 1, :])
    out[...] = back


def forward_scan(take, x, received, before, jac, obs, gain, smooth):
    steps, n, _ = jac.shape
    return kernel_call(
        scan_body,
        [(steps, n), (steps, n), (PAD, n)],
        [SMEM, VMEM, VMEM, VMEM, ANY, VMEM, VMEM, VMEM],
        (take, x, received, before, jac, obs, gain, smooth),
        "forward_scan",
        scratch=[pltpu.VMEM((steps, n, n), F32), pltpu.SemaphoreType.DMA((steps,))],
        flops=200 * steps * n * n,
        size=4 * steps * n * n,
    )


def powers_body(steps, count, outer_count, smooth, inner, outer):
    n = smooth.shape[0]
    square = smooth[...].T
    reach = 1
    while reach < steps:
        square = dot_nn(square, square)
        reach *= 2
    for dest, number in ((inner, count), (outer, outer_count)):
        level = 0
        reach = 1
        while reach < number:
            dest[level] = square
            square = dot_nn(square, square)
            reach *= 2
            level += 1


def powers(smooth, steps, count, outer_count):
    n = smooth.shape[0]
    shapes = [(count.bit_length() - 1, n, n), (outer_count.bit_length() - 1, n, n)]
    return kernel_call(
        functools.partial(powers_body, steps, count, outer_count),
        shapes,
        [VMEM],
        (smooth,),
        "powers",
        flops=150 * n**3,
        size=40 * n * n,
    )


def lift_body(place, powers_ref, out):
    levels, n, _ = powers_ref.shape
    left = (1 << levels) - 1 - place[0]
    row = lax.broadcasted_iota(jnp.int32, (n, n), 0)
    column = lax.broadcasted_iota(jnp.int32, (n, n), 1)
    out[...] = jnp.where(row == column, 1.0, 0.0).astype(F32)
    for level in range(levels):
        @pl.when((left >> level) % 2 == 1)
        def _():
            out[...] = dot_nn(out[...], powers_ref[level])


def lift(place, powers_ref):
    levels, n, _ = powers_ref.shape
    return kernel_call(
        lift_body, (n, n), [SMEM, VMEM], (place, powers_ref), "lift", flops=48 * n**3, size=20 * n * n
    )


def fold(rows, powers_ref):
    level = 0
    while len(rows) > 1:
        half = len(rows) // 2
        later = jnp.concatenate([rows[2 * i + 1] for i in range(half)], 0)
        moved = dot_nn(later, powers_ref[level])
        rows = [rows[2 * i] + moved[PAD * i : PAD * (i + 1)] for i in range(half)]
        level += 1
    return rows[0]


def gather_fold(place, got, powers_ref):
    count, n = got.shape
    sub = lax.broadcasted_iota(jnp.int32, (PAD, n), 0)
    rows = []
    for k in range(count):
        source = place[0] + 1 + k
        inside = source < count
        mine = got[pl.ds(jnp.where(inside, source, 0), 1), :]
        mine = jnp.where(inside, mine, jnp.zeros_like(mine))
        rows.append(
            jnp.where(
                sub < 4, jnp.broadcast_to(mine, (PAD, n)), jnp.broadcast_to(got[k : k + 1, :], (PAD, n))
            )
        )
    return fold(rows, powers_ref)


def inner_body(place, got, powers_ref, after, total):
    both = gather_fold(place, got, powers_ref)
    n = both.shape[1]
    after[...] = jnp.broadcast_to(both[:1], (PAD, n))
    total[...] = jnp.broadcast_to(both[4:5], total.shape)


def backward_body(place, got, powers_ref, after, lifted, pred, filt, smooth, out):
    both = gather_fold(place, got, powers_ref)
    steps, n = pred.shape
    boundary = jnp.broadcast_to(both[:1], (PAD, n))
    back = after[...] + dot_nn(boundary, lifted[...])
    gs = smooth[...]
    for t in reversed(range(steps)):
        back = dot_nt(back, gs) + (filt[t : t + 1, :] - pred[t : t + 1, :])
        out[t : t + 1, :] = pred[t : t + 1, :] + back[:1]


def shards(jac, obs, gain_filter, gain_smooth, init_mean):
    steps, n, _ = jac.shape
    inner_count, outer_count = lax.axis_size("inner"), lax.axis_size("outer")
    inner, outer = lax.axis_index("inner"), lax.axis_index("outer")
    gain = gain_filter[None, :]

    def bit(index, k):
        return ((index >> k) % 2).astype(jnp.int32)[None]

    with jax.named_scope("compose"):
        total = local_map(jac, obs, gain)
    before = None
    stages = [("inner", inner, 1, 0), ("inner", inner, 3, 1), ("inner", inner, 4, 2), ("inner", inner, 12, 3)]
    stages += [("outer", outer, 1, 0), ("outer", outer, 2, 1)]
    counts = {"inner": inner_count, "outer": outer_count}
    for axis, index, flip, k in stages:
        with jax.named_scope(f"join_{axis}_{k}"):
            other = lax.ppermute(total, axis, [(i, i ^ flip) for i in range(counts[axis])])
            upper = bit(index, k)
            if before is None:
                eye = jnp.concatenate([jnp.eye(n, dtype=F32), jnp.zeros((PAD, n), F32)], 0)
                before = jnp.where(upper[0] == 1, other, eye)
            else:
                before = pair_call(before_body, upper, before, other, "before")
            total = pair_call(total_body, upper, total, other, "total")
    inner_powers, outer_powers = powers(gain_smooth, steps, inner_count, outer_count)
    place = inner.astype(jnp.int32)[None]
    lifted = lift(place, inner_powers)

    x = jnp.broadcast_to(init_mean[None, :], (PAD, n))
    received = x
    group = 4
    supers = outer_count // group
    chain = [(i, i + group) for i in range(outer_count - group)]
    for h in range(supers - 1):
        with jax.named_scope(f"hop_{h}"):
            take = (outer // group == h).astype(jnp.int32)[None]
            x, y = hop(take, x, received, total)
            received = lax.ppermute(y, "outer", chain)
    take = (outer // group == supers - 1).astype(jnp.int32)[None]
    with jax.named_scope("forward"):
        pred, filt, offset = forward_scan(take, x, received, before, jac, obs, gain, gain_smooth)
    with jax.named_scope("suffix_inner"):
        sent = jnp.broadcast_to(offset[:1], (inner_count, n))
        got = lax.all_to_all(sent, "inner", 0, 0, tiled=True)
        after, group_total = kernel_call(
            inner_body,
            [(PAD, n), (outer_count, n)],
            [SMEM, VMEM, VMEM],
            (place, got, inner_powers),
            "suffix_inner",
            flops=100 * n * n,
            size=16 * n * n,
        )
    with jax.named_scope("suffix_outer"):
        got = lax.all_to_all(group_total, "outer", 0, 0, tiled=True)
        smoothed = kernel_call(
            backward_body,
            (steps, n),
            [SMEM] + [VMEM] * 7,
            (outer.astype(jnp.int32)[None], got, outer_powers, after, lifted, pred, filt, gain_smooth),
            "backward",
            flops=200 * n * n,
            size=24 * n * n,
        )
    return (filt, smoothed)


def solution(mesh):
    return jax.shard_map(
        shards,
        mesh=mesh,
        in_specs=(P(("outer", "inner"), None, None), P(("outer", "inner"), None), P(), P(), P()),
        out_specs=(P(("outer", "inner"), None), P(("outer", "inner"), None)),
        check_vma=False,
    )
```

```python
import functools

import jax
import jax.numpy as jnp
from jax import lax
from jax.experimental import pallas as pl
from jax.experimental.pallas import tpu as pltpu
from jax.sharding import PartitionSpec as P

HIGHEST = lax.Precision.HIGHEST
F32 = jnp.float32
VMEM = pl.BlockSpec(memory_space=pltpu.VMEM)
SMEM = pl.BlockSpec(memory_space=pltpu.SMEM)
HBM = pl.BlockSpec(memory_space=pltpu.MemorySpace.HBM)
PAD = 8


def dot_nn(a, b):
    return lax.dot_general(
        a, b, (((1,), (0,)), ((), ())), precision=HIGHEST, preferred_element_type=F32
    )


def dot_nt(a, b):
    return lax.dot_general(
        a, b, (((1,), (1,)), ((), ())), precision=HIGHEST, preferred_element_type=F32
    )


def kernel_call(body, out_shape, in_specs, args, name, scratch=(), flops=0, size=0, grant=4):
    many = isinstance(out_shape, list)
    shapes = [jax.ShapeDtypeStruct(s, F32) for s in (out_shape if many else [out_shape])]
    out = pl.pallas_call(
        body,
        out_shape=shapes,
        in_specs=in_specs,
        out_specs=[VMEM] * len(shapes),
        scratch_shapes=list(scratch),
        cost_estimate=pl.CostEstimate(flops=flops, bytes_accessed=size, transcendentals=0),
        compiler_params=pltpu.CompilerParams(vmem_limit_bytes=grant << 20),
        name=name,
    )(*args)
    return out if many else out[0]


def local_map_body(jac_hbm, obs_hbm, gain_hbm, out, quarter, half, third, buf, obs, gain, chain, sems):
    steps, n, _ = buf.shape
    small = [(obs_hbm, obs, steps), (gain_hbm, gain, steps + 1)]
    for source, dest, k in small:
        pltpu.make_async_copy(source, dest, sems.at[k]).start()
    pairs = steps // 2
    order = [2 * c + i for i in range(2) for c in range(pairs)]
    for t in order:
        pltpu.make_async_copy(jac_hbm.at[t], buf.at[t], sems.at[t]).start()
    for source, dest, k in small:
        pltpu.make_async_copy(source, dest, sems.at[k]).wait()
    g = gain[...]
    retain = 1.0 - g
    for t in order:
        pltpu.make_async_copy(jac_hbm.at[t], buf.at[t], sems.at[t]).wait()
        c = t // 2
        offset = jnp.broadcast_to(g * obs[t : t + 1, :], (PAD, n))
        if t % 2 == 0:
            chain[c, :n] = buf[t].T * retain
            chain[c, n:] = offset
        else:
            moved = dot_nt(chain[c], buf[t]) * retain
            chain[c, :n] = moved[:n]
            chain[c, n:] = moved[n:] + offset
    kept = {(0, pairs): out, (0, pairs // 2): half}
    kept[(0, pairs // 4)] = quarter
    kept[(pairs // 2, 3 * pairs // 4)] = third
    width = 1
    while width < pairs:
        for c in range(0, pairs, 2 * width):
            moved = dot_nn(chain[c], chain[c + width, :n])
            later = chain[c + width, n:]
            span = (c, c + 2 * width)
            dest = kept.get(span, chain.at[c])
            dest[:n] = moved[:n]
            dest[n:] = moved[n:] + later
            if span in kept and 2 * width < pairs:
                chain[c] = dest[...]
        width *= 2


def local_map(jac, obs, gain):
    steps, n, _ = jac.shape
    return kernel_call(
        local_map_body,
        [(n + PAD, n)] * 4,
        [HBM, HBM, HBM],
        (jac, obs, gain),
        "local_map",
        scratch=[
            pltpu.VMEM((steps, n, n), F32),
            pltpu.VMEM((steps, n), F32),
            pltpu.VMEM((1, n), F32),
            pltpu.VMEM((steps // 2, n + PAD, n), F32),
            pltpu.SemaphoreType.DMA((steps + 2,)),
        ],
        flops=12 * steps * n**3,
        size=4 * steps * n * n,
        grant=52,
    )


def join(earlier, later, out):
    n = out.shape[1]
    moved = dot_nn(earlier[...], later[:n])
    out[:n] = moved[:n]
    out[n:] = moved[n:] + later[n:]


def total_body(upper, own, other, out):
    @pl.when(upper[0] == 1)
    def _():
        join(other, own, out)

    @pl.when(upper[0] == 0)
    def _():
        join(own, other, out)


def before_body(upper, before, other, out):
    @pl.when(upper[0] == 1)
    def _():
        join(other, before, out)

    @pl.when(upper[0] == 0)
    def _():
        out[...] = before[...]


def pair_call(body, upper, a, b, name):
    n = a.shape[1]
    return kernel_call(
        body, a.shape, [SMEM, VMEM, VMEM], (upper, a, b), name, flops=12 * n**3, size=12 * n * n
    )


def join_body(earlier, later, out):
    join(earlier, later, out)


def advance_body(count, *refs):
    x, maps, out = refs[0], refs[1 : 1 + count], refs[1 + count]
    n = x.shape[1]
    state = x[...]
    for m in maps:
        state = dot_nn(state, m[:n]) + m[n:]
    out[...] = state


def advance(x, *maps):
    n = x.shape[1]
    return kernel_call(
        functools.partial(advance_body, len(maps)),
        (PAD, n),
        [VMEM] * (1 + len(maps)),
        (x, *maps),
        "advance",
        flops=96 * n * n,
        size=4 * n * n,
    )


def forward_body(
    x, before, quarter, half, three, jac_hbm, obs, gain, base_powers, filt, base, sent, pred, shifted, jac, sems
):
    steps, n, _ = jac.shape
    lanes = 4
    depth = steps // lanes
    for i in range(depth):
        for c in range(lanes):
            t = c * depth + i
            pltpu.make_async_copy(jac_hbm.at[t], jac.at[t], sems.at[t]).start()
    g = gain[...]
    state = dot_nn(x[...], before[:n]) + before[n:]
    states = [state] + [dot_nn(state, m[:n]) + m[n:] for m in (quarter, half, three)]
    for i in range(depth):
        for c in range(lanes):
            t = c * depth + i
            pltpu.make_async_copy(jac_hbm.at[t], jac.at[t], sems.at[t]).wait()
            predicted = dot_nt(states[c], jac[t])
            states[c] = predicted + g * (obs[t : t + 1, :] - predicted)
            pred[t : t + 1, :] = predicted[:1]
            filt[t : t + 1, :] = states[c][:1]
    back = filt[...] - pred[...]
    shifted[steps:, :] = jnp.zeros((steps, n), F32)
    level = 0
    reach = 1
    while reach < steps:
        shifted[:steps, :] = back
        back = back + dot_nn(shifted[reach : reach + steps, :], base_powers[level])
        reach *= 2
        level += 1
    base[...] = pred[...] + back
    sent[...] = jnp.broadcast_to(back[:1][None], sent.shape)


def base_powers_body(steps, smooth, base, top):
    square = smooth[...].T
    level = 0
    reach = 1
    while reach < steps:
        base[level] = square
        square = dot_nn(square, square)
        reach *= 2
        level += 1
    top[...] = square


def high_powers_body(count, outer_count, top, inner, outer):
    square = top[...]
    for dest, number in ((inner, count), (outer, outer_count)):
        level = 0
        reach = 1
        while reach < number:
            dest[level] = square
            square = dot_nn(square, square)
            reach *= 2
            level += 1


def lift_body(place, powers_ref, out):
    levels, n, _ = powers_ref.shape
    left = (1 << levels) - 1 - place[0]
    row = lax.broadcasted_iota(jnp.int32, (n, n), 0)
    column = lax.broadcasted_iota(jnp.int32, (n, n), 1)
    out[...] = jnp.where(row == column, 1.0, 0.0).astype(F32)
    for level in range(levels):
        @pl.when((left >> level) % 2 == 1)
        def _():
            out[...] = dot_nn(out[...], powers_ref[level])


def fold(rows, powers_ref):
    size = rows[0].shape[0]
    level = 0
    while len(rows) > 1:
        half = len(rows) // 2
        later = jnp.concatenate([rows[2 * i + 1] for i in range(half)], 0)
        moved = dot_nn(later, powers_ref[level])
        rows = [rows[2 * i] + moved[size * i : size * (i + 1)] for i in range(half)]
        level += 1
    return rows[0]


def backward_body(place, got, inner_powers, outer_powers, lifted, base_powers, top, base, out, totals):
    steps, n = base.shape
    outer_count = 1 << outer_powers.shape[0]
    inner_count = 1 << inner_powers.shape[0]
    here, group = place[0], place[1]

    def row(ref, index, inside):
        value = ref[pl.ds(jnp.where(inside, index, 0), 1), :]
        return jnp.broadcast_to(jnp.where(inside, value, jnp.zeros_like(value)), (PAD, n))

    blocks = []
    for k in range(inner_count):
        source = here + 1 + k
        mine = row(got, source * outer_count + group, source < inner_count)
        blocks.append(jnp.concatenate([got[k * outer_count : (k + 1) * outer_count, :], mine], 0))
    both = fold(blocks, inner_powers)
    totals[...] = both[:outer_count]
    after = both[outer_count:]
    blocks = []
    for k in range(outer_count):
        source = group + 1 + k
        blocks.append(row(totals, source, source < outer_count))
    boundary = after + dot_nn(fold(blocks, outer_powers), lifted[...])
    left = steps - lax.broadcasted_iota(jnp.int32, (steps, n), 0)
    back = jnp.broadcast_to(boundary[:1], (steps, n))
    factors = [base_powers[k] for k in range(base_powers.shape[0])] + [top[...]]
    for level, factor in enumerate(factors):
        back = jnp.where((left >> level) % 2 == 1, dot_nn(back, factor), back)
    out[...] = base[...] + back


def shards(jac, obs, gain_filter, gain_smooth, init_mean):
    steps, n, _ = jac.shape
    inner_count, outer_count = lax.axis_size("inner"), lax.axis_size("outer")
    counts = {"inner": inner_count, "outer": outer_count}
    inner, outer = lax.axis_index("inner"), lax.axis_index("outer")
    gain = gain_filter[None, :]

    def bit(index, k):
        return ((index >> k) % 2).astype(jnp.int32)[None]

    def exchange(total, axis, flip, beside):
        other = lax.ppermute(total, axis, [(i, i ^ flip) for i in range(counts[axis])])
        work = beside()
        return lax.optimization_barrier((other, work))

    with jax.named_scope("compose"):
        total, quarter, half, third = local_map(jac, obs, gain)

    def base_work():
        levels = steps.bit_length() - 1
        return kernel_call(
            functools.partial(base_powers_body, steps),
            [(levels, n, n), (n, n)],
            [VMEM],
            (gain_smooth,),
            "base_powers",
            flops=60 * n**3,
            size=20 * n * n,
        )

    with jax.named_scope("join_inner_0"):
        first, (base_powers, top) = exchange(total, "inner", 1, base_work)
        upper = bit(inner, 0)
        total = pair_call(total_body, upper, total, first, "total")

    with jax.named_scope("join_inner_1"):
        eye = jnp.concatenate([jnp.eye(n, dtype=F32), jnp.zeros((PAD, n), F32)], 0)
        second, before = exchange(total, "inner", 3, lambda: jnp.where(upper[0] == 1, first, eye))
        total = pair_call(total_body, bit(inner, 1), total, second, "total")

    with jax.named_scope("join_inner_2"):
        third_map, before = exchange(
            total, "inner", 4, lambda: pair_call(before_body, bit(inner, 1), before, second, "before")
        )
        total = pair_call(total_body, bit(inner, 2), total, third_map, "total")

    def three_work():
        three = kernel_call(
            join_body, (n + PAD, n), [VMEM, VMEM], (half, third), "join", flops=12 * n**3, size=12 * n * n
        )
        return three, pair_call(before_body, bit(inner, 2), before, third_map, "before")

    with jax.named_scope("join_inner_3"):
        other, (three, before) = exchange(total, "inner", 12, three_work)
        group_map = pair_call(total_body, bit(inner, 3), total, other, "total")
    with jax.named_scope("join_core"):
        twin, before = exchange(
            group_map, "outer", 1, lambda: pair_call(before_body, bit(inner, 3), before, other, "before")
        )
        total = pair_call(total_body, bit(outer, 0), group_map, twin, "total")
    with jax.named_scope("join_z"):
        other, before = exchange(
            total, "outer", 2, lambda: pair_call(before_body, bit(outer, 0), before, twin, "before")
        )
        total = pair_call(total_body, bit(outer, 1), total, other, "total")

    group = outer_count // 4
    super_here = outer // group
    x = jnp.broadcast_to(init_mean[None, :], (PAD, n))

    def mirror(source, dest):
        return [
            (source * group + z * 2 + c, dest * group + (group // 2 - 1 - z) * 2 + c)
            for z in range(group // 2)
            for c in range(2)
        ]

    with jax.named_scope("hop_0"):
        y = advance(x, total)
        arrived = lax.ppermute(y, "outer", mirror(0, 1))
        before = pair_call(before_body, bit(outer, 1), before, other, "before")
        arrived, before = lax.optimization_barrier((arrived, before))
        x = jnp.where(super_here == 1, arrived, x)
    with jax.named_scope("hop_1"):
        y = advance(x, total)
        near = lax.ppermute(y, "outer", mirror(1, 2))
        far = lax.ppermute(y, "outer", mirror(1, 3))
        skipped = lax.ppermute(total, "outer", mirror(2, 3))
        x = jnp.where(super_here == 2, near, x)
        x = jnp.where(super_here == 3, advance(far, skipped), x)
    with jax.named_scope("forward"):
        devices = inner_count * outer_count
        filt, base, sent = kernel_call(
            forward_body,
            [(steps, n), (steps, n), (devices, 1, n)],
            [VMEM] * 5 + [HBM] + [VMEM] * 3,
            (x, before, quarter, half, three, jac, obs, gain, base_powers),
            "forward",
            scratch=[
                pltpu.VMEM((steps, n), F32),
                pltpu.VMEM((2 * steps, n), F32),
                pltpu.VMEM((steps, n, n), F32),
                pltpu.SemaphoreType.DMA((steps,)),
            ],
            grant=52,
            flops=200 * steps * n * n,
            size=4 * steps * n * n,
        )
    def high_work():
        shapes = [(inner_count.bit_length() - 1, n, n), (outer_count.bit_length() - 1, n, n)]
        return kernel_call(
            functools.partial(high_powers_body, inner_count, outer_count),
            shapes,
            [VMEM],
            (top,),
            "high_powers",
            flops=90 * n**3,
            size=40 * n * n,
        )

    with jax.named_scope("offsets"):
        sent, top = lax.optimization_barrier((sent, top))
        got = lax.all_to_all(sent, ("inner", "outer"), 0, 0, tiled=True)
        inner_powers, outer_powers = high_work()
        lifted = kernel_call(
            lift_body,
            (n, n),
            [SMEM, VMEM],
            (inner.astype(jnp.int32)[None], inner_powers),
            "lift",
            flops=48 * n**3,
            size=20 * n * n,
        )
        got, lifted = lax.optimization_barrier((got.reshape(devices, n), lifted))
    with jax.named_scope("backward"):
        place = jnp.stack([inner, outer]).astype(jnp.int32)
        smoothed = kernel_call(
            backward_body,
            (steps, n),
            [SMEM] + [VMEM] * 7,
            (place, got, inner_powers, outer_powers, lifted, base_powers, top, base),
            "backward",
            scratch=[pltpu.VMEM((outer_count, n), F32)],
            flops=200 * n * n,
            size=24 * n * n,
        )
    return (filt, smoothed)


def solution(mesh):
    return jax.shard_map(
        shards,
        mesh=mesh,
        in_specs=(P(("outer", "inner"), None, None), P(("outer", "inner"), None), P(), P(), P()),
        out_specs=(P(("outer", "inner"), None), P(("outer", "inner"), None)),
        check_vma=False,
    )
```

```python
import functools

import jax
import jax.numpy as jnp
from jax import lax
from jax.experimental import pallas as pl
from jax.experimental.pallas import tpu as pltpu
from jax.sharding import PartitionSpec as P

HIGHEST = lax.Precision.HIGHEST
F32 = jnp.float32
VMEM = pl.BlockSpec(memory_space=pltpu.VMEM)
SMEM = pl.BlockSpec(memory_space=pltpu.SMEM)
HBM = pl.BlockSpec(memory_space=pltpu.MemorySpace.HBM)
PAD = 8


def dot_nn(a, b):
    return lax.dot_general(
        a, b, (((1,), (0,)), ((), ())), precision=HIGHEST, preferred_element_type=F32
    )


def dot_nt(a, b):
    return lax.dot_general(
        a, b, (((1,), (1,)), ((), ())), precision=HIGHEST, preferred_element_type=F32
    )


def kernel_call(body, out_shape, in_specs, args, name, scratch=(), flops=0, size=0, grant=4):
    many = isinstance(out_shape, list)
    shapes = [jax.ShapeDtypeStruct(s, F32) for s in (out_shape if many else [out_shape])]
    out = pl.pallas_call(
        body,
        out_shape=shapes,
        in_specs=in_specs,
        out_specs=[VMEM] * len(shapes),
        scratch_shapes=list(scratch),
        cost_estimate=pl.CostEstimate(flops=flops, bytes_accessed=size, transcendentals=0),
        compiler_params=pltpu.CompilerParams(vmem_limit_bytes=grant << 20),
        name=name,
    )(*args)
    return out if many else out[0]


def local_map_body(jac_hbm, obs_hbm, gain_hbm, out, quarter, half, third, buf, obs, gain, chain, sems):
    steps, n, _ = buf.shape
    small = [(obs_hbm, obs, steps), (gain_hbm, gain, steps + 1)]
    for source, dest, k in small:
        pltpu.make_async_copy(source, dest, sems.at[k]).start()
    pairs = steps // 2
    order = [2 * c + i for i in range(2) for c in range(pairs)]
    for t in order:
        pltpu.make_async_copy(jac_hbm.at[t], buf.at[t], sems.at[t]).start()
    for source, dest, k in small:
        pltpu.make_async_copy(source, dest, sems.at[k]).wait()
    g = gain[...]
    retain = 1.0 - g
    for t in order:
        pltpu.make_async_copy(jac_hbm.at[t], buf.at[t], sems.at[t]).wait()
        c = t // 2
        offset = jnp.broadcast_to(g * obs[t : t + 1, :], (PAD, n))
        if t % 2 == 0:
            chain[c, :n] = buf[t].T * retain
            chain[c, n:] = offset
        else:
            moved = dot_nt(chain[c], buf[t]) * retain
            chain[c, :n] = moved[:n]
            chain[c, n:] = moved[n:] + offset
    kept = {(0, pairs): out, (0, pairs // 2): half}
    kept[(0, pairs // 4)] = quarter
    kept[(pairs // 2, 3 * pairs // 4)] = third
    width = 1
    while width < pairs:
        for c in range(0, pairs, 2 * width):
            moved = dot_nn(chain[c], chain[c + width, :n])
            later = chain[c + width, n:]
            span = (c, c + 2 * width)
            dest = kept.get(span, chain.at[c])
            dest[:n] = moved[:n]
            dest[n:] = moved[n:] + later
            if span in kept and 2 * width < pairs:
                chain[c] = dest[...]
        width *= 2


def local_map(jac, obs, gain):
    steps, n, _ = jac.shape
    return kernel_call(
        local_map_body,
        [(n + PAD, n)] * 4,
        [HBM, HBM, HBM],
        (jac, obs, gain),
        "local_map",
        scratch=[
            pltpu.VMEM((steps, n, n), F32),
            pltpu.VMEM((steps, n), F32),
            pltpu.VMEM((1, n), F32),
            pltpu.VMEM((steps // 2, n + PAD, n), F32),
            pltpu.SemaphoreType.DMA((steps + 2,)),
        ],
        flops=12 * steps * n**3,
        size=4 * steps * n * n,
        grant=52,
    )


def join(earlier, later, out):
    n = out.shape[1]
    moved = dot_nn(earlier[...], later[:n])
    out[:n] = moved[:n]
    out[n:] = moved[n:] + later[n:]


def total_body(upper, own, other, out):
    @pl.when(upper[0] == 1)
    def _():
        join(other, own, out)

    @pl.when(upper[0] == 0)
    def _():
        join(own, other, out)


def before_body(upper, before, other, out):
    @pl.when(upper[0] == 1)
    def _():
        join(other, before, out)

    @pl.when(upper[0] == 0)
    def _():
        out[...] = before[...]


def pair_call(body, upper, a, b, name):
    n = a.shape[1]
    return kernel_call(
        body, a.shape, [SMEM, VMEM, VMEM], (upper, a, b), name, flops=12 * n**3, size=12 * n * n
    )


def join_body(earlier, later, out):
    join(earlier, later, out)


def advance_body(count, *refs):
    x, maps, out = refs[0], refs[1 : 1 + count], refs[1 + count]
    n = x.shape[1]
    state = x[...]
    for m in maps:
        state = dot_nn(state, m[:n]) + m[n:]
    out[...] = state


def advance(x, *maps):
    n = x.shape[1]
    return kernel_call(
        functools.partial(advance_body, len(maps)),
        (PAD, n),
        [VMEM] * (1 + len(maps)),
        (x, *maps),
        "advance",
        flops=96 * n * n,
        size=4 * n * n,
    )


def maps_body(first, *refs):
    if first:
        quarter, half, three, jac, obs, gain, base_powers, pi, pairs, phi, later, moving = refs
        starts = [None, quarter, half, three]
    else:
        given, jac, obs, gain, base_powers, pi, pairs, later, moving = refs
        starts = [given.at[c] for c in range(4)]
    n = jac.shape[1]
    size = n + PAD
    lanes = 4
    depth = jac.shape[0] // lanes
    g = gain[...]
    retain = 1.0 - g
    for i in range(2):
        for c in range(lanes):
            t = c * depth + i + (0 if first else 2)
            k = 2 * c + i
            source = starts[c] if i == 0 else moving.at[c]
            if source is None:
                pi[k, :n] = jac[t].T
                pi[k, n:] = jnp.zeros((PAD, n), F32)
            else:
                pi[k] = dot_nt(source[...], jac[t])
            offset = g * obs[t : t + 1, :]
            predicted = pi[k]
            if i == 0 or first:
                dest = moving if i == 0 else phi
                dest[c, :n] = predicted[:n] * retain
                dest[c, n:] = predicted[n:] * retain + offset
            change = -(predicted * g)
            if i == 0:
                pairs[c, :n] = change[:n]
                pairs[c, n:] = change[n:] + offset
            else:
                later[c * size : c * size + n] = change[:n]
                later[c * size + n : (c + 1) * size] = change[n:] + offset
    moved = dot_nn(later[...], base_powers[0])
    for c in range(lanes):
        pairs[c] = pairs[c] + moved[c * size : (c + 1) * size]


def maps(first, starts, jac, obs, gain, base_powers):
    n = jac.shape[1]
    size = n + PAD
    shapes = [(8, size, n), (4, size, n)] + ([(4, size, n)] if first else [])
    return kernel_call(
        functools.partial(maps_body, first),
        shapes,
        [VMEM] * (len(starts) + 4),
        (*starts, jac, obs, gain, base_powers),
        "maps",
        scratch=[pltpu.VMEM((4 * size, n), F32), pltpu.VMEM((4, size, n), F32)],
        flops=12 * 12 * n**3,
        size=8 * 12 * n * n,
        grant=10,
    )


def offset_map_body(even, odd, base_powers, out, later):
    size, n = out.shape
    for c in range(4):
        later[c * size : (c + 1) * size] = odd[c]
    moved = dot_nn(later[...], base_powers[1])
    quads = [even[c] + moved[c * size : (c + 1) * size] for c in range(4)]
    halves = []
    for c in (0, 2):
        halves.append(quads[c] + dot_nn(quads[c + 1], base_powers[2]))
    out[...] = halves[0] + dot_nn(halves[1], base_powers[3])


def base_powers_body(steps, smooth, base, top):
    square = smooth[...].T
    level = 0
    reach = 1
    while reach < steps:
        base[level] = square
        square = dot_nn(square, square)
        reach *= 2
        level += 1
    top[...] = square


def high_powers_body(stages, top, out):
    unit = top[...]
    for k in range(stages):
        out[3 * k] = unit
        double = dot_nn(unit, unit)
        out[3 * k + 1] = double
        if k < stages - 1:
            out[3 * k + 2] = dot_nn(double, unit)
            unit = dot_nn(double, double)


def lift_body(digits, powers_ref, base_powers, lifts, ends):
    n = base_powers.shape[1]
    stages = lifts.shape[0]
    row = lax.broadcasted_iota(jnp.int32, (n, n), 0)
    column = lax.broadcasted_iota(jnp.int32, (n, n), 1)
    eye = jnp.where(row == column, 1.0, 0.0).astype(F32)
    for k in range(stages):
        left = 3 - digits[k]
        index = 3 * k + jnp.maximum(left - 1, 0)
        own = powers_ref[index]
        if k == 0:
            lifts[k] = jnp.where(left == 0, eye, own)
        else:
            lifts[k] = jnp.where(left == 0, lifts[k - 1], dot_nn(lifts[k - 1], own))
    ends[0] = dot_nn(lifts[stages - 1], base_powers[0])
    ends[1] = dot_nn(ends[0], powers_ref[3 * stages])
    ends[2] = dot_nn(ends[0], powers_ref[3 * stages + 1])


def offset_body(x, before, offset_map, entry, out):
    n = x.shape[1]
    state = dot_nn(x[...], before[:n]) + before[n:]
    entry[...] = state
    out[...] = dot_nn(state, offset_map[:n]) + offset_map[n:]


def states_body(entry, even, odd, obs, gain, pred, filt):
    steps, n = pred.shape
    g = gain[...]
    state = entry[...]
    for t in range(steps):
        c, i = t // 4, t % 4
        pi = even if i < 2 else odd
        k = 2 * c + i % 2
        predicted = (dot_nn(state, pi[k, :n]) + pi[k, n:])[:1]
        pred[t : t + 1, :] = predicted
        filt[t : t + 1, :] = predicted + g * (obs[t : t + 1, :] - predicted)


def local_back_body(pred, filt, base_powers, base, shifted):
    steps, n = pred.shape
    back = filt[...] - pred[...]
    shifted[steps:, :] = jnp.zeros((steps, n), F32)
    level = 0
    reach = 1
    while reach < steps:
        shifted[:steps, :] = back
        back = back + dot_nn(shifted[reach : reach + steps, :], base_powers[level])
        reach *= 2
        level += 1
    base[...] = pred[...] + back


def pick(digit, vectors, i):
    index = jnp.bitwise_xor(digit, i)
    value = vectors[0]
    for f in range(1, 4):
        value = jnp.where(index == f, vectors[f], value)
    return jnp.where(i < 4, value, jnp.zeros_like(value))


def spread_body(k, digits, own, one, two, three, powers_ref, total, behind):
    digit = digits[k]
    vectors = [own[...], one[...], two[...], three[...]]
    total_value = pick(digit, vectors, 0)
    behind_value = pick(digit, vectors, digit + 1)
    for m in range(1, 4):
        rows = pick(digit, vectors, m)
        if m < 3:
            rows = jnp.concatenate([rows, pick(digit, vectors, digit + 1 + m)], 0)
        moved = dot_nn(rows, powers_ref[3 * k + m - 1])
        total_value = total_value + moved[:PAD]
        if m < 3:
            behind_value = behind_value + moved[PAD:]
    total[...] = total_value
    behind[...] = behind_value


def gathered_body(b0, b1, b2, lifts, base_powers, out):
    value = b0[...] + (dot_nn(b1[...], lifts[0]) + dot_nn(b2[...], lifts[1]))
    out[...] = dot_nn(value, base_powers[0])


def backward_body(digits, own, one, two, three, gathered, ends, base_powers, base, out):
    steps, n = base.shape
    digit = digits[3]
    vectors = [own[...], one[...], two[...], three[...]]
    value = gathered[...]
    for j in range(3):
        value = value + dot_nn(pick(digit, vectors, digit + 1 + j), ends[j])
    left = steps - 1 - lax.broadcasted_iota(jnp.int32, (steps, n), 0)
    back = jnp.concatenate([value, value], 0)
    for level in range(base_powers.shape[0]):
        back = jnp.where((left >> level) % 2 == 1, dot_nn(back, base_powers[level]), back)
    out[...] = base[...] + back


def shards(jac, obs, gain_filter, gain_smooth, init_mean):
    steps, n, _ = jac.shape
    inner_count, outer_count = lax.axis_size("inner"), lax.axis_size("outer")
    counts = {"inner": inner_count, "outer": outer_count}
    inner, outer = lax.axis_index("inner"), lax.axis_index("outer")
    gain = gain_filter[None, :]

    def bit(index, k):
        return ((index >> k) % 2).astype(jnp.int32)[None]

    def exchange(total, axis, flip, beside):
        other = lax.ppermute(total, axis, [(i, i ^ flip) for i in range(counts[axis])])
        work = beside()
        return lax.optimization_barrier((other, work))

    with jax.named_scope("compose"):
        total, quarter, half, third = local_map(jac, obs, gain)

    def base_work():
        levels = steps.bit_length() - 1
        return kernel_call(
            functools.partial(base_powers_body, steps),
            [(levels, n, n), (n, n)],
            [VMEM],
            (gain_smooth,),
            "base_powers",
            flops=60 * n**3,
            size=20 * n * n,
        )

    with jax.named_scope("join_inner_0"):

        def work():
            three = kernel_call(
                join_body, (n + PAD, n), [VMEM, VMEM], (half, third), "join", flops=12 * n**3, size=12 * n * n
            )
            return base_work(), three

        first, ((base_powers, top), three) = exchange(total, "inner", 1, work)
        upper = bit(inner, 0)
        total = pair_call(total_body, upper, total, first, "total")
    with jax.named_scope("join_inner_1"):
        eye = jnp.concatenate([jnp.eye(n, dtype=F32), jnp.zeros((PAD, n), F32)], 0)

        def work():
            made = maps(True, (quarter, half, three), jac, obs, gain, base_powers)
            return made, jnp.where(upper[0] == 1, first, eye)

        second, ((pi_even, even, phi), before) = exchange(total, "inner", 3, work)
        total = pair_call(total_body, bit(inner, 1), total, second, "total")
    with jax.named_scope("join_inner_2"):

        def work():
            made = maps(False, (phi,), jac, obs, gain, base_powers)
            return made, pair_call(before_body, bit(inner, 1), before, second, "before")

        other, ((pi_odd, odd), before) = exchange(total, "inner", 4, work)
        total = pair_call(total_body, bit(inner, 2), total, other, "total")
    with jax.named_scope("join_inner_3"):

        def work():
            made = kernel_call(
                offset_map_body,
                (n + PAD, n),
                [VMEM] * 3,
                (even, odd, base_powers),
                "offset_map",
                scratch=[pltpu.VMEM((4 * (n + PAD), n), F32)],
                flops=84 * n**3,
                size=36 * n * n,
                grant=8,
            )
            return made, pair_call(before_body, bit(inner, 2), before, other, "before")

        row, (offset_map, before) = exchange(total, "inner", 12, work)
        group_map = pair_call(total_body, bit(inner, 3), total, row, "total")
    with jax.named_scope("join_core"):
        twin, before = exchange(
            group_map, "outer", 1, lambda: pair_call(before_body, bit(inner, 3), before, row, "before")
        )
        total = pair_call(total_body, bit(outer, 0), group_map, twin, "total")
    with jax.named_scope("join_z"):

        def work():
            made = kernel_call(
                functools.partial(high_powers_body, 4),
                (11, n, n),
                [VMEM],
                (top,),
                "high_powers",
                flops=120 * n**3,
                size=44 * n * n,
                grant=8,
            )
            return made, pair_call(before_body, bit(outer, 0), before, twin, "before")

        other, (high, before) = exchange(total, "outer", 2, work)
        total = pair_call(total_body, bit(outer, 1), total, other, "total")

    group = outer_count // 4
    super_here = outer // group
    x = jnp.broadcast_to(init_mean[None, :], (PAD, n))

    def mirror(source, dest):
        return [
            (source * group + z * 2 + c, dest * group + (group // 2 - 1 - z) * 2 + c)
            for z in range(group // 2)
            for c in range(2)
        ]

    with jax.named_scope("hop_0"):
        y = advance(x, total)
        arrived = lax.ppermute(y, "outer", mirror(0, 1))
        before = pair_call(before_body, bit(outer, 1), before, other, "before")
        digits = jnp.stack([inner % 4, inner // 4, outer % 4, outer // 4]).astype(jnp.int32)
        lifts, ends = kernel_call(
            lift_body,
            [(3, n, n), (3, n, n)],
            [SMEM, VMEM, VMEM],
            (digits, high, base_powers),
            "lift",
            flops=60 * n**3,
            size=60 * n * n,
            grant=8,
        )
        arrived, before, lifts, ends = lax.optimization_barrier((arrived, before, lifts, ends))
        x = jnp.where(super_here == 1, arrived, x)
    with jax.named_scope("hop_1"):
        y = advance(x, total)
        near = lax.ppermute(y, "outer", mirror(1, 2))
        far = lax.ppermute(y, "outer", mirror(1, 3))
        skipped = lax.ppermute(total, "outer", mirror(2, 3))
        x = jnp.where(super_here == 2, near, x)
        x = jnp.where(super_here == 3, advance(far, skipped), x)
    with jax.named_scope("offset"):
        entry, offset = kernel_call(
            offset_body,
            [(PAD, n), (PAD, n)],
            [VMEM] * 3,
            (x, before, offset_map),
            "offset",
            flops=192 * n * n,
            size=8 * n * n,
        )

    def spread(value, axis, flips, beside):
        parts = [lax.ppermute(value, axis, [(i, i ^ f) for i in range(counts[axis])]) for f in flips]
        work = beside()
        return lax.optimization_barrier((parts, work))

    def spread_call(k, own, parts):
        return kernel_call(
            functools.partial(spread_body, k),
            [(PAD, n), (PAD, n)],
            [SMEM] + [VMEM] * 5,
            (digits, own, *parts, high),
            "spread",
            flops=600 * n * n,
            size=12 * n * n,
            grant=8,
        )

    def states_work():
        return kernel_call(
            states_body,
            [(steps, n), (steps, n)],
            [VMEM] * 5,
            (entry, pi_even, pi_odd, obs, gain),
            "states",
            flops=16 * 96 * n * n,
            size=64 * n * n,
            grant=8,
        )

    with jax.named_scope("spread_y"):
        parts, _ = spread(offset, "inner", (1, 2, 3), lambda: ())
        value, behind_0 = spread_call(0, offset, parts)
    with jax.named_scope("spread_x"):
        parts, (pred, filt) = spread(value, "inner", (4, 8, 12), states_work)
        value, behind_1 = spread_call(1, value, parts)
    with jax.named_scope("spread_core"):

        def work():
            return kernel_call(
                local_back_body,
                (steps, n),
                [VMEM] * 3,
                (pred, filt, base_powers),
                "local_back",
                scratch=[pltpu.VMEM((2 * steps, n), F32)],
                flops=400 * n * n,
                size=16 * n * n,
            )

        parts, base = spread(value, "outer", (1, 2, 3), work)
        value, behind_2 = spread_call(2, value, parts)
    with jax.named_scope("spread_z"):

        def work():
            return kernel_call(
                gathered_body,
                (PAD, n),
                [VMEM] * 5,
                (behind_0, behind_1, behind_2, lifts, base_powers),
                "gathered",
                flops=300 * n * n,
                size=12 * n * n,
            )

        parts, gathered = spread(value, "outer", (4, 10, 12), work)
    with jax.named_scope("backward"):
        smoothed = kernel_call(
            backward_body,
            (steps, n),
            [SMEM] + [VMEM] * 8,
            (digits, value, *parts, gathered, ends, base_powers, base),
            "backward",
            flops=600 * n * n,
            size=24 * n * n,
        )
    return (filt, smoothed)


def solution(mesh):
    return jax.shard_map(
        shards,
        mesh=mesh,
        in_specs=(P(("outer", "inner"), None, None), P(("outer", "inner"), None), P(), P(), P()),
        out_specs=(P(("outer", "inner"), None), P(("outer", "inner"), None)),
        check_vma=False,
    )
```

```python
import functools

import jax
import jax.numpy as jnp
from jax import lax
from jax.experimental import pallas as pl
from jax.experimental.pallas import tpu as pltpu
from jax.sharding import PartitionSpec as P

HIGHEST = lax.Precision.HIGHEST
F32 = jnp.float32
VMEM = pl.BlockSpec(memory_space=pltpu.VMEM)
SMEM = pl.BlockSpec(memory_space=pltpu.SMEM)
HBM = pl.BlockSpec(memory_space=pltpu.MemorySpace.HBM)
PAD = 8


def dot_nn(a, b):
    return lax.dot_general(
        a, b, (((1,), (0,)), ((), ())), precision=HIGHEST, preferred_element_type=F32
    )


def dot_nt(a, b):
    return lax.dot_general(
        a, b, (((1,), (1,)), ((), ())), precision=HIGHEST, preferred_element_type=F32
    )


def kernel_call(body, out_shape, in_specs, args, name, scratch=(), flops=0, size=0, grant=4, out_specs=None):
    many = isinstance(out_shape, list)
    shapes = [jax.ShapeDtypeStruct(s, F32) for s in (out_shape if many else [out_shape])]
    out = pl.pallas_call(
        body,
        out_shape=shapes,
        in_specs=in_specs,
        out_specs=out_specs or [VMEM] * len(shapes),
        scratch_shapes=list(scratch),
        cost_estimate=pl.CostEstimate(flops=flops, bytes_accessed=size, transcendentals=0),
        compiler_params=pltpu.CompilerParams(vmem_limit_bytes=grant << 20),
        name=name,
    )(*args)
    return out if many else out[0]


def local_map_body(jac_hbm, obs_hbm, gain_hbm, out, quarter, half, third, buf, obs, gain, chain, sems):
    steps, n, _ = buf.shape
    small = [(obs_hbm, obs, steps), (gain_hbm, gain, steps + 1)]
    for source, dest, k in small:
        pltpu.make_async_copy(source, dest, sems.at[k]).start()
    pairs = steps // 2
    order = [2 * c + i for i in range(2) for c in range(pairs)]
    for t in order:
        pltpu.make_async_copy(jac_hbm.at[t], buf.at[t], sems.at[t]).start()
    for source, dest, k in small:
        pltpu.make_async_copy(source, dest, sems.at[k]).wait()
    g = gain[...]
    retain = 1.0 - g
    for t in order:
        pltpu.make_async_copy(jac_hbm.at[t], buf.at[t], sems.at[t]).wait()
        c = t // 2
        offset = jnp.broadcast_to(g * obs[t : t + 1, :], (PAD, n))
        if t % 2 == 0:
            chain[c, :n] = buf[t].T * retain
            chain[c, n:] = offset
        else:
            moved = dot_nt(chain[c], buf[t]) * retain
            chain[c, :n] = moved[:n]
            chain[c, n:] = moved[n:] + offset
    kept = {(0, pairs): out, (0, pairs // 2): half}
    kept[(0, pairs // 4)] = quarter
    kept[(pairs // 2, 3 * pairs // 4)] = third
    width = 1
    while width < pairs:
        for c in range(0, pairs, 2 * width):
            moved = dot_nn(chain[c], chain[c + width, :n])
            later = chain[c + width, n:]
            span = (c, c + 2 * width)
            dest = kept.get(span, chain.at[c])
            dest[:n] = moved[:n]
            dest[n:] = moved[n:] + later
            if span in kept and 2 * width < pairs:
                chain[c] = dest[...]
        width *= 2


def local_map(jac, obs, gain):
    steps, n, _ = jac.shape
    return kernel_call(
        local_map_body,
        [(n + PAD, n)] * 4,
        [HBM, HBM, HBM],
        (jac, obs, gain),
        "local_map",
        scratch=[
            pltpu.VMEM((steps, n, n), F32),
            pltpu.VMEM((steps, n), F32),
            pltpu.VMEM((1, n), F32),
            pltpu.VMEM((steps // 2, n + PAD, n), F32),
            pltpu.SemaphoreType.DMA((steps + 2,)),
        ],
        flops=12 * steps * n**3,
        size=4 * steps * n * n,
        grant=52,
    )


def join(earlier, later, out):
    n = out.shape[1]
    moved = dot_nn(earlier[...], later[:n])
    out[:n] = moved[:n]
    out[n:] = moved[n:] + later[n:]


def total_body(upper, own, other, out):
    @pl.when(upper[0] == 1)
    def _():
        join(other, own, out)

    @pl.when(upper[0] == 0)
    def _():
        join(own, other, out)


def before_body(upper, before, other, out):
    @pl.when(upper[0] == 1)
    def _():
        join(other, before, out)

    @pl.when(upper[0] == 0)
    def _():
        out[...] = before[...]


def pair_call(body, upper, a, b, name):
    n = a.shape[1]
    return kernel_call(
        body, a.shape, [SMEM, VMEM, VMEM], (upper, a, b), name, flops=12 * n**3, size=12 * n * n
    )


def join_body(earlier, later, out):
    join(earlier, later, out)


def advance_body(count, *refs):
    x, maps, out = refs[0], refs[1 : 1 + count], refs[1 + count]
    n = x.shape[1]
    state = x[...]
    for m in maps:
        state = dot_nn(state, m[:n]) + m[n:]
    out[...] = state


def advance(x, *maps):
    n = x.shape[1]
    return kernel_call(
        functools.partial(advance_body, len(maps)),
        (PAD, n),
        [VMEM] * (1 + len(maps)),
        (x, *maps),
        "advance",
        flops=96 * n * n,
        size=4 * n * n,
    )


def maps_body(first, *refs):
    if first:
        quarter, half, third, jac_hbm, obs, gain, smooth, pi_hbm, pairs, phi = refs[:10]
        pi, later, moving, jac, in_sems, out_sems = refs[10:]
    else:
        given, even, jac_hbm, obs, gain, base_powers, pi_hbm, offset_map = refs[:8]
        pi, later, moving, jac, pairs, in_sems, out_sems = refs[8:]
    n = jac.shape[1]
    size = n + PAD
    lanes = 4
    depth = jac_hbm.shape[0] // lanes
    steps = [(2 * c + i, c * depth + i + (0 if first else 2)) for i in range(2) for c in range(lanes)]
    for k, t in steps:
        pltpu.make_async_copy(jac_hbm.at[t], jac.at[k], in_sems.at[k]).start()
    if first:
        join(half, third, moving.at[3])
        starts = [None, quarter, half, moving.at[3]]
        factor = smooth[...].T
    else:
        starts = [given.at[c] for c in range(4)]
        factor = base_powers[0]
    g = gain[...]
    retain = 1.0 - g
    for k, t in steps:
        c, i = k // 2, k % 2
        pltpu.make_async_copy(jac_hbm.at[t], jac.at[k], in_sems.at[k]).wait()
        source = starts[c] if i == 0 else moving.at[c]
        if source is None:
            pi[k, :n] = jac[k].T
            pi[k, n:] = jnp.zeros((PAD, n), F32)
        else:
            pi[k] = dot_nt(source[...], jac[k])
        pltpu.make_async_copy(pi.at[k], pi_hbm.at[k], out_sems.at[k]).start()
        offset = g * obs[t : t + 1, :]
        predicted = pi[k]
        if i == 0 or first:
            dest = moving if i == 0 else phi
            dest[c, :n] = predicted[:n] * retain
            dest[c, n:] = predicted[n:] * retain + offset
        change = -(predicted * g)
        if i == 0:
            pairs[c, :n] = change[:n]
            pairs[c, n:] = change[n:] + offset
        else:
            later[c * size : c * size + n] = change[:n]
            later[c * size + n : (c + 1) * size] = change[n:] + offset
    moved = dot_nn(later[...], factor)
    for c in range(lanes):
        pairs[c] = pairs[c] + moved[c * size : (c + 1) * size]
    if not first:
        for c in range(lanes):
            later[c * size : (c + 1) * size] = pairs[c]
        moved = dot_nn(later[...], base_powers[1])
        quads = [even[c] + moved[c * size : (c + 1) * size] for c in range(4)]
        halves = [quads[c] + dot_nn(quads[c + 1], base_powers[2]) for c in (0, 2)]
        offset_map[...] = halves[0] + dot_nn(halves[1], base_powers[3])
    for k, t in steps:
        pltpu.make_async_copy(pi.at[k], pi_hbm.at[k], out_sems.at[k]).wait()


def maps(first, starts, jac, obs, gain, factor):
    n = jac.shape[1]
    size = n + PAD
    four = (4, size, n)
    shapes = [(8, size, n)] + ([four, four] if first else [(size, n)])
    scratch = [(8, size, n), (4 * size, n), four, (8, n, n)] + ([] if first else [four])
    return kernel_call(
        functools.partial(maps_body, first),
        shapes,
        [VMEM] * len(starts) + [HBM] + [VMEM] * 3,
        (*starts, jac, obs, gain, factor),
        "maps",
        scratch=[pltpu.VMEM(x, F32) for x in scratch] + [pltpu.SemaphoreType.DMA((8,))] * 2,
        flops=12 * 16 * n**3,
        size=8 * 12 * n * n,
        grant=52,
        out_specs=[HBM] + [VMEM] * (len(shapes) - 1),
    )


def base_powers_body(steps, smooth, base, top):
    square = smooth[...].T
    level = 0
    reach = 1
    while reach < steps:
        base[level] = square
        square = dot_nn(square, square)
        reach *= 2
        level += 1
    top[...] = square


def high_powers_body(top, out):
    square = top[...]
    count = out.shape[0]
    for k in range(count):
        out[k] = square
        if k + 1 < count:
            square = dot_nn(square, square)


def offsets_join_body(level, upper, own_map, other_map, own, other, high, through, out):
    n = out.shape[1]

    @pl.when(upper[0] == 1)
    def _():
        join(other_map, own, through)
        out[...] = other[...] + dot_nn(through[...], high[level])

    @pl.when(upper[0] == 0)
    def _():
        join(own_map, other, through)
        out[...] = own[...] + dot_nn(through[...], high[level])


def inside_body(level, upper, other_map, through, high, before, behind, lift, before_out, behind_out, lift_out):
    @pl.when(upper[0] == 1)
    def _():
        join(other_map, before, before_out)
        join(other_map, behind, behind_out)
        lift_out[...] = lift[...]

    @pl.when(upper[0] == 0)
    def _():
        before_out[...] = before[...]
        behind_out[...] = behind[...] + dot_nn(through[...], lift[...])
        lift_out[...] = dot_nn(lift[...], high[level])


def offset_body(upper, x, chip_map, offset_map, entry, sent):
    n = x.shape[1]
    state = x[...]
    state = jnp.where(upper[0] == 1, dot_nn(state, chip_map[:n]) + chip_map[n:], state)
    entry[...] = state
    value = dot_nn(state, offset_map[:n]) + offset_map[n:]
    sent[...] = jnp.broadcast_to(value[:1][None], sent.shape)


def states_body(entry, before, behind, lift, even, odd, obs, gain, base_powers, filt, base, back, end, pred, shifted):
    steps, n = pred.shape
    g = gain[...]
    state = entry[...]
    inside = dot_nn(state, behind[:n]) + behind[n:]
    back[...] = dot_nn(inside, base_powers[0])
    end[...] = dot_nn(lift[...], base_powers[0])
    state = dot_nn(state, before[:n]) + before[n:]
    for t in range(steps):
        c, i = t // 4, t % 4
        pi = even if i < 2 else odd
        k = 2 * c + i % 2
        predicted = (dot_nn(state, pi[k, :n]) + pi[k, n:])[:1]
        pred[t : t + 1, :] = predicted
        filt[t : t + 1, :] = predicted + g * (obs[t : t + 1, :] - predicted)
    local = filt[...] - pred[...]
    shifted[steps:, :] = jnp.zeros((steps, n), F32)
    level = 0
    reach = 1
    while reach < steps:
        shifted[:steps, :] = local
        local = local + dot_nn(shifted[reach : reach + steps, :], base_powers[level])
        reach *= 2
        level += 1
    base[...] = pred[...] + local


def backward_body(first, place, got, high, back, end, base_powers, base, out):
    steps, n = base.shape
    count = got.shape[0]
    rows = []
    for k in range(count - 1):
        source = place[0] + 1 + k
        value = got[jnp.where(source < count, source, 0)]
        value = jnp.broadcast_to(value, (PAD, n))
        rows.append(jnp.where(source < count, value, jnp.zeros_like(value)))
    rows.append(jnp.zeros((PAD, n), F32))
    level = first
    while len(rows) > 1:
        half = len(rows) // 2
        later = jnp.concatenate([rows[2 * i + 1] for i in range(half)], 0)
        moved = dot_nn(later, high[level])
        rows = [rows[2 * i] + moved[PAD * i : PAD * (i + 1)] for i in range(half)]
        level += 1
    value = back[...] + dot_nn(rows[0], end[...])
    left = steps - 1 - lax.broadcasted_iota(jnp.int32, (steps, n), 0)
    value = jnp.concatenate([value, value], 0)
    for level in range(base_powers.shape[0]):
        value = jnp.where((left >> level) % 2 == 1, dot_nn(value, base_powers[level]), value)
    out[...] = base[...] + value


def shards(jac, obs, gain_filter, gain_smooth, init_mean):
    steps, n, _ = jac.shape
    inner_count, outer_count = lax.axis_size("inner"), lax.axis_size("outer")
    counts = {"inner": inner_count, "outer": outer_count}
    inner, outer = lax.axis_index("inner"), lax.axis_index("outer")
    gain = gain_filter[None, :]

    def bit(index, k):
        return ((index >> k) % 2).astype(jnp.int32)[None]

    def exchange(total, axis, flip, beside):
        other = lax.ppermute(total, axis, [(i, i ^ flip) for i in range(counts[axis])])
        work = beside()
        return lax.optimization_barrier((other, work))

    with jax.named_scope("compose"):
        total, quarter, half, third = local_map(jac, obs, gain)

    def base_work():
        levels = steps.bit_length() - 1
        return kernel_call(
            functools.partial(base_powers_body, steps),
            [(levels, n, n), (n, n)],
            [VMEM],
            (gain_smooth,),
            "base_powers",
            flops=60 * n**3,
            size=20 * n * n,
        )

    eye = jnp.eye(n, dtype=F32)
    aside = {
        "before": jnp.concatenate([eye, jnp.zeros((PAD, n), F32)], 0),
        "behind": jnp.zeros((n + PAD, n), F32),
        "lift": eye,
    }

    def offsets_join(level, upper, own_map, other_map, own, other):
        return kernel_call(
            functools.partial(offsets_join_body, level),
            [(n + PAD, n), (n + PAD, n)],
            [SMEM] + [VMEM] * 5,
            (upper, own_map, other_map, own, other, high),
            "offsets_join",
            flops=24 * n**3,
            size=28 * n * n,
            grant=6,
        )

    def inside(level, upper, other_map, through):
        made = kernel_call(
            functools.partial(inside_body, level),
            [(n + PAD, n), (n + PAD, n), (n, n)],
            [SMEM] + [VMEM] * 6,
            (upper, other_map, through, high, aside["before"], aside["behind"], aside["lift"]),
            "inside",
            flops=24 * n**3,
            size=36 * n * n,
            grant=6,
        )
        aside["before"], aside["behind"], aside["lift"] = made
        return made

    def partner(value, axis, flip):
        return lax.ppermute(value, axis, [(i, i ^ flip) for i in range(counts[axis])])

    uppers = [bit(inner, 0), bit(inner, 1), bit(inner, 2), bit(inner, 3), bit(outer, 0)]
    own_maps, other_maps = [total], []
    with jax.named_scope("join_0"):
        other, (pi_even, even, phi) = exchange(
            total,
            "inner",
            1,
            lambda: maps(True, (quarter, half, third), jac, obs, gain, gain_smooth),
        )
        other_maps.append(other)
        own_maps.append(pair_call(total_body, uppers[0], own_maps[0], other, "total"))
    with jax.named_scope("join_1"):

        def work():
            base_powers, top = base_work()
            pi_odd, offset_map = maps(False, (phi, even), jac, obs, gain, base_powers)
            return base_powers, top, pi_odd, offset_map

        other, (base_powers, top, pi_odd, offsets) = exchange(own_maps[1], "inner", 3, work)
        other_maps.append(other)
        own_maps.append(pair_call(total_body, uppers[1], own_maps[1], other, "total"))
    with jax.named_scope("join_2"):

        def work():
            return kernel_call(
                high_powers_body,
                (8, n, n),
                [VMEM],
                (top,),
                "high_powers",
                flops=84 * n**3,
                size=36 * n * n,
                grant=6,
            )

        far = partner(offsets, "inner", 1)
        other, high = exchange(own_maps[2], "inner", 4, work)
        other_maps.append(other)
        own_maps.append(pair_call(total_body, uppers[2], own_maps[2], other, "total"))
    with jax.named_scope("join_3"):

        def work():
            return offsets_join(0, uppers[0], own_maps[0], other_maps[0], offsets, far)

        other, (through, offsets) = exchange(own_maps[3], "inner", 12, work)
        far = partner(offsets, "inner", 3)
        inside(0, uppers[0], other_maps[0], through)
        other_maps.append(other)
        own_maps.append(pair_call(total_body, uppers[3], own_maps[3], other, "total"))
    with jax.named_scope("join_core"):
        other = partner(own_maps[4], "outer", 1)
        other_maps.append(other)
        own_maps.append(pair_call(total_body, uppers[4], own_maps[4], other, "total"))
    with jax.named_scope("join_z"):

        def work():
            return offsets_join(1, uppers[1], own_maps[1], other_maps[1], offsets, far)

        chip_map, (through, offsets) = exchange(own_maps[5], "outer", 2, work)
        far = partner(offsets, "inner", 4)
        inside(1, uppers[1], other_maps[1], through)
        total = pair_call(total_body, bit(outer, 1), own_maps[5], chip_map, "total")

    group = outer_count // 4
    super_here = outer // group
    x = jnp.broadcast_to(init_mean[None, :], (PAD, n))

    def mirror(source, dest):
        return [
            (source * group + z * 2 + c, dest * group + (group // 2 - 1 - z) * 2 + c)
            for z in range(group // 2)
            for c in range(2)
        ]

    with jax.named_scope("hop_0"):
        y = advance(x, total)
        arrived = lax.ppermute(y, "outer", mirror(0, 1))
        through, offsets = offsets_join(2, uppers[2], own_maps[2], other_maps[2], offsets, far)
        arrived, offsets = lax.optimization_barrier((arrived, offsets))
        far = partner(offsets, "inner", 12)
        inside(2, uppers[2], other_maps[2], through)
        x = jnp.where(super_here == 1, arrived, x)
    with jax.named_scope("hop_1"):
        y = advance(x, total)
        near = lax.ppermute(y, "outer", mirror(1, 2))
        farther = lax.ppermute(y, "outer", mirror(1, 3))
        skipped = lax.ppermute(total, "outer", mirror(2, 3))
        through, offsets = offsets_join(3, uppers[3], own_maps[3], other_maps[3], offsets, far)
        near, farther, offsets = lax.optimization_barrier((near, farther, offsets))
        far = partner(offsets, "outer", 1)
        inside(3, uppers[3], other_maps[3], through)
        x = jnp.where(super_here == 2, near, x)
        x = jnp.where(super_here == 3, advance(farther, skipped), x)
    with jax.named_scope("offset"):
        through, offsets = offsets_join(4, uppers[4], own_maps[4], other_maps[4], offsets, far)
        chips = outer_count // 2
        entry, sent = kernel_call(
            offset_body,
            [(PAD, n), (chips, 1, n)],
            [SMEM] + [VMEM] * 3,
            (bit(outer, 1), x, chip_map, offsets),
            "offset",
            flops=192 * n * n,
            size=8 * n * n,
        )
        cores = [[2 * z + c for z in range(chips)] for c in range(2)]
        got = lax.all_to_all(sent, "outer", 0, 0, axis_index_groups=cores, tiled=True)
        inside(4, uppers[4], other_maps[4], through)
        filt, base, back, end = kernel_call(
            states_body,
            [(steps, n), (steps, n), (PAD, n), (n, n)],
            [VMEM] * 9,
            (entry, aside["before"], aside["behind"], aside["lift"], pi_even, pi_odd, obs, gain, base_powers),
            "states",
            scratch=[pltpu.VMEM((steps, n), F32), pltpu.VMEM((2 * steps, n), F32)],
            flops=12 * n**3 + 30 * 96 * n * n,
            size=80 * n * n,
            grant=8,
        )
        got, base = lax.optimization_barrier((got, base))
    with jax.named_scope("backward"):
        smoothed = kernel_call(
            functools.partial(backward_body, 5),
            (steps, n),
            [SMEM] + [VMEM] * 6,
            ((outer // 2).astype(jnp.int32)[None], got, high, back, end, base_powers, base),
            "backward",
            flops=600 * n * n,
            size=24 * n * n,
            grant=6,
        )
    return (filt, smoothed)


def solution(mesh):
    return jax.shard_map(
        shards,
        mesh=mesh,
        in_specs=(P(("outer", "inner"), None, None), P(("outer", "inner"), None), P(), P(), P()),
        out_specs=(P(("outer", "inner"), None), P(("outer", "inner"), None)),
        check_vma=False,
    )
```

```python
import functools

import jax
import jax.numpy as jnp
from jax import lax
from jax.experimental import pallas as pl
from jax.experimental.pallas import tpu as pltpu
from jax.sharding import PartitionSpec as P

HIGHEST = lax.Precision.HIGHEST
F32 = jnp.float32
VMEM = pl.BlockSpec(memory_space=pltpu.VMEM)
SMEM = pl.BlockSpec(memory_space=pltpu.SMEM)
HBM = pl.BlockSpec(memory_space=pltpu.MemorySpace.HBM)
PAD = 8


def dot_nn(a, b):
    return lax.dot_general(
        a, b, (((1,), (0,)), ((), ())), precision=HIGHEST, preferred_element_type=F32
    )


def dot_nt(a, b):
    return lax.dot_general(
        a, b, (((1,), (1,)), ((), ())), precision=HIGHEST, preferred_element_type=F32
    )


def kernel_call(body, out_shape, in_specs, args, name, scratch=(), flops=0, size=0, grant=4, out_specs=None):
    many = isinstance(out_shape, list)
    shapes = [jax.ShapeDtypeStruct(s, F32) for s in (out_shape if many else [out_shape])]
    out = pl.pallas_call(
        body,
        out_shape=shapes,
        in_specs=in_specs,
        out_specs=out_specs or [VMEM] * len(shapes),
        scratch_shapes=list(scratch),
        cost_estimate=pl.CostEstimate(flops=flops, bytes_accessed=size, transcendentals=0),
        compiler_params=pltpu.CompilerParams(vmem_limit_bytes=grant << 20),
        name=name,
    )(*args)
    return out if many else out[0]


def local_map_body(place, jac_hbm, obs_hbm, gain_hbm, out, quarter, half, third, buf, obs, gain, chain, sems):
    steps, n, _ = buf.shape
    small = [(obs_hbm, obs, steps), (gain_hbm, gain, steps + 1)]
    for source, dest, k in small:
        pltpu.make_async_copy(source, dest, sems.at[k]).start()
    pairs = steps // 2
    order = [2 * c + i for i in range(2) for c in range(pairs)]
    for t in order:
        pltpu.make_async_copy(jac_hbm.at[t], buf.at[t], sems.at[t]).start()
    for source, dest, k in small:
        pltpu.make_async_copy(source, dest, sems.at[k]).wait()
    g = gain[...]
    retain = 1.0 - g
    for t in order:
        pltpu.make_async_copy(jac_hbm.at[t], buf.at[t], sems.at[t]).wait()
        c = t // 2
        offset = jnp.broadcast_to(g * obs[t : t + 1, :], (PAD, n))
        if t % 2 == 0:
            chain[c, :n] = buf[t].T * retain
            chain[c, n:] = offset
        else:
            moved = dot_nt(chain[c], buf[t]) * retain
            chain[c, :n] = moved[:n]
            chain[c, n:] = moved[n:] + offset
    kept = {(0, pairs): out, (0, pairs // 2): half}
    kept[(0, pairs // 4)] = quarter
    kept[(pairs // 2, 3 * pairs // 4)] = third
    width = 1
    while width < pairs:
        for c in range(0, pairs, 2 * width):
            moved = dot_nn(chain[c], chain[c + width, :n])
            later = chain[c + width, n:]
            span = (c, c + 2 * width)
            dest = kept.get(span, chain.at[c])
            dest[:n] = moved[:n]
            dest[n:] = moved[n:] + later
            if span in kept and 2 * width < pairs:
                chain[c] = dest[...]
        width *= 2


def local_map(place, jac, obs, gain):
    steps, n, _ = jac.shape
    return kernel_call(
        local_map_body,
        [(n + PAD, n)] * 4 + [(steps, n, n)],
        [SMEM, HBM, HBM, HBM],
        (place, jac, obs, gain),
        "local_map",
        scratch=[
            pltpu.VMEM((steps, n), F32),
            pltpu.VMEM((1, n), F32),
            pltpu.VMEM((steps // 2, n + PAD, n), F32),
            pltpu.SemaphoreType.DMA((steps + 2,)),
        ],
        flops=12 * steps * n**3,
        size=4 * steps * n * n,
        grant=47,
    )


def join(earlier, later, out):
    n = out.shape[1]
    moved = dot_nn(earlier[...], later[:n])
    out[:n] = moved[:n]
    out[n:] = moved[n:] + later[n:]


def late(place, level):
    return jnp.bitwise_and(jnp.right_shift(place[level // 4], level % 4), 1) == 1


def total_body(level, place, own, other, out):
    @pl.when(late(place, level))
    def _():
        join(other, own, out)

    @pl.when(jnp.logical_not(late(place, level)))
    def _():
        join(own, other, out)


def total_call(level, place, a, b):
    n = a.shape[1]
    return kernel_call(
        functools.partial(total_body, level),
        a.shape,
        [SMEM, VMEM, VMEM],
        (place, a, b),
        "total",
        flops=12 * n**3,
        size=12 * n * n,
    )


def hop_body(stage, place, first, arrived, group_map, out):
    n = out.shape[1]
    state = jnp.broadcast_to(first[...], (PAD, n))
    if stage == 1:
        state = jnp.where(jnp.right_shift(place[1], 2) == 1, arrived[...], state)
    out[...] = dot_nn(state, group_map[:n]) + group_map[n:]


def hop(stage, place, first, arrived, group_map):
    n = group_map.shape[1]
    return kernel_call(
        functools.partial(hop_body, stage),
        (PAD, n),
        [SMEM] + [VMEM] * 3,
        (place, first, arrived, group_map),
        "hop",
        flops=96 * n * n,
        size=4 * n * n,
    )


def maps_body(first, *refs):
    if first:
        quarter, half, third, jac, obs, gain, smooth, pi, pairs, phi = refs[:10]
        later, moving = refs[10:]
    else:
        given, even, jac, obs, gain, base_powers, pi, offset_map = refs[:8]
        later, moving, pairs = refs[8:]
    n = jac.shape[1]
    size = n + PAD
    lanes = 4
    depth = jac.shape[0] // lanes
    steps = [(2 * c + i, c * depth + i + (0 if first else 2)) for i in range(2) for c in range(lanes)]
    if first:
        join(half, third, moving.at[3])
        starts = [None, quarter, half, moving.at[3]]
        factor = smooth[...].T
    else:
        starts = [given.at[c] for c in range(4)]
        factor = base_powers[0]
    g = gain[...]
    retain = 1.0 - g
    for k, t in steps:
        c, i = k // 2, k % 2
        source = starts[c] if i == 0 else moving.at[c]
        if source is None:
            pi[k, :n] = jac[t].T
            pi[k, n:] = jnp.zeros((PAD, n), F32)
        else:
            pi[k] = dot_nt(source[...], jac[t])
        offset = g * obs[t : t + 1, :]
        predicted = pi[k]
        if i == 0 or first:
            dest = moving if i == 0 else phi
            dest[c, :n] = predicted[:n] * retain
            dest[c, n:] = predicted[n:] * retain + offset
        change = -(predicted * g)
        if i == 0:
            pairs[c, :n] = change[:n]
            pairs[c, n:] = change[n:] + offset
        else:
            later[c * size : c * size + n] = change[:n]
            later[c * size + n : (c + 1) * size] = change[n:] + offset
    moved = dot_nn(later[...], factor)
    for c in range(lanes):
        pairs[c] = pairs[c] + moved[c * size : (c + 1) * size]
    if not first:
        for c in range(lanes):
            later[c * size : (c + 1) * size] = pairs[c]
        moved = dot_nn(later[...], base_powers[1])
        quads = [even[c] + moved[c * size : (c + 1) * size] for c in range(4)]
        halves = [quads[c] + dot_nn(quads[c + 1], base_powers[2]) for c in (0, 2)]
        offset_map[...] = halves[0] + dot_nn(halves[1], base_powers[3])


def maps(first, starts, jac, obs, gain, factor):
    n = jac.shape[1]
    size = n + PAD
    four = (4, size, n)
    shapes = [(8, size, n)] + ([four, four] if first else [(size, n)])
    scratch = [(4 * size, n), four] + ([] if first else [four])
    return kernel_call(
        functools.partial(maps_body, first),
        shapes,
        [VMEM] * (len(starts) + 4),
        (*starts, jac, obs, gain, factor),
        "maps",
        scratch=[pltpu.VMEM(x, F32) for x in scratch],
        flops=12 * 16 * n**3,
        size=8 * 12 * n * n,
        grant=8,
    )


def base_powers_body(steps, smooth, base, top):
    square = smooth[...].T
    level = 0
    reach = 1
    while reach < steps:
        base[level] = square
        square = dot_nn(square, square)
        reach *= 2
        level += 1
    top[...] = square


def high_powers_body(top, *outs):
    square = top[...]
    for out in outs:
        square = dot_nn(square, square)
        out[...] = square


def offsets_join_body(level, place, own_map, other_map, own, other, factor, through, out):
    n = out.shape[1]

    @pl.when(late(place, level))
    def _():
        join(other_map, own, through)
        out[...] = other[...] + dot_nn(through[...], factor[...])

    @pl.when(jnp.logical_not(late(place, level)))
    def _():
        join(own_map, other, through)
        out[...] = own[...] + dot_nn(through[...], factor[...])


def inside_body(level, place, other_map, through, factor, *refs):
    before_out, behind_out, lift_out = refs[-3:]
    n = factor.shape[1]
    if level == 0:
        row = lax.broadcasted_iota(jnp.int32, (n + PAD, n), 0)
        column = lax.broadcasted_iota(jnp.int32, (n + PAD, n), 1)
        eye = jnp.where(row == column, 1.0, 0.0).astype(F32)
        is_late = late(place, level)
        before_out[...] = jnp.where(is_late, other_map[...], eye)
        behind_out[...] = jnp.where(is_late, jnp.zeros_like(eye), through[...])
        lift_out[...] = jnp.where(is_late, eye[:n], factor[...])
        return
    before, behind, lift = refs[:3]

    @pl.when(late(place, level))
    def _():
        join(other_map, before, before_out)
        join(other_map, behind, behind_out)
        lift_out[...] = lift[...]

    @pl.when(jnp.logical_not(late(place, level)))
    def _():
        before_out[...] = before[...]
        behind_out[...] = behind[...] + dot_nn(through[...], lift[...])
        lift_out[...] = dot_nn(lift[...], factor[...])


def offset_body(place, first, arrived, near, far, skipped, chip_map, offset_map, entry, sent):
    n = chip_map.shape[1]
    here = jnp.right_shift(place[1], 2)
    state = dot_nn(far[...], skipped[:n]) + skipped[n:]
    state = jnp.where(here == 3, state, near[...])
    state = jnp.where(here == 1, arrived[...], state)
    state = jnp.where(here == 0, jnp.broadcast_to(first[...], (PAD, n)), state)
    moved = dot_nn(state, chip_map[:n]) + chip_map[n:]
    state = jnp.where(late(place, 5), moved, state)
    entry[...] = state
    value = dot_nn(state, offset_map[:n]) + offset_map[n:]
    sent[...] = jnp.broadcast_to(value[:1][None], sent.shape)


def states_body(entry, before, behind, lift, even, odd, obs, gain, base_powers, filt, base, back, end, pred, shifted):
    steps, n = pred.shape
    g = gain[...]
    state = entry[...]
    inside = dot_nn(state, behind[:n]) + behind[n:]
    back[...] = dot_nn(inside, base_powers[0])
    end[...] = dot_nn(lift[...], base_powers[0])
    state = dot_nn(state, before[:n]) + before[n:]
    for t in range(steps):
        c, i = t // 4, t % 4
        pi = even if i < 2 else odd
        k = 2 * c + i % 2
        predicted = (dot_nn(state, pi[k, :n]) + pi[k, n:])[:1]
        pred[t : t + 1, :] = predicted
        filt[t : t + 1, :] = predicted + g * (obs[t : t + 1, :] - predicted)
    local = filt[...] - pred[...]
    shifted[steps:, :] = jnp.zeros((steps, n), F32)
    level = 0
    reach = 1
    while reach < steps:
        shifted[:steps, :] = local
        local = local + dot_nn(shifted[reach : reach + steps, :], base_powers[level])
        reach *= 2
        level += 1
    base[...] = pred[...] + local


def backward_body(place, got, unit, double, fourth, back, end, base_powers, base, out):
    steps, n = base.shape
    count = got.shape[0]
    rows = []
    for k in range(count - 1):
        source = jnp.right_shift(place[1], 1) + 1 + k
        value = got[jnp.where(source < count, source, 0)]
        value = jnp.broadcast_to(value, (PAD, n))
        rows.append(jnp.where(source < count, value, jnp.zeros_like(value)))
    rows.append(jnp.zeros((PAD, n), F32))
    for factor in (unit, double, fourth):
        half = len(rows) // 2
        later = jnp.concatenate([rows[2 * i + 1] for i in range(half)], 0)
        moved = dot_nn(later, factor[...])
        rows = [rows[2 * i] + moved[PAD * i : PAD * (i + 1)] for i in range(half)]
    value = back[...] + dot_nn(rows[0], end[...])
    left = steps - 1 - lax.broadcasted_iota(jnp.int32, (steps, n), 0)
    value = jnp.concatenate([value, value], 0)
    for level in range(base_powers.shape[0]):
        value = jnp.where((left >> level) % 2 == 1, dot_nn(value, base_powers[level]), value)
    out[...] = base[...] + value


def shards(jac, obs, gain_filter, gain_smooth, init_mean):
    steps, n, _ = jac.shape
    inner_count, outer_count = lax.axis_size("inner"), lax.axis_size("outer")
    counts = {"inner": inner_count, "outer": outer_count}
    place = jnp.stack([lax.axis_index("inner"), lax.axis_index("outer")]).astype(jnp.int32)
    gain = gain_filter[None, :]
    first = init_mean[None, :]

    def exchange(total, axis, flip, beside):
        other = lax.ppermute(total, axis, [(i, i ^ flip) for i in range(counts[axis])])
        work = beside()
        return lax.optimization_barrier((other, work))

    with jax.named_scope("compose"):
        total, quarter, half, third, loaded = local_map(place, jac, obs, gain)

    def base_work():
        levels = steps.bit_length() - 1
        return kernel_call(
            functools.partial(base_powers_body, steps),
            [(levels, n, n), (n, n)],
            [VMEM],
            (gain_smooth,),
            "base_powers",
            flops=60 * n**3,
            size=20 * n * n,
        )

    aside = []

    def offsets_join(level, own_map, other_map, own, other):
        return kernel_call(
            functools.partial(offsets_join_body, level),
            [(n + PAD, n), (n + PAD, n)],
            [SMEM] + [VMEM] * 5,
            (place, own_map, other_map, own, other, high[level]),
            "offsets_join",
            flops=24 * n**3,
            size=28 * n * n,
            grant=6,
        )

    def inside(level, other_map, through):
        aside[:] = kernel_call(
            functools.partial(inside_body, level),
            [(n + PAD, n), (n + PAD, n), (n, n)],
            [SMEM] + [VMEM] * (3 + len(aside)),
            (place, other_map, through, high[level], *aside),
            "inside",
            flops=24 * n**3,
            size=36 * n * n,
        )

    def partner(value, axis, flip):
        return lax.ppermute(value, axis, [(i, i ^ flip) for i in range(counts[axis])])

    own_maps, other_maps = [total], []
    with jax.named_scope("join_0"):
        other, (pi_even, even, phi) = exchange(
            total,
            "inner",
            1,
            lambda: maps(True, (quarter, half, third), loaded, obs, gain, gain_smooth),
        )
        other_maps.append(other)
        own_maps.append(total_call(0, place, own_maps[0], other))
    with jax.named_scope("join_1"):

        def work():
            base_powers, top = base_work()
            pi_odd, offset_map = maps(False, (phi, even), loaded, obs, gain, base_powers)
            return base_powers, top, pi_odd, offset_map

        other, (base_powers, top, pi_odd, offsets) = exchange(own_maps[1], "inner", 3, work)
        other_maps.append(other)
        own_maps.append(total_call(1, place, own_maps[1], other))
    with jax.named_scope("join_2"):

        def work():
            return kernel_call(
                high_powers_body,
                [(n, n)] * 7,
                [VMEM],
                (top,),
                "high_powers",
                flops=84 * n**3,
                size=36 * n * n,
                grant=6,
            )

        far = partner(offsets, "inner", 1)
        other, high = exchange(own_maps[2], "inner", 4, work)
        high = [top, *high]
        other_maps.append(other)
        own_maps.append(total_call(2, place, own_maps[2], other))
    with jax.named_scope("join_3"):

        def work():
            return offsets_join(0, own_maps[0], other_maps[0], offsets, far)

        other, (through, offsets) = exchange(own_maps[3], "inner", 12, work)
        far = partner(offsets, "inner", 3)
        inside(0, other_maps[0], through)
        other_maps.append(other)
        own_maps.append(total_call(3, place, own_maps[3], other))
    with jax.named_scope("join_core"):
        other = partner(own_maps[4], "outer", 1)
        other_maps.append(other)
        own_maps.append(total_call(4, place, own_maps[4], other))
    with jax.named_scope("join_z"):

        def work():
            return offsets_join(1, own_maps[1], other_maps[1], offsets, far)

        chip_map, (through, offsets) = exchange(own_maps[5], "outer", 2, work)
        far = partner(offsets, "inner", 4)
        inside(1, other_maps[1], through)
        total = total_call(5, place, own_maps[5], chip_map)

    group = outer_count // 4
    def mirror(source, dest):
        return [
            (source * group + z * 2 + c, dest * group + (group // 2 - 1 - z) * 2 + c)
            for z in range(group // 2)
            for c in range(2)
        ]

    with jax.named_scope("hop_0"):
        y = hop(0, place, first, first, total)
        arrived = lax.ppermute(y, "outer", mirror(0, 1))
        through, offsets = offsets_join(2, own_maps[2], other_maps[2], offsets, far)
        arrived, offsets, aside[:] = lax.optimization_barrier((arrived, offsets, aside))
        far = partner(offsets, "inner", 12)
        inside(2, other_maps[2], through)
    with jax.named_scope("hop_1"):
        y = hop(1, place, first, arrived, total)
        near = lax.ppermute(y, "outer", mirror(1, 2))
        farther = lax.ppermute(y, "outer", mirror(1, 3))
        skipped = lax.ppermute(total, "outer", mirror(2, 3))
        through, offsets = offsets_join(3, own_maps[3], other_maps[3], offsets, far)
        near, farther, offsets, aside[:] = lax.optimization_barrier((near, farther, offsets, aside))
        far = partner(offsets, "outer", 1)
        inside(3, other_maps[3], through)
    with jax.named_scope("offset"):
        through, offsets = offsets_join(4, own_maps[4], other_maps[4], offsets, far)
        chips = outer_count // 2
        entry, sent = kernel_call(
            offset_body,
            [(PAD, n), (chips, 1, n)],
            [SMEM] + [VMEM] * 7,
            (place, first, arrived, near, farther, skipped, chip_map, offsets),
            "offset",
            flops=192 * n * n,
            size=8 * n * n,
        )
        cores = [[2 * z + c for z in range(chips)] for c in range(2)]
        got = lax.all_to_all(sent, "outer", 0, 0, axis_index_groups=cores, tiled=True)
        inside(4, other_maps[4], through)
        filt, base, back, end = kernel_call(
            states_body,
            [(steps, n), (steps, n), (PAD, n), (n, n)],
            [VMEM] * 9,
            (entry, *aside, pi_even, pi_odd, obs, gain, base_powers),
            "states",
            scratch=[pltpu.VMEM((steps, n), F32), pltpu.VMEM((2 * steps, n), F32)],
            flops=12 * n**3 + 30 * 96 * n * n,
            size=80 * n * n,
            grant=8,
        )
        got, base = lax.optimization_barrier((got, base))
    with jax.named_scope("backward"):
        smoothed = kernel_call(
            backward_body,
            (steps, n),
            [SMEM] + [VMEM] * 8,
            (place, got, *high[5:], back, end, base_powers, base),
            "backward",
            flops=600 * n * n,
            size=24 * n * n,
            grant=6,
        )
    return (filt, smoothed)


def solution(mesh):
    return jax.shard_map(
        shards,
        mesh=mesh,
        in_specs=(P(("outer", "inner"), None, None), P(("outer", "inner"), None), P(), P(), P()),
        out_specs=(P(("outer", "inner"), None), P(("outer", "inner"), None)),
        check_vma=False,
    )
```

```python
import functools

import jax
import jax.numpy as jnp
from jax import lax
from jax.experimental import pallas as pl
from jax.experimental.pallas import tpu as pltpu
from jax.sharding import PartitionSpec as P

HIGHEST = lax.Precision.HIGHEST
F32 = jnp.float32
VMEM = pl.BlockSpec(memory_space=pltpu.VMEM)
SMEM = pl.BlockSpec(memory_space=pltpu.SMEM)
HBM = pl.BlockSpec(memory_space=pltpu.MemorySpace.HBM)
PAD = 8


def dot_nn(a, b):
    return lax.dot_general(
        a, b, (((1,), (0,)), ((), ())), precision=HIGHEST, preferred_element_type=F32
    )


def dot_nt(a, b):
    return lax.dot_general(
        a, b, (((1,), (1,)), ((), ())), precision=HIGHEST, preferred_element_type=F32
    )


def kernel_call(body, out_shape, in_specs, args, name, scratch=(), flops=0, size=0, grant=4, out_specs=None):
    many = isinstance(out_shape, list)
    shapes = [jax.ShapeDtypeStruct(s, F32) for s in (out_shape if many else [out_shape])]
    out = pl.pallas_call(
        body,
        out_shape=shapes,
        in_specs=in_specs,
        out_specs=out_specs or [VMEM] * len(shapes),
        scratch_shapes=list(scratch),
        cost_estimate=pl.CostEstimate(flops=flops, bytes_accessed=size, transcendentals=0),
        compiler_params=pltpu.CompilerParams(vmem_limit_bytes=grant << 20),
        name=name,
    )(*args)
    return out if many else out[0]


def local_map_body(inner, outer, jac_hbm, obs_hbm, gain_hbm, out, quarter, half, third, buf, obs, gain, chain, sems):
    steps, n, _ = buf.shape
    small = [(obs_hbm, obs, steps), (gain_hbm, gain, steps + 1)]
    for source, dest, k in small:
        pltpu.make_async_copy(source, dest, sems.at[k]).start()
    pairs = steps // 2
    order = [2 * c + i for i in range(2) for c in range(pairs)]
    for t in order:
        pltpu.make_async_copy(jac_hbm.at[t], buf.at[t], sems.at[t]).start()
    for source, dest, k in small:
        pltpu.make_async_copy(source, dest, sems.at[k]).wait()
    g = gain[...]
    retain = 1.0 - g
    for t in order:
        pltpu.make_async_copy(jac_hbm.at[t], buf.at[t], sems.at[t]).wait()
        c = t // 2
        offset = jnp.broadcast_to(g * obs[t : t + 1, :], (PAD, n))
        if t % 2 == 0:
            chain[c, :n] = buf[t].T * retain
            chain[c, n:] = offset
        else:
            moved = dot_nt(chain[c], buf[t]) * retain
            chain[c, :n] = moved[:n]
            chain[c, n:] = moved[n:] + offset
    kept = {(0, pairs): out, (0, pairs // 2): half}
    kept[(0, pairs // 4)] = quarter
    kept[(pairs // 2, 3 * pairs // 4)] = third
    width = 1
    while width < pairs:
        for c in range(0, pairs, 2 * width):
            moved = dot_nn(chain[c], chain[c + width, :n])
            later = chain[c + width, n:]
            span = (c, c + 2 * width)
            dest = kept.get(span, chain.at[c])
            dest[:n] = moved[:n]
            dest[n:] = moved[n:] + later
            if span in kept and 2 * width < pairs:
                chain[c] = dest[...]
        width *= 2


def local_map(place, jac, obs, gain):
    steps, n, _ = jac.shape
    return kernel_call(
        local_map_body,
        [(n + PAD, n)] * 4 + [(steps, n, n)],
        [SMEM, SMEM, HBM, HBM, HBM],
        (*place, jac, obs, gain),
        "local_map",
        scratch=[
            pltpu.VMEM((steps, n), F32),
            pltpu.VMEM((1, n), F32),
            pltpu.VMEM((steps // 2, n + PAD, n), F32),
            pltpu.SemaphoreType.DMA((steps + 2,)),
        ],
        flops=12 * steps * n**3,
        size=4 * steps * n * n,
        grant=47,
    )


def join(earlier, later, out):
    n = out.shape[1]
    moved = dot_nn(earlier[...], later[:n])
    out[:n] = moved[:n]
    out[n:] = moved[n:] + later[n:]


def late(inner, outer, level):
    index = inner if level < 4 else outer
    return jnp.bitwise_and(jnp.right_shift(index[0], level % 4), 1) == 1


def total_body(level, inner, outer, own, other, out):
    @pl.when(late(inner, outer, level))
    def _():
        join(other, own, out)

    @pl.when(jnp.logical_not(late(inner, outer, level)))
    def _():
        join(own, other, out)


def total_call(level, place, a, b):
    n = a.shape[1]
    return kernel_call(
        functools.partial(total_body, level),
        a.shape,
        [SMEM, SMEM, VMEM, VMEM],
        (*place, a, b),
        "total",
        flops=12 * n**3,
        size=12 * n * n,
    )


def hop_body(stage, outer, first, arrived, group_map, out):
    n = out.shape[1]
    state = jnp.broadcast_to(first[...], (PAD, n))
    if stage == 1:
        state = jnp.where(jnp.right_shift(outer[0], 2) == 1, arrived[...], state)
    out[...] = dot_nn(state, group_map[:n]) + group_map[n:]


def hop(stage, place, first, arrived, group_map):
    n = group_map.shape[1]
    return kernel_call(
        functools.partial(hop_body, stage),
        (PAD, n),
        [SMEM] + [VMEM] * 3,
        (place[1], first, arrived, group_map),
        "hop",
        flops=96 * n * n,
        size=4 * n * n,
    )


def maps_body(first, *refs):
    if first:
        quarter, half, third, jac, obs, gain, smooth, pi, pairs, phi = refs[:10]
        later, moving = refs[10:]
    else:
        given, even, jac, obs, gain, base_powers, pi, offset_map = refs[:8]
        later, moving, pairs = refs[8:]
    n = jac.shape[1]
    size = n + PAD
    lanes = 4
    depth = jac.shape[0] // lanes
    steps = [(2 * c + i, c * depth + i + (0 if first else 2)) for i in range(2) for c in range(lanes)]
    if first:
        join(half, third, moving.at[3])
        starts = [None, quarter, half, moving.at[3]]
        factor = smooth[...].T
    else:
        starts = [given.at[c] for c in range(4)]
        factor = base_powers[0]
    g = gain[...]
    retain = 1.0 - g
    for k, t in steps:
        c, i = k // 2, k % 2
        source = starts[c] if i == 0 else moving.at[c]
        if source is None:
            pi[k, :n] = jac[t].T
            pi[k, n:] = jnp.zeros((PAD, n), F32)
        else:
            pi[k] = dot_nt(source[...], jac[t])
        offset = g * obs[t : t + 1, :]
        predicted = pi[k]
        if i == 0 or first:
            dest = moving if i == 0 else phi
            dest[c, :n] = predicted[:n] * retain
            dest[c, n:] = predicted[n:] * retain + offset
        change = -(predicted * g)
        if i == 0:
            pairs[c, :n] = change[:n]
            pairs[c, n:] = change[n:] + offset
        else:
            later[c * size : c * size + n] = change[:n]
            later[c * size + n : (c + 1) * size] = change[n:] + offset
    moved = dot_nn(later[...], factor)
    for c in range(lanes):
        pairs[c] = pairs[c] + moved[c * size : (c + 1) * size]
    if not first:
        for c in range(lanes):
            later[c * size : (c + 1) * size] = pairs[c]
        moved = dot_nn(later[...], base_powers[1])
        quads = [even[c] + moved[c * size : (c + 1) * size] for c in range(4)]
        halves = [quads[c] + dot_nn(quads[c + 1], base_powers[2]) for c in (0, 2)]
        offset_map[...] = halves[0] + dot_nn(halves[1], base_powers[3])


def maps(first, starts, jac, obs, gain, factor):
    n = jac.shape[1]
    size = n + PAD
    four = (4, size, n)
    shapes = [(8, size, n)] + ([four, four] if first else [(size, n)])
    scratch = [(4 * size, n), four] + ([] if first else [four])
    return kernel_call(
        functools.partial(maps_body, first),
        shapes,
        [VMEM] * (len(starts) + 4),
        (*starts, jac, obs, gain, factor),
        "maps",
        scratch=[pltpu.VMEM(x, F32) for x in scratch],
        flops=12 * 16 * n**3,
        size=8 * 12 * n * n,
        grant=8,
    )


def base_powers_body(steps, smooth, base, top):
    square = smooth[...].T
    level = 0
    reach = 1
    while reach < steps:
        base[level] = square
        square = dot_nn(square, square)
        reach *= 2
        level += 1
    top[...] = square


def high_powers_body(top, *outs):
    square = top[...]
    for out in outs:
        square = dot_nn(square, square)
        out[...] = square


def offsets_join_body(level, inner, outer, own_map, other_map, own, other, factor, through, out):
    n = out.shape[1]

    @pl.when(late(inner, outer, level))
    def _():
        join(other_map, own, through)
        out[...] = other[...] + dot_nn(through[...], factor[...])

    @pl.when(jnp.logical_not(late(inner, outer, level)))
    def _():
        join(own_map, other, through)
        out[...] = own[...] + dot_nn(through[...], factor[...])


def inside_body(level, inner, outer, other_map, through, factor, *refs):
    before_out, behind_out, lift_out = refs[-3:]
    n = factor.shape[1]
    if level == 0:
        row = lax.broadcasted_iota(jnp.int32, (n + PAD, n), 0)
        column = lax.broadcasted_iota(jnp.int32, (n + PAD, n), 1)
        eye = jnp.where(row == column, 1.0, 0.0).astype(F32)
        is_late = late(inner, outer, level)
        before_out[...] = jnp.where(is_late, other_map[...], eye)
        behind_out[...] = jnp.where(is_late, jnp.zeros_like(eye), through[...])
        lift_out[...] = jnp.where(is_late, eye[:n], factor[...])
        return
    before, behind, lift = refs[:3]

    @pl.when(late(inner, outer, level))
    def _():
        join(other_map, before, before_out)
        join(other_map, behind, behind_out)
        lift_out[...] = lift[...]

    @pl.when(jnp.logical_not(late(inner, outer, level)))
    def _():
        before_out[...] = before[...]
        behind_out[...] = behind[...] + dot_nn(through[...], lift[...])
        lift_out[...] = dot_nn(lift[...], factor[...])


def entry_map_body(inner, outer, twin, chip_map, out):
    n = out.shape[1]
    row = lax.broadcasted_iota(jnp.int32, (n + PAD, n), 0)
    column = lax.broadcasted_iota(jnp.int32, (n + PAD, n), 1)
    eye = jnp.where(row == column, 1.0, 0.0).astype(F32)
    out[...] = jnp.where(late(inner, outer, 4), twin[...], eye)

    @pl.when(late(inner, outer, 5))
    def _():
        moved = dot_nn(chip_map[...], out[:n])
        later = out[n:]
        out[:n] = moved[:n]
        out[n:] = moved[n:] + later


def offset_body(outer, first, arrived, near, far, skipped, entry_map, offset_map, entry, offset):
    n = entry_map.shape[1]
    here = jnp.right_shift(outer[0], 2)
    state = dot_nn(far[...], skipped[:n]) + skipped[n:]
    state = jnp.where(here == 3, state, near[...])
    state = jnp.where(here == 1, arrived[...], state)
    state = jnp.where(here == 0, jnp.broadcast_to(first[...], (PAD, n)), state)
    state = dot_nn(state, entry_map[:n]) + entry_map[n:]
    entry[...] = state
    offset[...] = dot_nn(state, offset_map[:n]) + offset_map[n:]


def spread_body(level, inner, outer, own, other, factor, out):
    is_late = late(inner, outer, level)
    early_half = jnp.where(is_late, other[...], own[...])
    late_half = jnp.where(is_late, own[...], other[...])
    out[...] = early_half + dot_nn(late_half, factor[...])


def ends_body(inner, outer, lift, base_powers, *refs):
    count = len(refs) // 2 + 1
    factors, ends = refs[: count - 1], refs[count - 1 :]
    ends[0][...] = dot_nn(lift[...], base_powers[0])
    for k in range(count - 1):
        is_late = late(inner, outer, 4 + k)

        @pl.when(is_late)
        def _():
            ends[k + 1][...] = ends[k][...]

        @pl.when(jnp.logical_not(is_late))
        def _():
            ends[k + 1][...] = dot_nn(ends[k][...], factors[k][...])


def states_body(entry, before, even, odd, obs, gain, pred, filt):
    steps, n = pred.shape
    g = gain[...]
    state = dot_nn(entry[...], before[:n]) + before[n:]
    for t in range(steps):
        c, i = t // 4, t % 4
        pi = even if i < 2 else odd
        k = 2 * c + i % 2
        predicted = (dot_nn(state, pi[k, :n]) + pi[k, n:])[:1]
        pred[t : t + 1, :] = predicted
        filt[t : t + 1, :] = predicted + g * (obs[t : t + 1, :] - predicted)


def local_body(pred, filt, base_powers, base, shifted):
    steps, n = pred.shape
    local = filt[...] - pred[...]
    shifted[steps:, :] = jnp.zeros((steps, n), F32)
    level = 0
    reach = 1
    while reach < steps:
        shifted[:steps, :] = local
        local = local + dot_nn(shifted[reach : reach + steps, :], base_powers[level])
        reach *= 2
        level += 1
    base[...] = pred[...] + local


def gather_body(inner, outer, entry, behind, base_powers, *refs):
    count = len(refs) // 2
    others, ends, out = refs[:count], refs[count : 2 * count], refs[2 * count]
    n = entry.shape[1]
    inside = dot_nn(entry[...], behind[:n]) + behind[n:]
    value = dot_nn(inside, base_powers[0])
    for k in range(count):
        other = others[k][...]
        other = jnp.where(late(inner, outer, 4 + k), jnp.zeros_like(other), other)
        value = value + dot_nn(other, ends[k][...])
    out[...] = value


def backward_body(inner, outer, other, end, back, base_powers, base, out):
    steps, n = base.shape
    value = other[...]
    value = jnp.where(late(inner, outer, 7), jnp.zeros_like(value), value)
    value = back[...] + dot_nn(value, end[...])
    left = steps - 1 - lax.broadcasted_iota(jnp.int32, (steps, n), 0)
    value = jnp.concatenate([value, value], 0)
    for level in range(base_powers.shape[0]):
        value = jnp.where((left >> level) % 2 == 1, dot_nn(value, base_powers[level]), value)
    out[...] = base[...] + value


def shards(jac, obs, gain_filter, gain_smooth, init_mean):
    steps, n, _ = jac.shape
    inner_count, outer_count = lax.axis_size("inner"), lax.axis_size("outer")
    counts = {"inner": inner_count, "outer": outer_count}
    place = [lax.axis_index(axis).astype(jnp.int32)[None] for axis in ("inner", "outer")]
    gain = gain_filter[None, :]
    first = init_mean[None, :]

    def exchange(total, axis, flip, beside):
        other = lax.ppermute(total, axis, [(i, i ^ flip) for i in range(counts[axis])])
        work = beside()
        return lax.optimization_barrier((other, work))

    with jax.named_scope("compose"):
        total, quarter, half, third, loaded = local_map(place, jac, obs, gain)

    def base_work():
        levels = steps.bit_length() - 1
        return kernel_call(
            functools.partial(base_powers_body, steps),
            [(levels, n, n), (n, n)],
            [VMEM],
            (gain_smooth,),
            "base_powers",
            flops=60 * n**3,
            size=20 * n * n,
        )

    aside = []

    def offsets_join(level, own_map, other_map, own, other):
        return kernel_call(
            functools.partial(offsets_join_body, level),
            [(n + PAD, n), (n + PAD, n)],
            [SMEM] * 2 + [VMEM] * 5,
            (*place, own_map, other_map, own, other, high[level]),
            "offsets_join",
            flops=24 * n**3,
            size=28 * n * n,
            grant=6,
        )

    def inside(level, other_map, through):
        aside[:] = kernel_call(
            functools.partial(inside_body, level),
            [(n + PAD, n), (n + PAD, n), (n, n)],
            [SMEM] * 2 + [VMEM] * (3 + len(aside)),
            (*place, other_map, through, high[level], *aside),
            "inside",
            flops=24 * n**3,
            size=36 * n * n,
        )

    def partner(value, axis, flip):
        return lax.ppermute(value, axis, [(i, i ^ flip) for i in range(counts[axis])])

    own_maps, other_maps = [total], []
    with jax.named_scope("join_0"):
        other, (pi_even, even, phi) = exchange(
            total,
            "inner",
            1,
            lambda: maps(True, (quarter, half, third), loaded, obs, gain, gain_smooth),
        )
        other_maps.append(other)
        own_maps.append(total_call(0, place, own_maps[0], other))
    with jax.named_scope("join_1"):

        def work():
            base_powers, top = base_work()
            pi_odd, offset_map = maps(False, (phi, even), loaded, obs, gain, base_powers)
            return base_powers, top, pi_odd, offset_map

        other, (base_powers, top, pi_odd, offsets) = exchange(own_maps[1], "inner", 3, work)
        other_maps.append(other)
        own_maps.append(total_call(1, place, own_maps[1], other))
    with jax.named_scope("join_2"):

        def work():
            return kernel_call(
                high_powers_body,
                [(n, n)] * 6,
                [VMEM],
                (top,),
                "high_powers",
                flops=72 * n**3,
                size=28 * n * n,
            )

        far = partner(offsets, "inner", 1)
        other, high = exchange(own_maps[2], "inner", 4, work)
        high = [top, *high]
        other_maps.append(other)
        own_maps.append(total_call(2, place, own_maps[2], other))
    with jax.named_scope("join_3"):

        def work():
            through, joined = offsets_join(0, own_maps[0], other_maps[0], offsets, far)
            return through, joined, partner(joined, "inner", 3)

        other = partner(own_maps[3], "inner", 12)
        through, offsets, far = work()
        other, through = lax.optimization_barrier((other, through))
        other_maps.append(other)
        own_maps.append(total_call(3, place, own_maps[3], other))
    with jax.named_scope("join_core"):
        twin = partner(own_maps[4], "outer", 1)
        own_maps.append(total_call(4, place, own_maps[4], twin))
    with jax.named_scope("join_z"):
        chip_map = partner(own_maps[5], "outer", 2)
        inside(0, other_maps[0], through)
        through, offsets = offsets_join(1, own_maps[1], other_maps[1], offsets, far)
        far = partner(offsets, "inner", 4)
        chip_map, aside[:] = lax.optimization_barrier((chip_map, aside))
        total = total_call(5, place, own_maps[5], chip_map)

    group = outer_count // 4
    def mirror(source, dest):
        return [
            (source * group + z * 2 + c, dest * group + (group // 2 - 1 - z) * 2 + c)
            for z in range(group // 2)
            for c in range(2)
        ]

    with jax.named_scope("hop_0"):
        y = hop(0, place, first, first, total)
        arrived = lax.ppermute(y, "outer", mirror(0, 1))
        skipped = lax.ppermute(total, "outer", mirror(2, 3))
        inside(1, other_maps[1], through)
        through, offsets = offsets_join(2, own_maps[2], other_maps[2], offsets, far)
        far = partner(offsets, "inner", 12)
        entry_map = kernel_call(
            entry_map_body,
            (n + PAD, n),
            [SMEM] * 2 + [VMEM] * 2,
            (*place, twin, chip_map),
            "entry_map",
            flops=12 * n**3,
            size=12 * n * n,
        )
        arrived, entry_map, aside[:] = lax.optimization_barrier((arrived, entry_map, aside))
    with jax.named_scope("hop_1"):
        y = hop(1, place, first, arrived, total)
        near = lax.ppermute(y, "outer", mirror(1, 2))
        farther = lax.ppermute(y, "outer", mirror(1, 3))
        inside(2, other_maps[2], through)
        through, offsets = offsets_join(3, own_maps[3], other_maps[3], offsets, far)
        near, farther, offsets, aside[:] = lax.optimization_barrier((near, farther, offsets, aside))
    with jax.named_scope("offset"):
        entry, value = kernel_call(
            offset_body,
            [(PAD, n), (PAD, n)],
            [SMEM] + [VMEM] * 7,
            (place[1], first, arrived, near, farther, skipped, entry_map, offsets),
            "offset",
            flops=300 * n * n,
            size=12 * n * n,
        )

    def spread(level, value, other):
        return kernel_call(
            functools.partial(spread_body, level),
            (PAD, n),
            [SMEM] * 2 + [VMEM] * 3,
            (*place, value, other, high[level]),
            "spread",
            flops=96 * n * n,
            size=4 * n * n,
        )

    others = []
    with jax.named_scope("spread_core"):
        others.append(partner(value, "outer", 1))
        value = spread(4, value, others[0])
    with jax.named_scope("spread_z0"):
        other = partner(value, "outer", 2)
        inside(3, other_maps[3], through)
        ends = kernel_call(
            ends_body,
            [(n, n)] * 4,
            [SMEM] * 2 + [VMEM] * 5,
            (*place, aside[2], base_powers, *high[4:7]),
            "ends",
            flops=48 * n**3,
            size=36 * n * n,
        )
        other, ends, aside[:] = lax.optimization_barrier((other, ends, aside))
        others.append(other)
        value = spread(5, value, other)
    with jax.named_scope("spread_z1"):
        other = partner(value, "outer", 4)
        pred, filt = kernel_call(
            states_body,
            [(steps, n), (steps, n)],
            [VMEM] * 6,
            (entry, aside[0], pi_even, pi_odd, obs, gain),
            "states",
            flops=17 * 96 * n * n,
            size=68 * n * n,
        )
        other, pred = lax.optimization_barrier((other, pred))
        others.append(other)
        value = spread(6, value, other)
    with jax.named_scope("spread_z2"):
        other = partner(value, "outer", 14)
        base = kernel_call(
            local_body,
            (steps, n),
            [VMEM] * 3,
            (pred, filt, base_powers),
            "local",
            scratch=[pltpu.VMEM((2 * steps, n), F32)],
            flops=4 * 192 * n * n,
            size=16 * n * n,
        )
        back = kernel_call(
            gather_body,
            (PAD, n),
            [SMEM] * 2 + [VMEM] * 9,
            (*place, entry, aside[1], base_powers, *others, *ends[:3]),
            "gather",
            flops=500 * n * n,
            size=20 * n * n,
        )
        other, base, back = lax.optimization_barrier((other, base, back))
    with jax.named_scope("backward"):
        smoothed = kernel_call(
            backward_body,
            (steps, n),
            [SMEM] * 2 + [VMEM] * 5,
            (*place, other, ends[3], back, base_powers, base),
            "backward",
            flops=600 * n * n,
            size=24 * n * n,
        )
    return (filt, smoothed)


def solution(mesh):
    return jax.shard_map(
        shards,
        mesh=mesh,
        in_specs=(P(("outer", "inner"), None, None), P(("outer", "inner"), None), P(), P(), P()),
        out_specs=(P(("outer", "inner"), None), P(("outer", "inner"), None)),
        check_vma=False,
    )
```

```python
import functools

import jax
import jax.numpy as jnp
from jax import lax
from jax.experimental import pallas as pl
from jax.experimental.pallas import tpu as pltpu
from jax.sharding import PartitionSpec as P

HIGHEST = lax.Precision.HIGHEST
F32 = jnp.float32
VMEM = pl.BlockSpec(memory_space=pltpu.VMEM)
SMEM = pl.BlockSpec(memory_space=pltpu.SMEM)
HBM = pl.BlockSpec(memory_space=pltpu.MemorySpace.HBM)
PAD = 8


def dot_nn(a, b):
    return lax.dot_general(
        a, b, (((1,), (0,)), ((), ())), precision=HIGHEST, preferred_element_type=F32
    )


def dot_nt(a, b):
    return lax.dot_general(
        a, b, (((1,), (1,)), ((), ())), precision=HIGHEST, preferred_element_type=F32
    )


def kernel_call(body, out_shape, in_specs, args, name, scratch=(), flops=0, size=0, grant=4, out_specs=None):
    many = isinstance(out_shape, list)
    shapes = [jax.ShapeDtypeStruct(s, F32) for s in (out_shape if many else [out_shape])]
    out = pl.pallas_call(
        body,
        out_shape=shapes,
        in_specs=in_specs,
        out_specs=out_specs or [VMEM] * len(shapes),
        scratch_shapes=list(scratch),
        cost_estimate=pl.CostEstimate(flops=flops, bytes_accessed=size, transcendentals=0),
        compiler_params=pltpu.CompilerParams(vmem_limit_bytes=grant << 20),
        name=name,
    )(*args)
    return out if many else out[0]


def local_map_body(inner, outer, jac_hbm, obs_hbm, gain_hbm, out, quarter, half, third, buf, obs, gain, chain, sems):
    steps, n, _ = buf.shape
    small = [(obs_hbm, obs, steps), (gain_hbm, gain, steps + 1)]
    for source, dest, k in small:
        pltpu.make_async_copy(source, dest, sems.at[k]).start()
    pairs = steps // 2
    order = [2 * c + i for i in range(2) for c in range(pairs)]
    for t in order:
        pltpu.make_async_copy(jac_hbm.at[t], buf.at[t], sems.at[t]).start()
    for source, dest, k in small:
        pltpu.make_async_copy(source, dest, sems.at[k]).wait()
    g = gain[...]
    retain = 1.0 - g
    for t in order:
        pltpu.make_async_copy(jac_hbm.at[t], buf.at[t], sems.at[t]).wait()
        c = t // 2
        offset = jnp.broadcast_to(g * obs[t : t + 1, :], (PAD, n))
        if t % 2 == 0:
            chain[c, :n] = buf[t].T * retain
            chain[c, n:] = offset
        else:
            moved = dot_nt(chain[c], buf[t]) * retain
            chain[c, :n] = moved[:n]
            chain[c, n:] = moved[n:] + offset
    kept = {(0, pairs): out, (0, pairs // 2): half}
    kept[(0, pairs // 4)] = quarter
    kept[(pairs // 2, 3 * pairs // 4)] = third
    width = 1
    while width < pairs:
        for c in range(0, pairs, 2 * width):
            moved = dot_nn(chain[c], chain[c + width, :n])
            later = chain[c + width, n:]
            span = (c, c + 2 * width)
            dest = kept.get(span, chain.at[c])
            dest[:n] = moved[:n]
            dest[n:] = moved[n:] + later
            if span in kept and 2 * width < pairs:
                chain[c] = dest[...]
        width *= 2


def local_map(place, jac, obs, gain):
    steps, n, _ = jac.shape
    return kernel_call(
        local_map_body,
        [(n + PAD, n)] * 4 + [(steps, n, n)],
        [SMEM, SMEM, HBM, HBM, HBM],
        (*place, jac, obs, gain),
        "local_map",
        scratch=[
            pltpu.VMEM((steps, n), F32),
            pltpu.VMEM((1, n), F32),
            pltpu.VMEM((steps // 2, n + PAD, n), F32),
            pltpu.SemaphoreType.DMA((steps + 2,)),
        ],
        flops=12 * steps * n**3,
        size=4 * steps * n * n,
        grant=47,
    )


def join(earlier, later, out):
    n = out.shape[1]
    moved = dot_nn(earlier[...], later[:n])
    out[:n] = moved[:n]
    out[n:] = moved[n:] + later[n:]


def late(inner, outer, level):
    index = inner if level < 4 else outer
    return jnp.bitwise_and(jnp.right_shift(index[0], level % 4), 1) == 1


def total_body(level, inner, outer, own, other, out):
    n = out.shape[1]
    is_late = late(inner, outer, level)
    earlier = jnp.where(is_late, other[...], own[...])
    later = jnp.where(is_late, own[...], other[...])
    moved = dot_nn(earlier, later[:n])
    out[:n] = moved[:n]
    out[n:] = moved[n:] + later[n:]


def total_call(level, place, a, b):
    n = a.shape[1]
    return kernel_call(
        functools.partial(total_body, level),
        a.shape,
        [SMEM, SMEM, VMEM, VMEM],
        (*place, a, b),
        "total",
        flops=12 * n**3,
        size=12 * n * n,
    )


def hop_body(stage, outer, first, arrived, group_map, out):
    n = out.shape[1]
    state = jnp.broadcast_to(first[...], (PAD, n))
    if stage == 1:
        state = jnp.where(jnp.right_shift(outer[0], 2) == 1, arrived[...], state)
    out[...] = dot_nn(state, group_map[:n]) + group_map[n:]


def hop(stage, place, first, arrived, group_map):
    n = group_map.shape[1]
    return kernel_call(
        functools.partial(hop_body, stage),
        (PAD, n),
        [SMEM] + [VMEM] * 3,
        (place[1], first, arrived, group_map),
        "hop",
        flops=96 * n * n,
        size=4 * n * n,
    )


def maps_body(first, *refs):
    if first:
        quarter, half, third, jac, obs, gain, smooth, pi, pairs, phi = refs[:10]
        later, moving = refs[10:]
    else:
        given, even, jac, obs, gain, base_powers, pi, offset_map = refs[:8]
        later, moving, pairs = refs[8:]
    n = jac.shape[1]
    size = n + PAD
    lanes = 4
    depth = jac.shape[0] // lanes
    if first:
        row = lax.broadcasted_iota(jnp.int32, (size, n), 0)
        column = lax.broadcasted_iota(jnp.int32, (size, n), 1)
        moving[0] = jnp.where(row == column, 1.0, 0.0).astype(F32)
        moving[1] = quarter[...]
        moving[2] = half[...]
        join(half, third, moving.at[3])
        starts = moving
    else:
        starts = given
        factor = base_powers.at[0]
    g = gain[...]
    retain = 1.0 - g

    @pl.loop(0, lanes // 2)
    def _(pair):
        for i in range(2):
            for u in range(2):
                c = 2 * pair + u
                k = 2 * c + i
                t = c * depth + i + (0 if first else 2)
                source = starts if i == 0 else moving
                predicted = dot_nt(source[c], jac[t])
                pi[k] = predicted
                offset = g * obs[pl.ds(t, 1), :]
                if i == 0 or first:
                    dest = moving if i == 0 else phi
                    dest[c, :n] = predicted[:n] * retain
                    dest[c, n:] = predicted[n:] * retain + offset
                change = -(predicted * g)
                dest = pairs if i == 0 else later
                dest[c, :n] = change[:n]
                dest[c, n:] = change[n:] + offset

    if first:
        moving[0, :n] = smooth[...].T

    @pl.loop(0, lanes)
    def _(c):
        pairs[c] = pairs[c] + dot_nn(later[c], factor[...] if not first else moving[0, :n])

    if not first:
        @pl.loop(0, lanes)
        def _(c):
            later[c] = even[c] + dot_nn(pairs[c], base_powers[1])

        halves = [later[c] + dot_nn(later[c + 1], base_powers[2]) for c in (0, 2)]
        offset_map[...] = halves[0] + dot_nn(halves[1], base_powers[3])


def maps(first, starts, jac, obs, gain, factor):
    n = jac.shape[1]
    size = n + PAD
    four = (4, size, n)
    shapes = [(8, size, n)] + ([four, four] if first else [(size, n)])
    scratch = [four, four] + ([] if first else [four])
    return kernel_call(
        functools.partial(maps_body, first),
        shapes,
        [VMEM] * (len(starts) + 4),
        (*starts, jac, obs, gain, factor),
        "maps",
        scratch=[pltpu.VMEM(x, F32) for x in scratch],
        flops=1,
        size=1,
        grant=8,
    )


def base_powers_body(smooth, out):
    out[0] = smooth[...].T

    @pl.loop(1, out.shape[0])
    def _(k):
        out[k] = dot_nn(out[k - 1], out[k - 1])


def high_powers_body(base_powers, out):
    out[0] = base_powers[base_powers.shape[0] - 1]

    @pl.loop(1, out.shape[0])
    def _(k):
        out[k] = dot_nn(out[k - 1], out[k - 1])


def offsets_join_body(level, inner, outer, own_map, other_map, own, other, high, through, out):
    n = out.shape[1]
    is_late = late(inner, outer, level)
    early_map = jnp.where(is_late, other_map[...], own_map[...])
    later = jnp.where(is_late, own[...], other[...])
    moved = dot_nn(early_map, later[:n])
    through[:n] = moved[:n]
    through[n:] = moved[n:] + later[n:]
    out[...] = jnp.where(is_late, other[...], own[...]) + dot_nn(through[...], high[level])


def inside_body(level, inner, outer, other_map, through, high, *refs):
    before_out, behind_out, lift_out = refs[-3:]
    n = high.shape[2]
    is_late = late(inner, outer, level)
    if level == 0:
        row = lax.broadcasted_iota(jnp.int32, (n + PAD, n), 0)
        column = lax.broadcasted_iota(jnp.int32, (n + PAD, n), 1)
        eye = jnp.where(row == column, 1.0, 0.0).astype(F32)
        before_out[...] = jnp.where(is_late, other_map[...], eye)
        behind_out[...] = jnp.where(is_late, jnp.zeros_like(eye), through[...])
        lift_out[...] = jnp.where(is_late, eye[:n], high[level])
        return
    before, behind, lift = refs[:3]
    first = jnp.where(is_late, other_map[...], through[...])
    moved = dot_nn(first, jnp.where(is_late, behind[:n], lift[...]))
    kept = behind[...]
    behind_out[:n] = moved[:n] + jnp.where(is_late, jnp.zeros_like(kept[:n]), kept[:n])
    behind_out[n:] = moved[n:] + kept[n:]
    second = jnp.where(is_late, other_map[:n], lift[...])
    moved = dot_nn(second, jnp.where(is_late, before[:n], high[level]))
    edge = dot_nn(other_map[n:], before[:n]) + before[n:]
    before_out[:n] = jnp.where(is_late, moved, before[:n])
    before_out[n:] = jnp.where(is_late, edge, before[n:])
    lift_out[...] = jnp.where(is_late, lift[...], moved)


def entry_map_body(inner, outer, twin, chip_map, out):
    n = out.shape[1]
    row = lax.broadcasted_iota(jnp.int32, (n + PAD, n), 0)
    column = lax.broadcasted_iota(jnp.int32, (n + PAD, n), 1)
    eye = jnp.where(row == column, 1.0, 0.0).astype(F32)
    out[...] = jnp.where(late(inner, outer, 4), twin[...], eye)

    @pl.when(late(inner, outer, 5))
    def _():
        moved = dot_nn(chip_map[...], out[:n])
        later = out[n:]
        out[:n] = moved[:n]
        out[n:] = moved[n:] + later


def offset_body(outer, first, arrived, near, far, skipped, entry_map, offset_map, entry, offset):
    n = entry_map.shape[1]
    here = jnp.right_shift(outer[0], 2)
    state = dot_nn(far[...], skipped[:n]) + skipped[n:]
    state = jnp.where(here == 3, state, near[...])
    state = jnp.where(here == 1, arrived[...], state)
    state = jnp.where(here == 0, jnp.broadcast_to(first[...], (PAD, n)), state)
    state = dot_nn(state, entry_map[:n]) + entry_map[n:]
    entry[...] = state
    offset[...] = dot_nn(state, offset_map[:n]) + offset_map[n:]


def spread_body(level, inner, outer, own, other, high, out):
    is_late = late(inner, outer, level)
    early_half = jnp.where(is_late, other[...], own[...])
    late_half = jnp.where(is_late, own[...], other[...])
    out[...] = early_half + dot_nn(late_half, high[level])


def ends_body(inner, outer, lift, base_powers, high, *ends):
    ends[0][...] = dot_nn(lift[...], base_powers[0])
    for k in range(len(ends) - 1):
        moved = dot_nn(ends[k][...], high[4 + k])
        ends[k + 1][...] = jnp.where(late(inner, outer, 4 + k), ends[k][...], moved)


def states_body(entry, before, even, odd, obs, gain, pred, filt):
    steps, n = pred.shape
    g = gain[...]
    state = dot_nn(entry[...], before[:n]) + before[n:]

    @pl.loop(0, 4)
    def _(c):
        for i in range(4):
            t = 4 * c + i
            pi = even if i < 2 else odd
            k = 2 * c + i % 2
            predicted = (dot_nn(state, pi[k, :n]) + pi[k, n:])[:1]
            pred[pl.ds(t, 1), :] = predicted
            filt[pl.ds(t, 1), :] = predicted + g * (obs[pl.ds(t, 1), :] - predicted)


def local_body(pred, filt, base_powers, base, shifted):
    steps, n = pred.shape
    local = filt[...] - pred[...]
    shifted[steps:, :] = jnp.zeros((steps, n), F32)
    level = 0
    reach = 1
    while reach < steps:
        shifted[:steps, :] = local
        local = local + dot_nn(shifted[reach : reach + steps, :], base_powers[level])
        reach *= 2
        level += 1
    base[...] = pred[...] + local


def gather_body(inner, outer, entry, behind, base_powers, *refs):
    count = len(refs) // 2
    others, ends, out = refs[:count], refs[count : 2 * count], refs[2 * count]
    n = entry.shape[1]
    inside = dot_nn(entry[...], behind[:n]) + behind[n:]
    value = dot_nn(inside, base_powers[0])
    for k in range(count):
        other = others[k][...]
        other = jnp.where(late(inner, outer, 4 + k), jnp.zeros_like(other), other)
        value = value + dot_nn(other, ends[k][...])
    out[...] = value


def backward_body(inner, outer, other, end, back, base_powers, base, out):
    steps, n = base.shape
    value = other[...]
    value = jnp.where(late(inner, outer, 7), jnp.zeros_like(value), value)
    value = back[...] + dot_nn(value, end[...])
    left = steps - 1 - lax.broadcasted_iota(jnp.int32, (steps, n), 0)
    value = jnp.concatenate([value, value], 0)
    for level in range(base_powers.shape[0] - 1):
        value = jnp.where((left >> level) % 2 == 1, dot_nn(value, base_powers[level]), value)
    out[...] = base[...] + value


def shards(jac, obs, gain_filter, gain_smooth, init_mean):
    steps, n, _ = jac.shape
    inner_count, outer_count = lax.axis_size("inner"), lax.axis_size("outer")
    counts = {"inner": inner_count, "outer": outer_count}
    place = [lax.axis_index(axis).astype(jnp.int32)[None] for axis in ("inner", "outer")]
    gain = gain_filter[None, :]
    first = init_mean[None, :]

    def exchange(total, axis, flip, beside):
        other = lax.ppermute(total, axis, [(i, i ^ flip) for i in range(counts[axis])])
        work = beside()
        return lax.optimization_barrier((other, work))

    with jax.named_scope("compose"):
        total, quarter, half, third, loaded = local_map(place, jac, obs, gain)

    def base_work():
        levels = steps.bit_length()
        return kernel_call(
            base_powers_body,
            (levels, n, n),
            [VMEM],
            (gain_smooth,),
            "base_powers",
            flops=1,
            size=1,
        )

    aside = []

    def offsets_join(level, own_map, other_map, own, other):
        return kernel_call(
            functools.partial(offsets_join_body, level),
            [(n + PAD, n), (n + PAD, n)],
            [SMEM] * 2 + [VMEM] * 5,
            (*place, own_map, other_map, own, other, high),
            "offsets_join",
            flops=1,
            size=1,
            grant=6,
        )

    def inside(level, other_map, through):
        aside[:] = kernel_call(
            functools.partial(inside_body, level),
            [(n + PAD, n), (n + PAD, n), (n, n)],
            [SMEM] * 2 + [VMEM] * (3 + len(aside)),
            (*place, other_map, through, high, *aside),
            "inside",
            flops=1,
            size=1,
        )

    def partner(value, axis, flip):
        return lax.ppermute(value, axis, [(i, i ^ flip) for i in range(counts[axis])])

    own_maps, other_maps = [total], []
    with jax.named_scope("join_0"):
        other, (pi_even, even, phi) = exchange(
            total,
            "inner",
            1,
            lambda: maps(True, (quarter, half, third), loaded, obs, gain, gain_smooth),
        )
        other_maps.append(other)
        own_maps.append(total_call(0, place, own_maps[0], other))
    with jax.named_scope("join_1"):

        def work():
            base_powers = base_work()
            pi_odd, offset_map = maps(False, (phi, even), loaded, obs, gain, base_powers)
            return base_powers, pi_odd, offset_map

        other, (base_powers, pi_odd, offsets) = exchange(own_maps[1], "inner", 3, work)
        other_maps.append(other)
        own_maps.append(total_call(1, place, own_maps[1], other))
    with jax.named_scope("join_2"):

        def work():
            return kernel_call(
                high_powers_body,
                (7, n, n),
                [VMEM],
                (base_powers,),
                "high_powers",
                flops=1,
                size=1,
            )

        far = partner(offsets, "inner", 1)
        other, high = exchange(own_maps[2], "inner", 4, work)
        other_maps.append(other)
        own_maps.append(total_call(2, place, own_maps[2], other))
    with jax.named_scope("join_3"):

        def work():
            through, joined = offsets_join(0, own_maps[0], other_maps[0], offsets, far)
            return through, joined, partner(joined, "inner", 3)

        other = partner(own_maps[3], "inner", 12)
        through, offsets, far = work()
        other, through = lax.optimization_barrier((other, through))
        other_maps.append(other)
        own_maps.append(total_call(3, place, own_maps[3], other))
    with jax.named_scope("join_core"):
        twin = partner(own_maps[4], "outer", 1)
        own_maps.append(total_call(4, place, own_maps[4], twin))
    with jax.named_scope("join_z"):
        chip_map = partner(own_maps[5], "outer", 2)
        inside(0, other_maps[0], through)
        far, _ = lax.optimization_barrier((far, own_maps[5]))
        through, offsets = offsets_join(1, own_maps[1], other_maps[1], offsets, far)
        far = partner(offsets, "inner", 4)
        inside(1, other_maps[1], through)
        chip_map, aside[:] = lax.optimization_barrier((chip_map, aside))
        total = total_call(5, place, own_maps[5], chip_map)

    group = outer_count // 4
    def mirror(source, dest):
        return [
            (source * group + z * 2 + c, dest * group + (group // 2 - 1 - z) * 2 + c)
            for z in range(group // 2)
            for c in range(2)
        ]

    with jax.named_scope("hop_0"):
        y = hop(0, place, first, first, total)
        arrived = lax.ppermute(y, "outer", mirror(0, 1))
        far, _ = lax.optimization_barrier((far, y))
        through, offsets = offsets_join(2, own_maps[2], other_maps[2], offsets, far)
        far = partner(offsets, "inner", 12)
        arrived, through = lax.optimization_barrier((arrived, through))
    with jax.named_scope("hop_1"):
        y = hop(1, place, first, arrived, total)
        near = lax.ppermute(y, "outer", mirror(1, 2))
        farther = lax.ppermute(y, "outer", mirror(1, 3))
        sent_map, _ = lax.optimization_barrier((total, y))
        skipped = lax.ppermute(sent_map, "outer", mirror(2, 3))
        entry_map = kernel_call(
            entry_map_body,
            (n + PAD, n),
            [SMEM] * 2 + [VMEM] * 2,
            (*place, twin, chip_map),
            "entry_map",
            flops=1,
            size=1,
        )
        inside(2, other_maps[2], through)
        far, _ = lax.optimization_barrier((far, y))
        through, offsets = offsets_join(3, own_maps[3], other_maps[3], offsets, far)
        near, farther, offsets, entry_map, aside[:] = lax.optimization_barrier(
            (near, farther, offsets, entry_map, aside)
        )
    with jax.named_scope("offset"):
        entry, value = kernel_call(
            offset_body,
            [(PAD, n), (PAD, n)],
            [SMEM] + [VMEM] * 7,
            (place[1], first, arrived, near, farther, skipped, entry_map, offsets),
            "offset",
            flops=300 * n * n,
            size=12 * n * n,
        )

    def spread(level, value, other):
        return kernel_call(
            functools.partial(spread_body, level),
            (PAD, n),
            [SMEM] * 2 + [VMEM] * 3,
            (*place, value, other, high),
            "spread",
            flops=96 * n * n,
            size=4 * n * n,
        )

    others = []
    with jax.named_scope("spread_core"):
        others.append(partner(value, "outer", 1))
        value = spread(4, value, others[0])
    with jax.named_scope("spread_z0"):
        other = partner(value, "outer", 2)
        inside(3, other_maps[3], through)
        ends = kernel_call(
            ends_body,
            [(n, n)] * 4,
            [SMEM] * 2 + [VMEM] * 3,
            (*place, aside[2], base_powers, high),
            "ends",
            flops=1,
            size=1,
        )
        other, ends, aside[:] = lax.optimization_barrier((other, ends, aside))
        others.append(other)
        value = spread(5, value, other)
    with jax.named_scope("spread_z1"):
        other = partner(value, "outer", 4)
        pred, filt = kernel_call(
            states_body,
            [(steps, n), (steps, n)],
            [VMEM] * 6,
            (entry, aside[0], pi_even, pi_odd, obs, gain),
            "states",
            flops=1,
            size=1,
        )
        other, pred = lax.optimization_barrier((other, pred))
        others.append(other)
        value = spread(6, value, other)
    with jax.named_scope("spread_z2"):
        other = partner(value, "outer", 14)
        base = kernel_call(
            local_body,
            (steps, n),
            [VMEM] * 3,
            (pred, filt, base_powers),
            "local",
            scratch=[pltpu.VMEM((2 * steps, n), F32)],
            flops=1,
            size=1,
        )
        back = kernel_call(
            gather_body,
            (PAD, n),
            [SMEM] * 2 + [VMEM] * 9,
            (*place, entry, aside[1], base_powers, *others, *ends[:3]),
            "gather",
            flops=1,
            size=1,
        )
        other, base, back = lax.optimization_barrier((other, base, back))
    with jax.named_scope("backward"):
        smoothed = kernel_call(
            backward_body,
            (steps, n),
            [SMEM] * 2 + [VMEM] * 5,
            (*place, other, ends[3], back, base_powers, base),
            "backward",
            flops=600 * n * n,
            size=24 * n * n,
        )
    return (filt, smoothed)


def solution(mesh):
    return jax.shard_map(
        shards,
        mesh=mesh,
        in_specs=(P(("outer", "inner"), None, None), P(("outer", "inner"), None), P(), P(), P()),
        out_specs=(P(("outer", "inner"), None), P(("outer", "inner"), None)),
        check_vma=False,
    )
```

```python
import functools

import jax
import jax.numpy as jnp
from jax import lax
from jax.experimental import pallas as pl
from jax.experimental.pallas import tpu as pltpu
from jax.sharding import PartitionSpec as P

HIGHEST = lax.Precision.HIGHEST
F32 = jnp.float32
VMEM = pl.BlockSpec(memory_space=pltpu.VMEM)
SMEM = pl.BlockSpec(memory_space=pltpu.SMEM)
HBM = pl.BlockSpec(memory_space=pltpu.MemorySpace.HBM)
PAD = 8


def dot_nn(a, b):
    return lax.dot_general(
        a, b, (((1,), (0,)), ((), ())), precision=HIGHEST, preferred_element_type=F32
    )


def dot_nt(a, b):
    return lax.dot_general(
        a, b, (((1,), (1,)), ((), ())), precision=HIGHEST, preferred_element_type=F32
    )


def kernel_call(body, out_shape, in_specs, args, name, scratch=(), flops=0, size=0, grant=4, out_specs=None):
    many = isinstance(out_shape, list)
    shapes = [jax.ShapeDtypeStruct(s, F32) for s in (out_shape if many else [out_shape])]
    out = pl.pallas_call(
        body,
        out_shape=shapes,
        in_specs=in_specs,
        out_specs=out_specs or [VMEM] * len(shapes),
        scratch_shapes=list(scratch),
        cost_estimate=pl.CostEstimate(flops=flops, bytes_accessed=size, transcendentals=0),
        compiler_params=pltpu.CompilerParams(vmem_limit_bytes=grant << 20),
        name=name,
    )(*args)
    return out if many else out[0]


def local_map_body(inner, outer, jac_hbm, obs_hbm, gain_hbm, out, quarter, half, third, buf, obs, gain, chain, sems):
    steps, n, _ = buf.shape
    small = [(obs_hbm, obs, steps), (gain_hbm, gain, steps + 1)]
    for source, dest, k in small:
        pltpu.make_async_copy(source, dest, sems.at[k]).start()
    pairs = steps // 2
    order = [2 * c + i for i in range(2) for c in range(pairs)]
    for t in order:
        pltpu.make_async_copy(jac_hbm.at[t], buf.at[t], sems.at[t]).start()
    for source, dest, k in small:
        pltpu.make_async_copy(source, dest, sems.at[k]).wait()
    g = gain[...]
    retain = 1.0 - g
    for t in order:
        pltpu.make_async_copy(jac_hbm.at[t], buf.at[t], sems.at[t]).wait()
        c = t // 2
        offset = jnp.broadcast_to(g * obs[t : t + 1, :], (PAD, n))
        if t % 2 == 0:
            chain[c, :n] = buf[t].T * retain
            chain[c, n:] = offset
        else:
            moved = dot_nt(chain[c], buf[t]) * retain
            chain[c, :n] = moved[:n]
            chain[c, n:] = moved[n:] + offset
    kept = {(0, pairs): out, (0, pairs // 2): half}
    kept[(0, pairs // 4)] = quarter
    kept[(pairs // 2, 3 * pairs // 4)] = third
    width = 1
    while width < pairs:
        for c in range(0, pairs, 2 * width):
            moved = dot_nn(chain[c], chain[c + width, :n])
            later = chain[c + width, n:]
            span = (c, c + 2 * width)
            dest = kept.get(span, chain.at[c])
            dest[:n] = moved[:n]
            dest[n:] = moved[n:] + later
            if span in kept and 2 * width < pairs:
                chain[c] = dest[...]
        width *= 2


def local_map(place, jac, obs, gain):
    steps, n, _ = jac.shape
    return kernel_call(
        local_map_body,
        [(n + PAD, n)] * 4 + [(steps, n, n)],
        [SMEM, SMEM, HBM, HBM, HBM],
        (*place, jac, obs, gain),
        "local_map",
        scratch=[
            pltpu.VMEM((steps, n), F32),
            pltpu.VMEM((1, n), F32),
            pltpu.VMEM((steps // 2, n + PAD, n), F32),
            pltpu.SemaphoreType.DMA((steps + 2,)),
        ],
        flops=12 * steps * n**3,
        size=4 * steps * n * n,
        grant=47,
    )


def join(earlier, later, out):
    n = out.shape[1]
    moved = dot_nn(earlier[...], later[:n])
    out[:n] = moved[:n]
    out[n:] = moved[n:] + later[n:]


def late(inner, outer, level):
    index = inner if level < 4 else outer
    return jnp.bitwise_and(jnp.right_shift(index[0], level % 4), 1) == 1


def total_body(level, inner, outer, own, other, out):
    n = out.shape[1]
    is_late = late(inner, outer, level)
    earlier = jnp.where(is_late, other[...], own[...])
    later = jnp.where(is_late, own[...], other[...])
    moved = dot_nn(earlier, later[:n])
    out[:n] = moved[:n]
    out[n:] = moved[n:] + later[n:]


def total_call(level, place, a, b):
    n = a.shape[1]
    return kernel_call(
        functools.partial(total_body, level),
        a.shape,
        [SMEM, SMEM, VMEM, VMEM],
        (*place, a, b),
        "total",
        flops=12 * n**3,
        size=12 * n * n,
    )


def hop_body(stage, outer, first, arrived, group_map, out):
    n = out.shape[1]
    state = jnp.broadcast_to(first[...], (PAD, n))
    if stage == 1:
        state = jnp.where(jnp.right_shift(outer[0], 2) == 1, arrived[...], state)
    out[...] = dot_nn(state, group_map[:n]) + group_map[n:]


def hop(stage, place, first, arrived, group_map):
    n = group_map.shape[1]
    return kernel_call(
        functools.partial(hop_body, stage),
        (PAD, n),
        [SMEM] + [VMEM] * 3,
        (place[1], first, arrived, group_map),
        "hop",
        flops=96 * n * n,
        size=4 * n * n,
    )


def maps_body(first, *refs):
    if first:
        quarter, half, third, jac, obs, gain, smooth, pi, pairs, phi = refs[:10]
        later, moving = refs[10:]
    else:
        given, jac, obs, gain, base_powers, pi, pairs = refs[:7]
        later, moving = refs[7:]
    n = jac.shape[1]
    size = n + PAD
    lanes = 4
    depth = jac.shape[0] // lanes
    if first:
        row = lax.broadcasted_iota(jnp.int32, (size, n), 0)
        column = lax.broadcasted_iota(jnp.int32, (size, n), 1)
        moving[0] = jnp.where(row == column, 1.0, 0.0).astype(F32)
        moving[1] = quarter[...]
        moving[2] = half[...]
        join(half, third, moving.at[3])
        starts = moving
    else:
        starts = given
        factor = base_powers.at[0]
    g = gain[...]
    retain = 1.0 - g

    def two(pair):
        for i in range(2):
            for u in range(2):
                c = 2 * pair + u
                k = 2 * c + i
                t = c * depth + i + (0 if first else 2)
                source = starts if i == 0 else moving
                predicted = dot_nt(source[c], jac[t])
                pi[k] = predicted
                offset = g * obs[pl.ds(t, 1), :]
                if i == 0 or first:
                    dest = moving if i == 0 else phi
                    dest[c, :n] = predicted[:n] * retain
                    dest[c, n:] = predicted[n:] * retain + offset
                change = -(predicted * g)
                dest = pairs if i == 0 else later
                dest[c, :n] = change[:n]
                dest[c, n:] = change[n:] + offset

    if first:
        pl.loop(0, lanes // 2)(two)
    else:
        two(0)
        two(1)
    if first:
        moving[0, :n] = smooth[...].T

    @pl.loop(0, lanes)
    def _(c):
        pairs[c] = pairs[c] + dot_nn(later[c], factor[...] if not first else moving[0, :n])


def offset_map_body(even, odd, base_powers, out, quads):
    @pl.loop(0, quads.shape[0])
    def _(c):
        quads[c] = even[c] + dot_nn(odd[c], base_powers[1])

    halves = [quads[c] + dot_nn(quads[c + 1], base_powers[2]) for c in (0, 2)]
    out[...] = halves[0] + dot_nn(halves[1], base_powers[3])


def maps(first, starts, jac, obs, gain, factor):
    n = jac.shape[1]
    size = n + PAD
    four = (4, size, n)
    shapes = [(8, size, n), four] + ([four] if first else [])
    scratch = [four, four]
    return kernel_call(
        functools.partial(maps_body, first),
        shapes,
        [VMEM] * (len(starts) + 4),
        (*starts, jac, obs, gain, factor),
        "maps",
        scratch=[pltpu.VMEM(x, F32) for x in scratch],
        flops=12 * 8 * n**3,
        size=8 * 12 * n * n,
        grant=8,
    )


def base_powers_body(smooth, out):
    out[0] = smooth[...].T

    @pl.loop(1, out.shape[0])
    def _(k):
        out[k] = dot_nn(out[k - 1], out[k - 1])


def high_powers_body(base_powers, out):
    out[0] = base_powers[base_powers.shape[0] - 1]

    @pl.loop(1, out.shape[0])
    def _(k):
        out[k] = dot_nn(out[k - 1], out[k - 1])


def offsets_join_body(level, inner, outer, own_map, other_map, own, other, high, through, out):
    n = out.shape[1]
    is_late = late(inner, outer, level)
    early_map = jnp.where(is_late, other_map[...], own_map[...])
    later = jnp.where(is_late, own[...], other[...])
    moved = dot_nn(early_map, later[:n])
    through[:n] = moved[:n]
    through[n:] = moved[n:] + later[n:]
    out[...] = jnp.where(is_late, other[...], own[...]) + dot_nn(through[...], high[level])


def inside_body(level, inner, outer, other_map, through, high, *refs):
    before_out, behind_out, lift_out = refs[-3:]
    n = high.shape[2]
    is_late = late(inner, outer, level)
    if level == 0:
        row = lax.broadcasted_iota(jnp.int32, (n + PAD, n), 0)
        column = lax.broadcasted_iota(jnp.int32, (n + PAD, n), 1)
        eye = jnp.where(row == column, 1.0, 0.0).astype(F32)
        before_out[...] = jnp.where(is_late, other_map[...], eye)
        behind_out[...] = jnp.where(is_late, jnp.zeros_like(eye), through[...])
        lift_out[...] = jnp.where(is_late, eye[:n], high[level])
        return
    before, behind, lift = refs[:3]
    first = jnp.where(is_late, other_map[...], through[...])
    moved = dot_nn(first, jnp.where(is_late, behind[:n], lift[...]))
    kept = behind[...]
    behind_out[:n] = moved[:n] + jnp.where(is_late, jnp.zeros_like(kept[:n]), kept[:n])
    behind_out[n:] = moved[n:] + kept[n:]
    second = jnp.where(is_late, other_map[:n], lift[...])
    moved = dot_nn(second, jnp.where(is_late, before[:n], high[level]))
    edge = dot_nn(other_map[n:], before[:n]) + before[n:]
    before_out[:n] = jnp.where(is_late, moved, before[:n])
    before_out[n:] = jnp.where(is_late, edge, before[n:])
    lift_out[...] = jnp.where(is_late, lift[...], moved)


def entry_map_body(inner, outer, row_map, twin, chip_map, out):
    n = out.shape[1]
    row = lax.broadcasted_iota(jnp.int32, (n + PAD, n), 0)
    column = lax.broadcasted_iota(jnp.int32, (n + PAD, n), 1)
    eye = jnp.where(row == column, 1.0, 0.0).astype(F32)
    out[...] = jnp.where(late(inner, outer, 3), row_map[...], eye)
    for level, earlier in ((4, twin), (5, chip_map)):
        is_late = late(inner, outer, level)
        moved = dot_nn(earlier[...], out[:n])
        later = out[...]
        out[:n] = jnp.where(is_late, moved[:n], later[:n])
        out[n:] = jnp.where(is_late, moved[n:] + later[n:], later[n:])


def offset_body(outer, first, arrived, near, far, skipped, entry_map, offset_map, entry, offset):
    n = entry_map.shape[1]
    here = jnp.right_shift(outer[0], 2)
    state = dot_nn(far[...], skipped[:n]) + skipped[n:]
    state = jnp.where(here == 3, state, near[...])
    state = jnp.where(here == 1, arrived[...], state)
    state = jnp.where(here == 0, jnp.broadcast_to(first[...], (PAD, n)), state)
    state = dot_nn(state, entry_map[:n]) + entry_map[n:]
    entry[...] = state
    offset[...] = dot_nn(state, offset_map[:n]) + offset_map[n:]


def spread_body(level, inner, outer, own, other, high, out):
    is_late = late(inner, outer, level)
    early_half = jnp.where(is_late, other[...], own[...])
    late_half = jnp.where(is_late, own[...], other[...])
    out[...] = early_half + dot_nn(late_half, high[level])


def ends_body(inner, outer, lift, base_powers, high, *ends):
    ends[0][...] = dot_nn(lift[...], base_powers[0])
    for k in range(len(ends) - 1):
        moved = dot_nn(ends[k][...], high[3 + k])
        ends[k + 1][...] = jnp.where(late(inner, outer, 3 + k), ends[k][...], moved)


def states_body(entry, before, even, odd, obs, gain, pred, filt):
    steps, n = pred.shape
    g = gain[...]
    state = dot_nn(entry[...], before[:n]) + before[n:]

    @pl.loop(0, 4)
    def _(c):
        for i in range(4):
            t = 4 * c + i
            pi = even if i < 2 else odd
            k = 2 * c + i % 2
            predicted = (dot_nn(state, pi[k, :n]) + pi[k, n:])[:1]
            pred[pl.ds(t, 1), :] = predicted
            filt[pl.ds(t, 1), :] = predicted + g * (obs[pl.ds(t, 1), :] - predicted)


def local_body(pred, filt, base_powers, base, shifted):
    steps, n = pred.shape
    local = filt[...] - pred[...]
    shifted[steps:, :] = jnp.zeros((steps, n), F32)
    level = 0
    reach = 1
    while reach < steps:
        shifted[:steps, :] = local
        local = local + dot_nn(shifted[reach : reach + steps, :], base_powers[level])
        reach *= 2
        level += 1
    base[...] = pred[...] + local


def gather_body(inner, outer, entry, behind, base_powers, *refs):
    count = len(refs) // 2
    others, ends, out = refs[:count], refs[count : 2 * count], refs[2 * count]
    n = entry.shape[1]
    inside = dot_nn(entry[...], behind[:n]) + behind[n:]
    value = dot_nn(inside, base_powers[0])
    for k in range(count):
        other = others[k][...]
        other = jnp.where(late(inner, outer, 3 + k), jnp.zeros_like(other), other)
        value = value + dot_nn(other, ends[k][...])
    out[...] = value


def backward_body(inner, outer, other, end, back, base_powers, base, out):
    steps, n = base.shape
    value = other[...]
    value = jnp.where(late(inner, outer, 7), jnp.zeros_like(value), value)
    value = back[...] + dot_nn(value, end[...])
    left = steps - 1 - lax.broadcasted_iota(jnp.int32, (steps, n), 0)
    value = jnp.concatenate([value, value], 0)
    for level in range(base_powers.shape[0] - 1):
        value = jnp.where((left >> level) % 2 == 1, dot_nn(value, base_powers[level]), value)
    out[...] = base[...] + value


def shards(jac, obs, gain_filter, gain_smooth, init_mean):
    steps, n, _ = jac.shape
    inner_count, outer_count = lax.axis_size("inner"), lax.axis_size("outer")
    counts = {"inner": inner_count, "outer": outer_count}
    place = [lax.axis_index(axis).astype(jnp.int32)[None] for axis in ("inner", "outer")]
    gain = gain_filter[None, :]
    first = init_mean[None, :]

    def exchange(total, axis, flip, beside):
        other = lax.ppermute(total, axis, [(i, i ^ flip) for i in range(counts[axis])])
        work = beside()
        return lax.optimization_barrier((other, work))

    with jax.named_scope("compose"):
        total, quarter, half, third, loaded = local_map(place, jac, obs, gain)

    def base_work():
        levels = steps.bit_length()
        return kernel_call(
            base_powers_body,
            (levels, n, n),
            [VMEM],
            (gain_smooth,),
            "base_powers",
            flops=60 * n**3,
            size=24 * n * n,
        )

    aside = []

    def offsets_join(level, own_map, other_map, own, other):
        return kernel_call(
            functools.partial(offsets_join_body, level),
            [(n + PAD, n), (n + PAD, n)],
            [SMEM] * 2 + [VMEM] * 5,
            (*place, own_map, other_map, own, other, high),
            "offsets_join",
            flops=1,
            size=1,
            grant=6,
        )

    def inside(level, other_map, through):
        aside[:] = kernel_call(
            functools.partial(inside_body, level),
            [(n + PAD, n), (n + PAD, n), (n, n)],
            [SMEM] * 2 + [VMEM] * (3 + len(aside)),
            (*place, other_map, through, high, *aside),
            "inside",
            flops=1,
            size=1,
        )

    def partner(value, axis, flip):
        return lax.ppermute(value, axis, [(i, i ^ flip) for i in range(counts[axis])])

    own_maps, other_maps = [total], []
    with jax.named_scope("join_0"):
        other, (pi_even, even, phi) = exchange(
            total,
            "inner",
            1,
            lambda: maps(True, (quarter, half, third), loaded, obs, gain, gain_smooth),
        )
        other_maps.append(other)
        own_maps.append(total_call(0, place, own_maps[0], other))
    with jax.named_scope("join_1"):

        def work():
            base_powers = base_work()
            pi_odd, odd = maps(False, (phi,), loaded, obs, gain, base_powers)
            return base_powers, pi_odd, odd

        other, (base_powers, pi_odd, odd) = exchange(own_maps[1], "inner", 3, work)
        other_maps.append(other)
        own_maps.append(total_call(1, place, own_maps[1], other))
    with jax.named_scope("join_2"):

        def work():
            return kernel_call(
                high_powers_body,
                (7, n, n),
                [VMEM],
                (base_powers,),
                "high_powers",
                flops=72 * n**3,
                size=28 * n * n,
            )

        other = partner(own_maps[2], "inner", 4)
        offsets = kernel_call(
            offset_map_body,
            (n + PAD, n),
            [VMEM] * 3,
            (even, odd, base_powers),
            "offset_map",
            scratch=[pltpu.VMEM((4, n + PAD, n), F32)],
            flops=84 * n**3,
            size=36 * n * n,
        )
        far = partner(offsets, "inner", 1)
        other, high, offsets_done = lax.optimization_barrier((other, work(), offsets))
        other_maps.append(other)
        own_maps.append(total_call(2, place, own_maps[2], other))
    with jax.named_scope("join_3"):

        def work():
            through, joined = offsets_join(0, own_maps[0], other_maps[0], offsets, far)
            return through, joined, partner(joined, "inner", 3)

        other = partner(own_maps[3], "inner", 12)
        through, offsets, far = work()
        other, through = lax.optimization_barrier((other, through))
        other_maps.append(other)
        own_maps.append(total_call(3, place, own_maps[3], other))
    with jax.named_scope("join_core"):
        twin = partner(own_maps[4], "outer", 1)
        own_maps.append(total_call(4, place, own_maps[4], twin))
    with jax.named_scope("join_z"):
        chip_map = partner(own_maps[5], "outer", 2)
        inside(0, other_maps[0], through)
        chip_map, aside[:] = lax.optimization_barrier((chip_map, aside))
        total = total_call(5, place, own_maps[5], chip_map)

    group = outer_count // 4
    def mirror(source, dest):
        return [
            (source * group + z * 2 + c, dest * group + (group // 2 - 1 - z) * 2 + c)
            for z in range(group // 2)
            for c in range(2)
        ]

    with jax.named_scope("hop_0"):
        y = hop(0, place, first, first, total)
        arrived = lax.ppermute(y, "outer", mirror(0, 1))
        far, _ = lax.optimization_barrier((far, y))
        through, offsets = offsets_join(1, own_maps[1], other_maps[1], offsets, far)
        far = partner(offsets, "inner", 4)
        arrived, through = lax.optimization_barrier((arrived, through))
    with jax.named_scope("hop_1"):
        y = hop(1, place, first, arrived, total)
        near = lax.ppermute(y, "outer", mirror(1, 2))
        farther = lax.ppermute(y, "outer", mirror(1, 3))
        sent_map, _ = lax.optimization_barrier((total, y))
        skipped = lax.ppermute(sent_map, "outer", mirror(2, 3))
        entry_map = kernel_call(
            entry_map_body,
            (n + PAD, n),
            [SMEM] * 2 + [VMEM] * 3,
            (*place, other_maps[3], twin, chip_map),
            "entry_map",
            flops=1,
            size=1,
        )
        inside(1, other_maps[1], through)
        through, offsets = offsets_join(2, own_maps[2], other_maps[2], offsets, far)
        near, farther, offsets, entry_map, aside[:] = lax.optimization_barrier(
            (near, farther, offsets, entry_map, aside)
        )
    with jax.named_scope("offset"):
        entry, value = kernel_call(
            offset_body,
            [(PAD, n), (PAD, n)],
            [SMEM] + [VMEM] * 7,
            (place[1], first, arrived, near, farther, skipped, entry_map, offsets),
            "offset",
            flops=300 * n * n,
            size=12 * n * n,
        )

    def spread(level, value, other):
        return kernel_call(
            functools.partial(spread_body, level),
            (PAD, n),
            [SMEM] * 2 + [VMEM] * 3,
            (*place, value, other, high),
            "spread",
            flops=96 * n * n,
            size=4 * n * n,
        )

    others = []
    with jax.named_scope("spread_x"):
        other = partner(value, "inner", 12)
        inside(2, other_maps[2], through)
        other, aside[:] = lax.optimization_barrier((other, aside))
        others.append(other)
        value = spread(3, value, other)
    with jax.named_scope("spread_core"):
        others.append(partner(value, "outer", 1))
        value = spread(4, value, others[1])
    with jax.named_scope("spread_z0"):
        other = partner(value, "outer", 2)
        ends = kernel_call(
            ends_body,
            [(n, n)] * 5,
            [SMEM] * 2 + [VMEM] * 3,
            (*place, aside[2], base_powers, high),
            "ends",
            flops=60 * n**3,
            size=36 * n * n,
        )
        other, ends = lax.optimization_barrier((other, ends))
        others.append(other)
        value = spread(5, value, other)
    with jax.named_scope("spread_z1"):
        other = partner(value, "outer", 4)
        pred, filt = kernel_call(
            states_body,
            [(steps, n), (steps, n)],
            [VMEM] * 6,
            (entry, aside[0], pi_even, pi_odd, obs, gain),
            "states",
            flops=17 * 96 * n * n,
            size=68 * n * n,
        )
        other, pred = lax.optimization_barrier((other, pred))
        others.append(other)
        value = spread(6, value, other)
    with jax.named_scope("spread_z2"):
        other = partner(value, "outer", 14)
        base = kernel_call(
            local_body,
            (steps, n),
            [VMEM] * 3,
            (pred, filt, base_powers),
            "local",
            scratch=[pltpu.VMEM((2 * steps, n), F32)],
            flops=8 * 96 * n * n,
            size=16 * n * n,
        )
        back = kernel_call(
            gather_body,
            (PAD, n),
            [SMEM] * 2 + [VMEM] * 11,
            (*place, entry, aside[1], base_powers, *others, *ends[:4]),
            "gather",
            flops=600 * n * n,
            size=20 * n * n,
        )
        other, base, back = lax.optimization_barrier((other, base, back))
    with jax.named_scope("backward"):
        smoothed = kernel_call(
            backward_body,
            (steps, n),
            [SMEM] * 2 + [VMEM] * 5,
            (*place, other, ends[4], back, base_powers, base),
            "backward",
            flops=600 * n * n,
            size=24 * n * n,
        )
    return (filt, smoothed)


def solution(mesh):
    return jax.shard_map(
        shards,
        mesh=mesh,
        in_specs=(P(("outer", "inner"), None, None), P(("outer", "inner"), None), P(), P(), P()),
        out_specs=(P(("outer", "inner"), None), P(("outer", "inner"), None)),
        check_vma=False,
    )
```

```python
import functools

import jax
import jax.numpy as jnp
from jax import lax
from jax.experimental import pallas as pl
from jax.experimental.pallas import tpu as pltpu
from jax.sharding import PartitionSpec as P

HIGHEST = lax.Precision.HIGHEST
F32 = jnp.float32
VMEM = pl.BlockSpec(memory_space=pltpu.VMEM)
SMEM = pl.BlockSpec(memory_space=pltpu.SMEM)
HBM = pl.BlockSpec(memory_space=pltpu.MemorySpace.HBM)
PAD = 8


def dot_nn(a, b):
    return lax.dot_general(
        a, b, (((1,), (0,)), ((), ())), precision=HIGHEST, preferred_element_type=F32
    )


def dot_nt(a, b):
    return lax.dot_general(
        a, b, (((1,), (1,)), ((), ())), precision=HIGHEST, preferred_element_type=F32
    )


def kernel_call(body, out_shape, in_specs, args, name, scratch=(), flops=0, size=0, grant=4, out_specs=None):
    many = isinstance(out_shape, list)
    shapes = [jax.ShapeDtypeStruct(s, F32) for s in (out_shape if many else [out_shape])]
    out = pl.pallas_call(
        body,
        out_shape=shapes,
        in_specs=in_specs,
        out_specs=out_specs or [VMEM] * len(shapes),
        scratch_shapes=list(scratch),
        cost_estimate=pl.CostEstimate(flops=flops, bytes_accessed=size, transcendentals=0),
        compiler_params=pltpu.CompilerParams(vmem_limit_bytes=grant << 20),
        name=name,
    )(*args)
    return out if many else out[0]


def local_map_body(inner, outer, jac_hbm, obs_hbm, gain_hbm, out, quarter, half, third, buf, obs, gain, chain, sems):
    steps, n, _ = buf.shape
    small = [(obs_hbm, obs, steps), (gain_hbm, gain, steps + 1)]
    for source, dest, k in small:
        pltpu.make_async_copy(source, dest, sems.at[k]).start()
    pairs = steps // 2
    order = [2 * c + i for i in range(2) for c in range(pairs)]
    for t in order:
        pltpu.make_async_copy(jac_hbm.at[t], buf.at[t], sems.at[t]).start()
    for source, dest, k in small:
        pltpu.make_async_copy(source, dest, sems.at[k]).wait()
    g = gain[...]
    retain = 1.0 - g
    for t in order:
        pltpu.make_async_copy(jac_hbm.at[t], buf.at[t], sems.at[t]).wait()
        c = t // 2
        offset = jnp.broadcast_to(g * obs[t : t + 1, :], (PAD, n))
        if t % 2 == 0:
            chain[c, :n] = buf[t].T * retain
            chain[c, n:] = offset
        else:
            moved = dot_nt(chain[c], buf[t]) * retain
            chain[c, :n] = moved[:n]
            chain[c, n:] = moved[n:] + offset
    kept = {(0, pairs): out, (0, pairs // 2): half}
    kept[(0, pairs // 4)] = quarter
    kept[(pairs // 2, 3 * pairs // 4)] = third
    width = 1
    while width < pairs:
        for c in range(0, pairs, 2 * width):
            moved = dot_nn(chain[c], chain[c + width, :n])
            later = chain[c + width, n:]
            span = (c, c + 2 * width)
            dest = kept.get(span, chain.at[c])
            dest[:n] = moved[:n]
            dest[n:] = moved[n:] + later
            if span in kept and 2 * width < pairs:
                chain[c] = dest[...]
        width *= 2


def local_map(place, jac, obs, gain):
    steps, n, _ = jac.shape
    return kernel_call(
        local_map_body,
        [(n + PAD, n)] * 4 + [(steps, n, n)],
        [SMEM, SMEM, HBM, HBM, HBM],
        (*place, jac, obs, gain),
        "local_map",
        scratch=[
            pltpu.VMEM((steps, n), F32),
            pltpu.VMEM((1, n), F32),
            pltpu.VMEM((steps // 2, n + PAD, n), F32),
            pltpu.SemaphoreType.DMA((steps + 2,)),
        ],
        flops=12 * steps * n**3,
        size=4 * steps * n * n,
        grant=47,
    )


def join(earlier, later, out):
    n = out.shape[1]
    moved = dot_nn(earlier[...], later[:n])
    out[:n] = moved[:n]
    out[n:] = moved[n:] + later[n:]


def late(inner, outer, level):
    index = inner if level < 4 else outer
    return jnp.bitwise_and(jnp.right_shift(index[0], level % 4), 1) == 1


def total_body(level, inner, outer, own, other, out):
    n = out.shape[1]
    is_late = late(inner, outer, level)
    earlier = jnp.where(is_late, other[...], own[...])
    later = jnp.where(is_late, own[...], other[...])
    moved = dot_nn(earlier, later[:n])
    out[:n] = moved[:n]
    out[n:] = moved[n:] + later[n:]


def total_call(level, place, a, b):
    n = a.shape[1]
    return kernel_call(
        functools.partial(total_body, level),
        a.shape,
        [SMEM, SMEM, VMEM, VMEM],
        (*place, a, b),
        "total",
        flops=12 * n**3,
        size=12 * n * n,
    )


def hop_body(stage, outer, first, arrived, group_map, out):
    n = out.shape[1]
    state = jnp.broadcast_to(first[...], (PAD, n))
    if stage == 1:
        state = jnp.where(jnp.right_shift(outer[0], 2) == 1, arrived[...], state)
    out[...] = dot_nn(state, group_map[:n]) + group_map[n:]


def hop(stage, place, first, arrived, group_map):
    n = group_map.shape[1]
    return kernel_call(
        functools.partial(hop_body, stage),
        (PAD, n),
        [SMEM] + [VMEM] * 3,
        (place[1], first, arrived, group_map),
        "hop",
        flops=96 * n * n,
        size=4 * n * n,
    )


def maps_body(first, *refs):
    if first:
        quarter, half, third, jac, obs, gain, smooth, pi, pairs, phi = refs[:10]
        later, moving = refs[10:]
    else:
        given, jac, obs, gain, base_powers, pi, pairs = refs[:7]
        later, moving = refs[7:]
    n = jac.shape[1]
    size = n + PAD
    lanes = 4
    depth = jac.shape[0] // lanes
    if first:
        row = lax.broadcasted_iota(jnp.int32, (size, n), 0)
        column = lax.broadcasted_iota(jnp.int32, (size, n), 1)
        moving[0] = jnp.where(row == column, 1.0, 0.0).astype(F32)
        moving[1] = quarter[...]
        moving[2] = half[...]
        join(half, third, moving.at[3])
        starts = moving
    else:
        starts = given
        factor = base_powers.at[0]
    g = gain[...]
    retain = 1.0 - g

    def two(pair):
        for i in range(2):
            for u in range(2):
                c = 2 * pair + u
                k = 2 * c + i
                t = c * depth + i + (0 if first else 2)
                source = starts if i == 0 else moving
                predicted = dot_nt(source[c], jac[t])
                pi[k] = predicted
                offset = g * obs[pl.ds(t, 1), :]
                if i == 0 or first:
                    dest = moving if i == 0 else phi
                    dest[c, :n] = predicted[:n] * retain
                    dest[c, n:] = predicted[n:] * retain + offset
                change = -(predicted * g)
                dest = pairs if i == 0 else later
                dest[c, :n] = change[:n]
                dest[c, n:] = change[n:] + offset

    if first:
        pl.loop(0, lanes // 2)(two)
    else:
        two(0)
        two(1)
    if first:
        moving[0, :n] = smooth[...].T

    @pl.loop(0, lanes)
    def _(c):
        pairs[c] = pairs[c] + dot_nn(later[c], factor[...] if not first else moving[0, :n])


def offset_map_body(even, odd, base_powers, out, quads):
    @pl.loop(0, quads.shape[0])
    def _(c):
        quads[c] = even[c] + dot_nn(odd[c], base_powers[1])

    halves = [quads[c] + dot_nn(quads[c + 1], base_powers[2]) for c in (0, 2)]
    out[...] = halves[0] + dot_nn(halves[1], base_powers[3])


def maps(first, starts, jac, obs, gain, factor):
    n = jac.shape[1]
    size = n + PAD
    four = (4, size, n)
    shapes = [(8, size, n), four] + ([four] if first else [])
    scratch = [four, four]
    return kernel_call(
        functools.partial(maps_body, first),
        shapes,
        [VMEM] * (len(starts) + 4),
        (*starts, jac, obs, gain, factor),
        "maps",
        scratch=[pltpu.VMEM(x, F32) for x in scratch],
        flops=12 * 8 * n**3,
        size=8 * 12 * n * n,
        grant=8,
    )


def base_powers_body(smooth, out):
    out[0] = smooth[...].T

    @pl.loop(1, out.shape[0])
    def _(k):
        out[k] = dot_nn(out[k - 1], out[k - 1])


def high_powers_body(base_powers, out):
    out[0] = base_powers[base_powers.shape[0] - 1]

    @pl.loop(1, out.shape[0])
    def _(k):
        out[k] = dot_nn(out[k - 1], out[k - 1])


def offsets_join_body(level, inner, outer, own_map, other_map, own, other, high, through, out):
    n = out.shape[1]
    is_late = late(inner, outer, level)
    early_map = jnp.where(is_late, other_map[...], own_map[...])
    later = jnp.where(is_late, own[...], other[...])
    moved = dot_nn(early_map, later[:n])
    through[:n] = moved[:n]
    through[n:] = moved[n:] + later[n:]
    out[...] = jnp.where(is_late, other[...], own[...]) + dot_nn(through[...], high[level])


def inside_body(level, inner, outer, other_map, through, ends, *refs):
    before_out, behind_out = refs[-2:]
    n = ends.shape[2]
    is_late = late(inner, outer, level)
    if level == 0:
        row = lax.broadcasted_iota(jnp.int32, (n + PAD, n), 0)
        column = lax.broadcasted_iota(jnp.int32, (n + PAD, n), 1)
        eye = jnp.where(row == column, 1.0, 0.0).astype(F32)
        before_out[...] = jnp.where(is_late, other_map[...], eye)
        moved = dot_nn(through[...], ends[0])
        behind_out[...] = jnp.where(is_late, jnp.zeros_like(moved), moved)
        return
    before, behind = refs[:2]
    first = jnp.where(is_late, other_map[...], through[...])
    moved = dot_nn(first, jnp.where(is_late, behind[:n], ends[level]))
    kept = behind[...]
    behind_out[:n] = moved[:n] + jnp.where(is_late, jnp.zeros_like(kept[:n]), kept[:n])
    behind_out[n:] = moved[n:] + kept[n:]
    moved = dot_nn(other_map[...], before[:n])
    kept = before[...]
    before_out[:n] = jnp.where(is_late, moved[:n], kept[:n])
    before_out[n:] = jnp.where(is_late, moved[n:] + kept[n:], kept[n:])


def entry_map_body(inner, outer, row_map, twin, chip_map, out):
    n = out.shape[1]
    row = lax.broadcasted_iota(jnp.int32, (n + PAD, n), 0)
    column = lax.broadcasted_iota(jnp.int32, (n + PAD, n), 1)
    eye = jnp.where(row == column, 1.0, 0.0).astype(F32)
    out[...] = jnp.where(late(inner, outer, 3), row_map[...], eye)
    for level, earlier in ((4, twin), (5, chip_map)):
        is_late = late(inner, outer, level)
        moved = dot_nn(earlier[...], out[:n])
        later = out[...]
        out[:n] = jnp.where(is_late, moved[:n], later[:n])
        out[n:] = jnp.where(is_late, moved[n:] + later[n:], later[n:])


def offset_body(outer, first, arrived, near, far, skipped, entry_map, offset_map, entry, offset):
    n = entry_map.shape[1]
    here = jnp.right_shift(outer[0], 2)
    state = dot_nn(far[...], skipped[:n]) + skipped[n:]
    state = jnp.where(here == 3, state, near[...])
    state = jnp.where(here == 1, arrived[...], state)
    state = jnp.where(here == 0, jnp.broadcast_to(first[...], (PAD, n)), state)
    state = dot_nn(state, entry_map[:n]) + entry_map[n:]
    entry[...] = state
    offset[...] = dot_nn(state, offset_map[:n]) + offset_map[n:]


def spread_body(level, inner, outer, own, other, high, out):
    is_late = late(inner, outer, level)
    early_half = jnp.where(is_late, other[...], own[...])
    late_half = jnp.where(is_late, own[...], other[...])
    out[...] = early_half + dot_nn(late_half, high[level])


def ends_body(inner, outer, base_powers, high, ends):
    ends[0] = base_powers[0]
    for k in range(ends.shape[0] - 1):
        moved = dot_nn(ends[k], high[k])
        ends[k + 1] = jnp.where(late(inner, outer, k), ends[k], moved)


def states_body(entry, before, even, odd, obs, gain, pred, filt):
    steps, n = pred.shape
    g = gain[...]
    state = dot_nn(entry[...], before[:n]) + before[n:]

    @pl.loop(0, 4)
    def _(c):
        for i in range(4):
            t = 4 * c + i
            pi = even if i < 2 else odd
            k = 2 * c + i % 2
            predicted = (dot_nn(state, pi[k, :n]) + pi[k, n:])[:1]
            pred[pl.ds(t, 1), :] = predicted
            filt[pl.ds(t, 1), :] = predicted + g * (obs[pl.ds(t, 1), :] - predicted)


def local_body(pred, filt, base_powers, base, shifted):
    steps, n = pred.shape
    local = filt[...] - pred[...]
    shifted[steps:, :] = jnp.zeros((steps, n), F32)
    level = 0
    reach = 1
    while reach < steps:
        shifted[:steps, :] = local
        local = local + dot_nn(shifted[reach : reach + steps, :], base_powers[level])
        reach *= 2
        level += 1
    base[...] = pred[...] + local


def gather_body(inner, outer, entry, behind, ends, *refs):
    others, out = refs[:-1], refs[-1]
    n = entry.shape[1]
    value = dot_nn(entry[...], behind[:n]) + behind[n:]
    for k, ref in enumerate(others):
        other = ref[...]
        other = jnp.where(late(inner, outer, 3 + k), jnp.zeros_like(other), other)
        value = value + dot_nn(other, ends[3 + k])
    out[...] = value


def backward_body(inner, outer, one, two, ends, back, base_powers, base, out):
    steps, n = base.shape
    value = back[...]
    for level, ref in ((6, one), (7, two)):
        other = ref[...]
        other = jnp.where(late(inner, outer, level), jnp.zeros_like(other), other)
        value = value + dot_nn(other, ends[level])
    left = steps - 1 - lax.broadcasted_iota(jnp.int32, (steps, n), 0)
    value = jnp.concatenate([value, value], 0)
    for level in range(base_powers.shape[0] - 1):
        value = jnp.where((left >> level) % 2 == 1, dot_nn(value, base_powers[level]), value)
    out[...] = base[...] + value


def shards(jac, obs, gain_filter, gain_smooth, init_mean):
    steps, n, _ = jac.shape
    inner_count, outer_count = lax.axis_size("inner"), lax.axis_size("outer")
    counts = {"inner": inner_count, "outer": outer_count}
    place = [lax.axis_index(axis).astype(jnp.int32)[None] for axis in ("inner", "outer")]
    gain = gain_filter[None, :]
    first = init_mean[None, :]

    def exchange(total, axis, flip, beside):
        other = lax.ppermute(total, axis, [(i, i ^ flip) for i in range(counts[axis])])
        work = beside()
        return lax.optimization_barrier((other, work))

    with jax.named_scope("compose"):
        total, quarter, half, third, loaded = local_map(place, jac, obs, gain)

    def base_work():
        levels = steps.bit_length()
        return kernel_call(
            base_powers_body,
            (levels, n, n),
            [VMEM],
            (gain_smooth,),
            "base_powers",
            flops=60 * n**3,
            size=24 * n * n,
        )

    aside = []

    def offsets_join(level, own_map, other_map, own, other):
        return kernel_call(
            functools.partial(offsets_join_body, level),
            [(n + PAD, n), (n + PAD, n)],
            [SMEM] * 2 + [VMEM] * 5,
            (*place, own_map, other_map, own, other, high),
            "offsets_join",
            flops=1,
            size=1,
            grant=6,
        )

    def inside(level, other_map, through):
        aside[:] = kernel_call(
            functools.partial(inside_body, level),
            [(n + PAD, n), (n + PAD, n)],
            [SMEM] * 2 + [VMEM] * (3 + len(aside)),
            (*place, other_map, through, ends, *aside),
            "inside",
            flops=1,
            size=1,
        )

    def partner(value, axis, flip):
        return lax.ppermute(value, axis, [(i, i ^ flip) for i in range(counts[axis])])

    own_maps, other_maps = [total], []
    with jax.named_scope("join_0"):
        other, (pi_even, even, phi) = exchange(
            total,
            "inner",
            1,
            lambda: maps(True, (quarter, half, third), loaded, obs, gain, gain_smooth),
        )
        other_maps.append(other)
        own_maps.append(total_call(0, place, own_maps[0], other))
    with jax.named_scope("join_1"):

        def work():
            base_powers = base_work()
            pi_odd, odd = maps(False, (phi,), loaded, obs, gain, base_powers)
            return base_powers, pi_odd, odd

        other, (base_powers, pi_odd, odd) = exchange(own_maps[1], "inner", 3, work)
        other_maps.append(other)
        own_maps.append(total_call(1, place, own_maps[1], other))
    with jax.named_scope("join_2"):

        def work():
            return kernel_call(
                high_powers_body,
                (7, n, n),
                [VMEM],
                (base_powers,),
                "high_powers",
                flops=72 * n**3,
                size=28 * n * n,
            )

        other = partner(own_maps[2], "inner", 4)
        offsets = kernel_call(
            offset_map_body,
            (n + PAD, n),
            [VMEM] * 3,
            (even, odd, base_powers),
            "offset_map",
            scratch=[pltpu.VMEM((4, n + PAD, n), F32)],
            flops=84 * n**3,
            size=36 * n * n,
        )
        far = partner(offsets, "inner", 1)
        other, high, offsets_done = lax.optimization_barrier((other, work(), offsets))
        other_maps.append(other)
        own_maps.append(total_call(2, place, own_maps[2], other))
    with jax.named_scope("join_3"):

        def work():
            through, joined = offsets_join(0, own_maps[0], other_maps[0], offsets, far)
            return through, joined, partner(joined, "inner", 3)

        other = partner(own_maps[3], "inner", 12)
        through, offsets, far = work()
        ends = kernel_call(
            ends_body,
            (8, n, n),
            [SMEM] * 2 + [VMEM] * 2,
            (*place, base_powers, high),
            "ends",
            flops=1,
            size=1,
        )
        other, through, ends = lax.optimization_barrier((other, through, ends))
        other_maps.append(other)
        own_maps.append(total_call(3, place, own_maps[3], other))
    with jax.named_scope("join_core"):
        twin = partner(own_maps[4], "outer", 1)
        own_maps.append(total_call(4, place, own_maps[4], twin))
    with jax.named_scope("join_z"):
        chip_map = partner(own_maps[5], "outer", 2)
        inside(0, other_maps[0], through)
        chip_map, aside[:] = lax.optimization_barrier((chip_map, aside))
        total = total_call(5, place, own_maps[5], chip_map)

    group = outer_count // 4
    def mirror(source, dest):
        return [
            (source * group + z * 2 + c, dest * group + (group // 2 - 1 - z) * 2 + c)
            for z in range(group // 2)
            for c in range(2)
        ]

    with jax.named_scope("hop_0"):
        y = hop(0, place, first, first, total)
        arrived = lax.ppermute(y, "outer", mirror(0, 1))
        far, _ = lax.optimization_barrier((far, y))
        through, offsets = offsets_join(1, own_maps[1], other_maps[1], offsets, far)
        far = partner(offsets, "inner", 4)
        arrived, through = lax.optimization_barrier((arrived, through))
    with jax.named_scope("hop_1"):
        y = hop(1, place, first, arrived, total)
        near = lax.ppermute(y, "outer", mirror(1, 2))
        farther = lax.ppermute(y, "outer", mirror(1, 3))
        sent_map, _ = lax.optimization_barrier((total, y))
        skipped = lax.ppermute(sent_map, "outer", mirror(2, 3))
        entry_map = kernel_call(
            entry_map_body,
            (n + PAD, n),
            [SMEM] * 2 + [VMEM] * 3,
            (*place, other_maps[3], twin, chip_map),
            "entry_map",
            flops=1,
            size=1,
        )
        inside(1, other_maps[1], through)
        through, offsets = offsets_join(2, own_maps[2], other_maps[2], offsets, far)
        near, farther, offsets, entry_map, aside[:] = lax.optimization_barrier(
            (near, farther, offsets, entry_map, aside)
        )
    with jax.named_scope("offset"):
        entry, value = kernel_call(
            offset_body,
            [(PAD, n), (PAD, n)],
            [SMEM] + [VMEM] * 7,
            (place[1], first, arrived, near, farther, skipped, entry_map, offsets),
            "offset",
            flops=300 * n * n,
            size=12 * n * n,
        )

    def spread(level, value, other):
        return kernel_call(
            functools.partial(spread_body, level),
            (PAD, n),
            [SMEM] * 2 + [VMEM] * 3,
            (*place, value, other, high),
            "spread",
            flops=96 * n * n,
            size=4 * n * n,
        )

    others = []
    with jax.named_scope("spread_x"):
        other = partner(value, "inner", 12)
        inside(2, other_maps[2], through)
        other, aside[:] = lax.optimization_barrier((other, aside))
        others.append(other)
        value = spread(3, value, other)
    with jax.named_scope("spread_core"):
        others.append(partner(value, "outer", 1))
        value = spread(4, value, others[1])
    with jax.named_scope("spread_z0"):
        other = partner(value, "outer", 2)
        pred, filt = kernel_call(
            states_body,
            [(steps, n), (steps, n)],
            [VMEM] * 6,
            (entry, aside[0], pi_even, pi_odd, obs, gain),
            "states",
            flops=1,
            size=1,
        )
        other, pred = lax.optimization_barrier((other, pred))
        others.append(other)
        value = spread(5, value, other)
    with jax.named_scope("spread_z1"):
        other = partner(value, "outer", 4)
        base = kernel_call(
            local_body,
            (steps, n),
            [VMEM] * 3,
            (pred, filt, base_powers),
            "local",
            scratch=[pltpu.VMEM((2 * steps, n), F32)],
            flops=1,
            size=1,
        )
        back = kernel_call(
            gather_body,
            (PAD, n),
            [SMEM] * 2 + [VMEM] * 6,
            (*place, entry, aside[1], ends, *others),
            "gather",
            flops=1,
            size=1,
        )
        other, base, back = lax.optimization_barrier((other, base, back))
        others.append(other)
        value = spread(6, value, other)
    with jax.named_scope("spread_z2"):
        other = partner(value, "outer", 14)
    with jax.named_scope("backward"):
        smoothed = kernel_call(
            backward_body,
            (steps, n),
            [SMEM] * 2 + [VMEM] * 6,
            (*place, others[3], other, ends, back, base_powers, base),
            "backward",
            flops=600 * n * n,
            size=24 * n * n,
        )
    return (filt, smoothed)


def solution(mesh):
    return jax.shard_map(
        shards,
        mesh=mesh,
        in_specs=(P(("outer", "inner"), None, None), P(("outer", "inner"), None), P(), P(), P()),
        out_specs=(P(("outer", "inner"), None), P(("outer", "inner"), None)),
        check_vma=False,
    )
```

```python
import functools

import jax
import jax.numpy as jnp
from jax import lax
from jax.experimental import pallas as pl
from jax.experimental.pallas import tpu as pltpu
from jax.sharding import PartitionSpec as P

HIGHEST = lax.Precision.HIGHEST
F32 = jnp.float32
VMEM = pl.BlockSpec(memory_space=pltpu.VMEM)
SMEM = pl.BlockSpec(memory_space=pltpu.SMEM)
HBM = pl.BlockSpec(memory_space=pltpu.MemorySpace.HBM)
PAD = 8


def dot_nn(a, b):
    return lax.dot_general(
        a, b, (((1,), (0,)), ((), ())), precision=HIGHEST, preferred_element_type=F32
    )


def dot_nt(a, b):
    return lax.dot_general(
        a, b, (((1,), (1,)), ((), ())), precision=HIGHEST, preferred_element_type=F32
    )


def kernel_call(body, out_shape, in_specs, args, name, scratch=(), flops=0, size=0, grant=4, out_specs=None):
    many = isinstance(out_shape, list)
    shapes = [jax.ShapeDtypeStruct(s, F32) for s in (out_shape if many else [out_shape])]
    out = pl.pallas_call(
        body,
        out_shape=shapes,
        in_specs=in_specs,
        out_specs=out_specs or [VMEM] * len(shapes),
        scratch_shapes=list(scratch),
        cost_estimate=pl.CostEstimate(flops=flops, bytes_accessed=size, transcendentals=0),
        compiler_params=pltpu.CompilerParams(vmem_limit_bytes=grant << 20),
        name=name,
    )(*args)
    return out if many else out[0]


def local_map_body(inner, outer, jac_hbm, obs_hbm, gain_hbm, out, quarter, half, third, buf, obs, gain, chain, sems):
    steps, n, _ = buf.shape
    small = [(obs_hbm, obs, steps), (gain_hbm, gain, steps + 1)]
    for source, dest, k in small:
        pltpu.make_async_copy(source, dest, sems.at[k]).start()
    pairs = steps // 2
    for t in range(steps):
        pltpu.make_async_copy(jac_hbm.at[t], buf.at[t], sems.at[t]).start()
    for source, dest, k in small:
        pltpu.make_async_copy(source, dest, sems.at[k]).wait()
    g = gain[...]
    retain = 1.0 - g

    def offset(t):
        return jnp.broadcast_to(g * obs[t : t + 1, :], (PAD, n))

    def arrive(c):
        for t in (2 * c, 2 * c + 1):
            pltpu.make_async_copy(jac_hbm.at[t], buf.at[t], sems.at[t]).wait()

    def begin(c):
        chain[c, :n] = buf[2 * c].T * retain
        chain[c, n:] = offset(2 * c)

    def finish(c):
        moved = dot_nt(chain[c], buf[2 * c + 1]) * retain
        chain[c, :n] = moved[:n]
        chain[c, n:] = moved[n:] + offset(2 * c + 1)

    kept = {(0, pairs): out, (0, pairs // 2): half}
    kept[(0, pairs // 4)] = quarter
    kept[(pairs // 2, 3 * pairs // 4)] = third

    def merge(c, width):
        moved = dot_nn(chain[c], chain[c + width, :n])
        later = chain[c + width, n:]
        span = (c, c + 2 * width)
        dest = kept.get(span, chain.at[c])
        dest[:n] = moved[:n]
        dest[n:] = moved[n:] + later
        if span in kept and 2 * width < pairs:
            chain[c] = dest[...]

    arrive(0)
    begin(0)
    waiting = []
    for c in range(pairs):
        if c + 1 < pairs:
            arrive(c + 1)
        ready, waiting = waiting, []
        finish(c)
        if c + 1 < pairs:
            begin(c + 1)
        for item in ready:
            merge(*item)
        if c % 2 == 1:
            waiting.append((c - 1, 1))
        for first, width in ready:
            if (first // width) % 4 == 2 and 4 * width < pairs + 1:
                waiting.append((first - 2 * width, 2 * width))
    while waiting:
        first, width = waiting.pop(0)
        merge(first, width)
        if (first // width) % 4 == 2 and 2 * width < pairs:
            waiting.append((first - 2 * width, 2 * width))


def local_map(place, jac, obs, gain):
    steps, n, _ = jac.shape
    return kernel_call(
        local_map_body,
        [(n + PAD, n)] * 4 + [(steps, n, n)],
        [SMEM, SMEM, HBM, HBM, HBM],
        (*place, jac, obs, gain),
        "local_map",
        scratch=[
            pltpu.VMEM((steps, n), F32),
            pltpu.VMEM((1, n), F32),
            pltpu.VMEM((steps // 2, n + PAD, n), F32),
            pltpu.SemaphoreType.DMA((steps + 2,)),
        ],
        flops=12 * steps * n**3,
        size=4 * steps * n * n,
        grant=47,
    )


def join(earlier, later, out):
    n = out.shape[1]
    moved = dot_nn(earlier[...], later[:n])
    out[:n] = moved[:n]
    out[n:] = moved[n:] + later[n:]


def late(inner, outer, level):
    index = inner if level < 4 else outer
    return jnp.bitwise_and(jnp.right_shift(index[0], level % 4), 1) == 1


def total_body(level, inner, outer, own, other, out):
    n = out.shape[1]
    is_late = late(inner, outer, level)
    earlier = jnp.where(is_late, other[...], own[...])
    later = jnp.where(is_late, own[...], other[...])
    moved = dot_nn(earlier, later[:n])
    out[:n] = moved[:n]
    out[n:] = moved[n:] + later[n:]


def total_call(level, place, a, b):
    n = a.shape[1]
    return kernel_call(
        functools.partial(total_body, level),
        a.shape,
        [SMEM, SMEM, VMEM, VMEM],
        (*place, a, b),
        "total",
        flops=12 * n**3,
        size=12 * n * n,
    )


def hop_body(stage, outer, first, arrived, group_map, out):
    n = out.shape[1]
    state = jnp.broadcast_to(first[...], (PAD, n))
    if stage == 1:
        state = jnp.where(jnp.right_shift(outer[0], 2) == 1, arrived[...], state)
    out[...] = dot_nn(state, group_map[:n]) + group_map[n:]


def hop(stage, place, first, arrived, group_map):
    n = group_map.shape[1]
    return kernel_call(
        functools.partial(hop_body, stage),
        (PAD, n),
        [SMEM] + [VMEM] * 3,
        (place[1], first, arrived, group_map),
        "hop",
        flops=96 * n * n,
        size=4 * n * n,
    )


def maps_body(first, *refs):
    if first:
        quarter, half, third, jac, obs, gain, smooth, pi, pairs, phi = refs[:10]
        later, moving = refs[10:]
    else:
        given, jac, obs, gain, base_powers, pi, pairs = refs[:7]
        later, moving = refs[7:]
    n = jac.shape[1]
    size = n + PAD
    lanes = 4
    depth = jac.shape[0] // lanes
    if first:
        row = lax.broadcasted_iota(jnp.int32, (size, n), 0)
        column = lax.broadcasted_iota(jnp.int32, (size, n), 1)
        moving[0] = jnp.where(row == column, 1.0, 0.0).astype(F32)
        moving[1] = quarter[...]
        moving[2] = half[...]
        join(half, third, moving.at[3])
        starts = moving
    else:
        starts = given
        factor = base_powers.at[0]
    g = gain[...]
    retain = 1.0 - g

    def two(pair):
        for i in range(2):
            for u in range(2):
                c = 2 * pair + u
                k = 2 * c + i
                t = c * depth + i + (0 if first else 2)
                source = starts if i == 0 else moving
                predicted = dot_nt(source[c], jac[t])
                pi[k] = predicted
                offset = g * obs[pl.ds(t, 1), :]
                if i == 0 or first:
                    dest = moving if i == 0 else phi
                    dest[c, :n] = predicted[:n] * retain
                    dest[c, n:] = predicted[n:] * retain + offset
                change = -(predicted * g)
                dest = pairs if i == 0 else later
                dest[c, :n] = change[:n]
                dest[c, n:] = change[n:] + offset

    if first:
        pl.loop(0, lanes // 2)(two)
    else:
        two(0)
        two(1)
    if first:
        moving[0, :n] = smooth[...].T

    @pl.loop(0, lanes)
    def _(c):
        pairs[c] = pairs[c] + dot_nn(later[c], factor[...] if not first else moving[0, :n])


def offset_map_body(even, odd, base_powers, out, quads):
    @pl.loop(0, quads.shape[0])
    def _(c):
        quads[c] = even[c] + dot_nn(odd[c], base_powers[1])

    halves = [quads[c] + dot_nn(quads[c + 1], base_powers[2]) for c in (0, 2)]
    out[...] = halves[0] + dot_nn(halves[1], base_powers[3])


def maps(first, starts, jac, obs, gain, factor):
    n = jac.shape[1]
    size = n + PAD
    four = (4, size, n)
    shapes = [(8, size, n), four] + ([four] if first else [])
    scratch = [four, four]
    return kernel_call(
        functools.partial(maps_body, first),
        shapes,
        [VMEM] * (len(starts) + 4),
        (*starts, jac, obs, gain, factor),
        "maps",
        scratch=[pltpu.VMEM(x, F32) for x in scratch],
        flops=12 * 8 * n**3,
        size=8 * 12 * n * n,
        grant=8,
    )


def base_powers_body(smooth, out):
    out[0] = smooth[...].T

    @pl.loop(1, out.shape[0])
    def _(k):
        out[k] = dot_nn(out[k - 1], out[k - 1])


def high_powers_body(base_powers, out):
    out[0] = base_powers[base_powers.shape[0] - 1]

    @pl.loop(1, out.shape[0])
    def _(k):
        out[k] = dot_nn(out[k - 1], out[k - 1])


def offsets_join_body(level, inner, outer, own_map, other_map, own, other, high, through, out):
    n = out.shape[1]
    is_late = late(inner, outer, level)
    early_map = jnp.where(is_late, other_map[...], own_map[...])
    later = jnp.where(is_late, own[...], other[...])
    moved = dot_nn(early_map, later[:n])
    through[:n] = moved[:n]
    through[n:] = moved[n:] + later[n:]
    out[...] = jnp.where(is_late, other[...], own[...]) + dot_nn(through[...], high[level])


def inside_body(level, inner, outer, other_map, through, high, *refs):
    before_out, behind_out, lift_out = refs[-3:]
    n = high.shape[2]
    is_late = late(inner, outer, level)
    if level == 0:
        row = lax.broadcasted_iota(jnp.int32, (n + PAD, n), 0)
        column = lax.broadcasted_iota(jnp.int32, (n + PAD, n), 1)
        eye = jnp.where(row == column, 1.0, 0.0).astype(F32)
        before_out[...] = jnp.where(is_late, other_map[...], eye)
        behind_out[...] = jnp.where(is_late, jnp.zeros_like(eye), through[...])
        lift_out[...] = jnp.where(is_late, eye[:n], high[level])
        return
    before, behind, lift = refs[:3]
    first = jnp.where(is_late, other_map[...], through[...])
    moved = dot_nn(first, jnp.where(is_late, behind[:n], lift[...]))
    kept = behind[...]
    behind_out[:n] = moved[:n] + jnp.where(is_late, jnp.zeros_like(kept[:n]), kept[:n])
    behind_out[n:] = moved[n:] + kept[n:]
    second = jnp.where(is_late, other_map[:n], lift[...])
    moved = dot_nn(second, jnp.where(is_late, before[:n], high[level]))
    edge = dot_nn(other_map[n:], before[:n]) + before[n:]
    before_out[:n] = jnp.where(is_late, moved, before[:n])
    before_out[n:] = jnp.where(is_late, edge, before[n:])
    lift_out[...] = jnp.where(is_late, lift[...], moved)


def entry_map_body(inner, outer, row_map, twin, chip_map, out):
    n = out.shape[1]
    row = lax.broadcasted_iota(jnp.int32, (n + PAD, n), 0)
    column = lax.broadcasted_iota(jnp.int32, (n + PAD, n), 1)
    eye = jnp.where(row == column, 1.0, 0.0).astype(F32)
    out[...] = jnp.where(late(inner, outer, 3), row_map[...], eye)
    for level, earlier in ((4, twin), (5, chip_map)):
        is_late = late(inner, outer, level)
        moved = dot_nn(earlier[...], out[:n])
        later = out[...]
        out[:n] = jnp.where(is_late, moved[:n], later[:n])
        out[n:] = jnp.where(is_late, moved[n:] + later[n:], later[n:])


def offset_body(outer, first, arrived, near, far, skipped, entry_map, offset_map, entry, offset):
    n = entry_map.shape[1]
    here = jnp.right_shift(outer[0], 2)
    state = dot_nn(far[...], skipped[:n]) + skipped[n:]
    state = jnp.where(here == 3, state, near[...])
    state = jnp.where(here == 1, arrived[...], state)
    state = jnp.where(here == 0, jnp.broadcast_to(first[...], (PAD, n)), state)
    state = dot_nn(state, entry_map[:n]) + entry_map[n:]
    entry[...] = state
    offset[...] = dot_nn(state, offset_map[:n]) + offset_map[n:]


def spread_body(level, inner, outer, own, other, high, out):
    is_late = late(inner, outer, level)
    early_half = jnp.where(is_late, other[...], own[...])
    late_half = jnp.where(is_late, own[...], other[...])
    out[...] = early_half + dot_nn(late_half, high[level])


def ends_body(inner, outer, lift, base_powers, high, *ends):
    ends[0][...] = dot_nn(lift[...], base_powers[0])
    for k in range(len(ends) - 1):
        moved = dot_nn(ends[k][...], high[3 + k])
        ends[k + 1][...] = jnp.where(late(inner, outer, 3 + k), ends[k][...], moved)


def states_body(entry, before, even, odd, obs, gain, pred, filt):
    steps, n = pred.shape
    g = gain[...]
    state = dot_nn(entry[...], before[:n]) + before[n:]

    @pl.loop(0, 4)
    def _(c):
        for i in range(4):
            t = 4 * c + i
            pi = even if i < 2 else odd
            k = 2 * c + i % 2
            predicted = (dot_nn(state, pi[k, :n]) + pi[k, n:])[:1]
            pred[pl.ds(t, 1), :] = predicted
            filt[pl.ds(t, 1), :] = predicted + g * (obs[pl.ds(t, 1), :] - predicted)


def local_body(pred, filt, base_powers, base, shifted):
    steps, n = pred.shape
    local = filt[...] - pred[...]
    shifted[steps:, :] = jnp.zeros((steps, n), F32)
    level = 0
    reach = 1
    while reach < steps:
        shifted[:steps, :] = local
        local = local + dot_nn(shifted[reach : reach + steps, :], base_powers[level])
        reach *= 2
        level += 1
    base[...] = pred[...] + local


def gather_body(inner, outer, entry, behind, base_powers, *refs):
    count = len(refs) // 2
    others, ends, out = refs[:count], refs[count : 2 * count], refs[2 * count]
    n = entry.shape[1]
    inside = dot_nn(entry[...], behind[:n]) + behind[n:]
    value = dot_nn(inside, base_powers[0])
    for k in range(count):
        other = others[k][...]
        other = jnp.where(late(inner, outer, 3 + k), jnp.zeros_like(other), other)
        value = value + dot_nn(other, ends[k][...])
    out[...] = value


def backward_body(inner, outer, other, end, back, base_powers, base, out):
    steps, n = base.shape
    value = other[...]
    value = jnp.where(late(inner, outer, 7), jnp.zeros_like(value), value)
    value = back[...] + dot_nn(value, end[...])
    left = steps - 1 - lax.broadcasted_iota(jnp.int32, (steps, n), 0)
    value = jnp.concatenate([value, value], 0)
    for level in range(base_powers.shape[0] - 1):
        value = jnp.where((left >> level) % 2 == 1, dot_nn(value, base_powers[level]), value)
    out[...] = base[...] + value


def shards(jac, obs, gain_filter, gain_smooth, init_mean):
    steps, n, _ = jac.shape
    inner_count, outer_count = lax.axis_size("inner"), lax.axis_size("outer")
    counts = {"inner": inner_count, "outer": outer_count}
    place = [lax.axis_index(axis).astype(jnp.int32)[None] for axis in ("inner", "outer")]
    gain = gain_filter[None, :]
    first = init_mean[None, :]

    def exchange(total, axis, flip, beside):
        other = lax.ppermute(total, axis, [(i, i ^ flip) for i in range(counts[axis])])
        work = beside()
        return lax.optimization_barrier((other, work))

    with jax.named_scope("compose"):
        total, quarter, half, third, loaded = local_map(place, jac, obs, gain)

    def base_work():
        levels = steps.bit_length()
        return kernel_call(
            base_powers_body,
            (levels, n, n),
            [VMEM],
            (gain_smooth,),
            "base_powers",
            flops=60 * n**3,
            size=24 * n * n,
        )

    aside = []

    def offsets_join(level, own_map, other_map, own, other):
        return kernel_call(
            functools.partial(offsets_join_body, level),
            [(n + PAD, n), (n + PAD, n)],
            [SMEM] * 2 + [VMEM] * 5,
            (*place, own_map, other_map, own, other, high),
            "offsets_join",
            flops=1,
            size=1,
            grant=6,
        )

    def inside(level, other_map, through):
        aside[:] = kernel_call(
            functools.partial(inside_body, level),
            [(n + PAD, n), (n + PAD, n), (n, n)],
            [SMEM] * 2 + [VMEM] * (3 + len(aside)),
            (*place, other_map, through, high, *aside),
            "inside",
            flops=1,
            size=1,
        )

    def partner(value, axis, flip):
        return lax.ppermute(value, axis, [(i, i ^ flip) for i in range(counts[axis])])

    own_maps, other_maps = [total], []
    with jax.named_scope("join_0"):
        other, (pi_even, even, phi) = exchange(
            total,
            "inner",
            1,
            lambda: maps(True, (quarter, half, third), loaded, obs, gain, gain_smooth),
        )
        other_maps.append(other)
        own_maps.append(total_call(0, place, own_maps[0], other))
    with jax.named_scope("join_1"):

        def work():
            base_powers = base_work()
            pi_odd, odd = maps(False, (phi,), loaded, obs, gain, base_powers)
            return base_powers, pi_odd, odd

        other, (base_powers, pi_odd, odd) = exchange(own_maps[1], "inner", 3, work)
        other_maps.append(other)
        own_maps.append(total_call(1, place, own_maps[1], other))
    with jax.named_scope("join_2"):

        def work():
            return kernel_call(
                high_powers_body,
                (7, n, n),
                [VMEM],
                (base_powers,),
                "high_powers",
                flops=72 * n**3,
                size=28 * n * n,
            )

        other = partner(own_maps[2], "inner", 4)
        offsets = kernel_call(
            offset_map_body,
            (n + PAD, n),
            [VMEM] * 3,
            (even, odd, base_powers),
            "offset_map",
            scratch=[pltpu.VMEM((4, n + PAD, n), F32)],
            flops=84 * n**3,
            size=36 * n * n,
        )
        far = partner(offsets, "inner", 1)
        other, high, offsets_done = lax.optimization_barrier((other, work(), offsets))
        other_maps.append(other)
        own_maps.append(total_call(2, place, own_maps[2], other))
    with jax.named_scope("join_3"):

        def work():
            through, joined = offsets_join(0, own_maps[0], other_maps[0], offsets, far)
            return through, joined, partner(joined, "inner", 3)

        other = partner(own_maps[3], "inner", 12)
        through, offsets, far = work()
        other, through = lax.optimization_barrier((other, through))
        other_maps.append(other)
        own_maps.append(total_call(3, place, own_maps[3], other))
    with jax.named_scope("join_core"):
        twin = partner(own_maps[4], "outer", 1)
        own_maps.append(total_call(4, place, own_maps[4], twin))
    with jax.named_scope("join_z"):
        chip_map = partner(own_maps[5], "outer", 2)
        inside(0, other_maps[0], through)
        chip_map, aside[:] = lax.optimization_barrier((chip_map, aside))
        total = total_call(5, place, own_maps[5], chip_map)

    group = outer_count // 4
    def mirror(source, dest):
        return [
            (source * group + z * 2 + c, dest * group + (group // 2 - 1 - z) * 2 + c)
            for z in range(group // 2)
            for c in range(2)
        ]

    with jax.named_scope("hop_0"):
        y = hop(0, place, first, first, total)
        arrived = lax.ppermute(y, "outer", mirror(0, 1))
        far, _ = lax.optimization_barrier((far, y))
        through, offsets = offsets_join(1, own_maps[1], other_maps[1], offsets, far)
        far = partner(offsets, "inner", 4)
        arrived, through = lax.optimization_barrier((arrived, through))
    with jax.named_scope("hop_1"):
        y = hop(1, place, first, arrived, total)
        near = lax.ppermute(y, "outer", mirror(1, 2))
        farther = lax.ppermute(y, "outer", mirror(1, 3))
        sent_map, _ = lax.optimization_barrier((total, y))
        skipped = lax.ppermute(sent_map, "outer", mirror(2, 3))
        entry_map = kernel_call(
            entry_map_body,
            (n + PAD, n),
            [SMEM] * 2 + [VMEM] * 3,
            (*place, other_maps[3], twin, chip_map),
            "entry_map",
            flops=1,
            size=1,
        )
        inside(1, other_maps[1], through)
        through, offsets = offsets_join(2, own_maps[2], other_maps[2], offsets, far)
        near, farther, offsets, entry_map, aside[:] = lax.optimization_barrier(
            (near, farther, offsets, entry_map, aside)
        )
    with jax.named_scope("offset"):
        entry, value = kernel_call(
            offset_body,
            [(PAD, n), (PAD, n)],
            [SMEM] + [VMEM] * 7,
            (place[1], first, arrived, near, farther, skipped, entry_map, offsets),
            "offset",
            flops=300 * n * n,
            size=12 * n * n,
        )

    def spread(level, value, other):
        return kernel_call(
            functools.partial(spread_body, level),
            (PAD, n),
            [SMEM] * 2 + [VMEM] * 3,
            (*place, value, other, high),
            "spread",
            flops=96 * n * n,
            size=4 * n * n,
        )

    others = []
    with jax.named_scope("spread_x"):
        other = partner(value, "inner", 12)
        inside(2, other_maps[2], through)
        other, aside[:] = lax.optimization_barrier((other, aside))
        others.append(other)
        value = spread(3, value, other)
    with jax.named_scope("spread_core"):
        others.append(partner(value, "outer", 1))
        value = spread(4, value, others[1])
    with jax.named_scope("spread_z0"):
        other = partner(value, "outer", 2)
        ends = kernel_call(
            ends_body,
            [(n, n)] * 5,
            [SMEM] * 2 + [VMEM] * 3,
            (*place, aside[2], base_powers, high),
            "ends",
            flops=60 * n**3,
            size=36 * n * n,
        )
        other, ends = lax.optimization_barrier((other, ends))
        others.append(other)
        value = spread(5, value, other)
    with jax.named_scope("spread_z1"):
        other = partner(value, "outer", 4)
        pred, filt = kernel_call(
            states_body,
            [(steps, n), (steps, n)],
            [VMEM] * 6,
            (entry, aside[0], pi_even, pi_odd, obs, gain),
            "states",
            flops=17 * 96 * n * n,
            size=68 * n * n,
        )
        other, pred = lax.optimization_barrier((other, pred))
        others.append(other)
        value = spread(6, value, other)
    with jax.named_scope("spread_z2"):
        other = partner(value, "outer", 14)
        base = kernel_call(
            local_body,
            (steps, n),
            [VMEM] * 3,
            (pred, filt, base_powers),
            "local",
            scratch=[pltpu.VMEM((2 * steps, n), F32)],
            flops=8 * 96 * n * n,
            size=16 * n * n,
        )
        back = kernel_call(
            gather_body,
            (PAD, n),
            [SMEM] * 2 + [VMEM] * 11,
            (*place, entry, aside[1], base_powers, *others, *ends[:4]),
            "gather",
            flops=600 * n * n,
            size=20 * n * n,
        )
        other, base, back = lax.optimization_barrier((other, base, back))
    with jax.named_scope("backward"):
        smoothed = kernel_call(
            backward_body,
            (steps, n),
            [SMEM] * 2 + [VMEM] * 5,
            (*place, other, ends[4], back, base_powers, base),
            "backward",
            flops=600 * n * n,
            size=24 * n * n,
        )
    return (filt, smoothed)


def solution(mesh):
    return jax.shard_map(
        shards,
        mesh=mesh,
        in_specs=(P(("outer", "inner"), None, None), P(("outer", "inner"), None), P(), P(), P()),
        out_specs=(P(("outer", "inner"), None), P(("outer", "inner"), None)),
        check_vma=False,
    )
```

```python
import functools

import jax
import jax.numpy as jnp
from jax import lax
from jax.experimental import pallas as pl
from jax.experimental.pallas import tpu as pltpu
from jax.sharding import PartitionSpec as P

HIGHEST = lax.Precision.HIGHEST
F32 = jnp.float32
VMEM = pl.BlockSpec(memory_space=pltpu.VMEM)
SMEM = pl.BlockSpec(memory_space=pltpu.SMEM)
HBM = pl.BlockSpec(memory_space=pltpu.MemorySpace.HBM)
PAD = 8


def dot_nn(a, b):
    return lax.dot_general(
        a, b, (((1,), (0,)), ((), ())), precision=HIGHEST, preferred_element_type=F32
    )


def dot_nt(a, b):
    return lax.dot_general(
        a, b, (((1,), (1,)), ((), ())), precision=HIGHEST, preferred_element_type=F32
    )


def kernel_call(body, out_shape, in_specs, args, name, scratch=(), flops=0, size=0, grant=4, out_specs=None):
    many = isinstance(out_shape, list)
    shapes = [jax.ShapeDtypeStruct(s, F32) for s in (out_shape if many else [out_shape])]
    out = pl.pallas_call(
        body,
        out_shape=shapes,
        in_specs=in_specs,
        out_specs=out_specs or [VMEM] * len(shapes),
        scratch_shapes=list(scratch),
        cost_estimate=pl.CostEstimate(flops=flops, bytes_accessed=size, transcendentals=0),
        compiler_params=pltpu.CompilerParams(vmem_limit_bytes=grant << 20),
        name=name,
    )(*args)
    return out if many else out[0]


def local_map_body(inner, outer, jac_hbm, obs_hbm, gain_hbm, out, quarter, half, third, buf, obs, gain, chain, sems):
    steps, n, _ = buf.shape
    small = [(obs_hbm, obs, steps), (gain_hbm, gain, steps + 1)]
    for source, dest, k in small:
        pltpu.make_async_copy(source, dest, sems.at[k]).start()
    pairs = steps // 2
    for t in range(steps):
        pltpu.make_async_copy(jac_hbm.at[t], buf.at[t], sems.at[t]).start()
    for source, dest, k in small:
        pltpu.make_async_copy(source, dest, sems.at[k]).wait()
    g = gain[...]
    retain = 1.0 - g

    def offset(t):
        return jnp.broadcast_to(g * obs[t : t + 1, :], (PAD, n))

    def arrive(c):
        for t in (2 * c, 2 * c + 1):
            pltpu.make_async_copy(jac_hbm.at[t], buf.at[t], sems.at[t]).wait()

    def begin(c):
        chain[c, :n] = buf[2 * c].T * retain
        chain[c, n:] = offset(2 * c)

    def finish(c):
        moved = dot_nt(chain[c], buf[2 * c + 1]) * retain
        chain[c, :n] = moved[:n]
        chain[c, n:] = moved[n:] + offset(2 * c + 1)

    kept = {(0, pairs): out, (0, pairs // 2): half}
    kept[(0, pairs // 4)] = quarter
    kept[(pairs // 2, 3 * pairs // 4)] = third

    def merge(c, width):
        moved = dot_nn(chain[c], chain[c + width, :n])
        later = chain[c + width, n:]
        span = (c, c + 2 * width)
        dest = kept.get(span, chain.at[c])
        dest[:n] = moved[:n]
        dest[n:] = moved[n:] + later
        if span in kept and 2 * width < pairs:
            chain[c] = dest[...]

    arrive(0)
    begin(0)
    waiting = []
    for c in range(pairs):
        if c + 1 < pairs:
            arrive(c + 1)
        ready, waiting = waiting, []
        finish(c)
        if c + 1 < pairs:
            begin(c + 1)
        for item in ready:
            merge(*item)
        if c % 2 == 1:
            waiting.append((c - 1, 1))
        for first, width in ready:
            if (first // width) % 4 == 2 and 4 * width < pairs + 1:
                waiting.append((first - 2 * width, 2 * width))
    while waiting:
        first, width = waiting.pop(0)
        merge(first, width)
        if (first // width) % 4 == 2 and 2 * width < pairs:
            waiting.append((first - 2 * width, 2 * width))


def local_map(place, jac, obs, gain):
    steps, n, _ = jac.shape
    return kernel_call(
        local_map_body,
        [(n + PAD, n)] * 4 + [(steps, n, n)],
        [SMEM, SMEM, HBM, HBM, HBM],
        (*place, jac, obs, gain),
        "local_map",
        scratch=[
            pltpu.VMEM((steps, n), F32),
            pltpu.VMEM((1, n), F32),
            pltpu.VMEM((steps // 2, n + PAD, n), F32),
            pltpu.SemaphoreType.DMA((steps + 2,)),
        ],
        flops=12 * steps * n**3,
        size=4 * steps * n * n,
        grant=47,
    )


def join(earlier, later, out):
    n = out.shape[1]
    moved = dot_nn(earlier[...], later[:n])
    out[:n] = moved[:n]
    out[n:] = moved[n:] + later[n:]


def late(inner, outer, level):
    index = inner if level < 4 else outer
    return jnp.bitwise_and(jnp.right_shift(index[0], level % 4), 1) == 1


def total_body(level, inner, outer, own, other, out):
    n = out.shape[1]
    is_late = late(inner, outer, level)
    earlier = jnp.where(is_late, other[...], own[...])
    later = jnp.where(is_late, own[...], other[...])
    moved = dot_nn(earlier, later[:n])
    out[:n] = moved[:n]
    out[n:] = moved[n:] + later[n:]


def total_call(level, place, a, b):
    n = a.shape[1]
    return kernel_call(
        functools.partial(total_body, level),
        a.shape,
        [SMEM, SMEM, VMEM, VMEM],
        (*place, a, b),
        "total",
        flops=12 * n**3,
        size=12 * n * n,
    )


def hop_body(stage, outer, first, arrived, group_map, out):
    n = out.shape[1]
    state = jnp.broadcast_to(first[...], (PAD, n))
    if stage == 1:
        state = jnp.where(jnp.right_shift(outer[0], 2) == 1, arrived[...], state)
    out[...] = dot_nn(state, group_map[:n]) + group_map[n:]


def hop(stage, place, first, arrived, group_map):
    n = group_map.shape[1]
    return kernel_call(
        functools.partial(hop_body, stage),
        (PAD, n),
        [SMEM] + [VMEM] * 3,
        (place[1], first, arrived, group_map),
        "hop",
        flops=96 * n * n,
        size=4 * n * n,
    )


def maps_body(first, *refs):
    if first:
        quarter, half, third, jac, obs, gain, smooth, pi, pairs, phi = refs[:10]
        later, moving = refs[10:]
    else:
        given, jac, obs, gain, base_powers, pi, pairs = refs[:7]
        later, moving = refs[7:]
    n = jac.shape[1]
    size = n + PAD
    lanes = 4
    depth = jac.shape[0] // lanes
    if first:
        row = lax.broadcasted_iota(jnp.int32, (size, n), 0)
        column = lax.broadcasted_iota(jnp.int32, (size, n), 1)
        moving[0] = jnp.where(row == column, 1.0, 0.0).astype(F32)
        moving[1] = quarter[...]
        moving[2] = half[...]
        join(half, third, moving.at[3])
        starts = moving
    else:
        starts = given
        factor = base_powers.at[0]
    g = gain[...]
    retain = 1.0 - g

    def two(pair):
        for i in range(2):
            for u in range(2):
                c = 2 * pair + u
                k = 2 * c + i
                t = c * depth + i + (0 if first else 2)
                source = starts if i == 0 else moving
                predicted = dot_nt(source[c], jac[t])
                pi[k] = predicted
                offset = g * obs[pl.ds(t, 1), :]
                if i == 0 or first:
                    dest = moving if i == 0 else phi
                    dest[c, :n] = predicted[:n] * retain
                    dest[c, n:] = predicted[n:] * retain + offset
                change = -(predicted * g)
                dest = pairs if i == 0 else later
                dest[c, :n] = change[:n]
                dest[c, n:] = change[n:] + offset

    if first:
        pl.loop(0, lanes // 2)(two)
    else:
        two(0)
        two(1)
    if first:
        moving[0, :n] = smooth[...].T

    @pl.loop(0, lanes)
    def _(c):
        pairs[c] = pairs[c] + dot_nn(later[c], factor[...] if not first else moving[0, :n])


def offset_map_body(even, odd, base_powers, out, quads):
    @pl.loop(0, quads.shape[0])
    def _(c):
        quads[c] = even[c] + dot_nn(odd[c], base_powers[1])

    halves = [quads[c] + dot_nn(quads[c + 1], base_powers[2]) for c in (0, 2)]
    out[...] = halves[0] + dot_nn(halves[1], base_powers[3])


def maps(first, starts, jac, obs, gain, factor):
    n = jac.shape[1]
    size = n + PAD
    four = (4, size, n)
    shapes = [(8, size, n), four] + ([four] if first else [])
    scratch = [four, four]
    return kernel_call(
        functools.partial(maps_body, first),
        shapes,
        [VMEM] * (len(starts) + 4),
        (*starts, jac, obs, gain, factor),
        "maps",
        scratch=[pltpu.VMEM(x, F32) for x in scratch],
        flops=12 * 8 * n**3,
        size=8 * 12 * n * n,
        grant=8,
    )


def base_powers_body(smooth, out):
    out[0] = smooth[...].T

    @pl.loop(1, out.shape[0])
    def _(k):
        out[k] = dot_nn(out[k - 1], out[k - 1])


def high_powers_body(base_powers, out):
    out[0] = base_powers[base_powers.shape[0] - 1]

    @pl.loop(1, out.shape[0])
    def _(k):
        out[k] = dot_nn(out[k - 1], out[k - 1])


def offsets_join_body(level, inner, outer, own_map, other_map, own, other, high, through, out):
    n = out.shape[1]
    is_late = late(inner, outer, level)
    early_map = jnp.where(is_late, other_map[...], own_map[...])
    later = jnp.where(is_late, own[...], other[...])
    moved = dot_nn(early_map, later[:n])
    through[:n] = moved[:n]
    through[n:] = moved[n:] + later[n:]
    out[...] = jnp.where(is_late, other[...], own[...]) + dot_nn(through[...], high[level])


def inside_body(level, inner, outer, other_map, through, high, *refs):
    before_out, behind_out, lift_out = refs[-3:]
    n = high.shape[2]
    is_late = late(inner, outer, level)
    if level == 0:
        row = lax.broadcasted_iota(jnp.int32, (n + PAD, n), 0)
        column = lax.broadcasted_iota(jnp.int32, (n + PAD, n), 1)
        eye = jnp.where(row == column, 1.0, 0.0).astype(F32)
        before_out[...] = jnp.where(is_late, other_map[...], eye)
        behind_out[...] = jnp.where(is_late, jnp.zeros_like(eye), through[...])
        lift_out[...] = jnp.where(is_late, eye[:n], high[level])
        return
    before, behind, lift = refs[:3]
    first = jnp.where(is_late, other_map[...], through[...])
    moved = dot_nn(first, jnp.where(is_late, behind[:n], lift[...]))
    kept = behind[...]
    behind_out[:n] = moved[:n] + jnp.where(is_late, jnp.zeros_like(kept[:n]), kept[:n])
    behind_out[n:] = moved[n:] + kept[n:]
    second = jnp.where(is_late, other_map[:n], lift[...])
    moved = dot_nn(second, jnp.where(is_late, before[:n], high[level]))
    edge = dot_nn(other_map[n:], before[:n]) + before[n:]
    before_out[:n] = jnp.where(is_late, moved, before[:n])
    before_out[n:] = jnp.where(is_late, edge, before[n:])
    lift_out[...] = jnp.where(is_late, lift[...], moved)


def entry_map_body(inner, outer, row_map, twin, chip_map, out):
    n = out.shape[1]
    row = lax.broadcasted_iota(jnp.int32, (n + PAD, n), 0)
    column = lax.broadcasted_iota(jnp.int32, (n + PAD, n), 1)
    eye = jnp.where(row == column, 1.0, 0.0).astype(F32)
    out[...] = jnp.where(late(inner, outer, 3), row_map[...], eye)
    for level, earlier in ((4, twin), (5, chip_map)):
        is_late = late(inner, outer, level)
        moved = dot_nn(earlier[...], out[:n])
        later = out[...]
        out[:n] = jnp.where(is_late, moved[:n], later[:n])
        out[n:] = jnp.where(is_late, moved[n:] + later[n:], later[n:])


def offset_body(outer, first, arrived, near, far, skipped, entry_map, offset_map, entry, offset):
    n = entry_map.shape[1]
    here = jnp.right_shift(outer[0], 2)
    state = dot_nn(far[...], skipped[:n]) + skipped[n:]
    state = jnp.where(here == 3, state, near[...])
    state = jnp.where(here == 1, arrived[...], state)
    state = jnp.where(here == 0, jnp.broadcast_to(first[...], (PAD, n)), state)
    state = dot_nn(state, entry_map[:n]) + entry_map[n:]
    entry[...] = state
    offset[...] = dot_nn(state, offset_map[:n]) + offset_map[n:]


def spread_body(level, inner, outer, own, other, high, out):
    is_late = late(inner, outer, level)
    early_half = jnp.where(is_late, other[...], own[...])
    late_half = jnp.where(is_late, own[...], other[...])
    out[...] = early_half + dot_nn(late_half, high[level])


def ends_body(inner, outer, lift, base_powers, high, *ends):
    ends[0][...] = dot_nn(lift[...], base_powers[0])
    for k in range(len(ends) - 1):
        moved = dot_nn(ends[k][...], high[3 + k])
        ends[k + 1][...] = jnp.where(late(inner, outer, 3 + k), ends[k][...], moved)


def states_body(entry, before, even, odd, obs, gain, pred, filt):
    steps, n = pred.shape
    g = gain[...]
    state = dot_nn(entry[...], before[:n]) + before[n:]

    @pl.loop(0, 4)
    def _(c):
        for i in range(4):
            t = 4 * c + i
            pi = even if i < 2 else odd
            k = 2 * c + i % 2
            predicted = (dot_nn(state, pi[k, :n]) + pi[k, n:])[:1]
            pred[pl.ds(t, 1), :] = predicted
            filt[pl.ds(t, 1), :] = predicted + g * (obs[pl.ds(t, 1), :] - predicted)


def local_body(pred, filt, base_powers, base, shifted):
    steps, n = pred.shape
    local = filt[...] - pred[...]
    shifted[steps:, :] = jnp.zeros((steps, n), F32)
    level = 0
    reach = 1
    while reach < steps:
        shifted[:steps, :] = local
        local = local + dot_nn(shifted[reach : reach + steps, :], base_powers[level])
        reach *= 2
        level += 1
    base[...] = pred[...] + local


def gather_body(inner, outer, entry, behind, base_powers, *refs):
    count = len(refs) // 2
    others, ends, out = refs[:count], refs[count : 2 * count], refs[2 * count]
    n = entry.shape[1]
    inside = dot_nn(entry[...], behind[:n]) + behind[n:]
    value = dot_nn(inside, base_powers[0])
    for k in range(count):
        other = others[k][...]
        other = jnp.where(late(inner, outer, 3 + k), jnp.zeros_like(other), other)
        value = value + dot_nn(other, ends[k][...])
    out[...] = value


def backward_body(inner, outer, other, end, back, base_powers, base, out):
    steps, n = base.shape
    value = other[...]
    value = jnp.where(late(inner, outer, 7), jnp.zeros_like(value), value)
    value = back[...] + dot_nn(value, end[...])
    left = steps - 1 - lax.broadcasted_iota(jnp.int32, (steps, n), 0)
    value = jnp.concatenate([value, value], 0)
    for level in range(base_powers.shape[0] - 1):
        value = jnp.where((left >> level) % 2 == 1, dot_nn(value, base_powers[level]), value)
    out[...] = base[...] + value


def shards(jac, obs, gain_filter, gain_smooth, init_mean):
    steps, n, _ = jac.shape
    inner_count, outer_count = lax.axis_size("inner"), lax.axis_size("outer")
    counts = {"inner": inner_count, "outer": outer_count}
    place = [lax.axis_index(axis).astype(jnp.int32)[None] for axis in ("inner", "outer")]
    gain = gain_filter[None, :]
    first = init_mean[None, :]

    def exchange(total, axis, flip, beside):
        other = lax.ppermute(total, axis, [(i, i ^ flip) for i in range(counts[axis])])
        work = beside()
        return lax.optimization_barrier((other, work))

    with jax.named_scope("compose"):
        total, quarter, half, third, loaded = local_map(place, jac, obs, gain)

    def base_work():
        levels = steps.bit_length()
        return kernel_call(
            base_powers_body,
            (levels, n, n),
            [VMEM],
            (gain_smooth,),
            "base_powers",
            flops=60 * n**3,
            size=24 * n * n,
        )

    aside = []

    def offsets_join(level, own_map, other_map, own, other):
        return kernel_call(
            functools.partial(offsets_join_body, level),
            [(n + PAD, n), (n + PAD, n)],
            [SMEM] * 2 + [VMEM] * 5,
            (*place, own_map, other_map, own, other, high),
            "offsets_join",
            flops=1,
            size=1,
            grant=6,
        )

    def inside(level, other_map, through):
        aside[:] = kernel_call(
            functools.partial(inside_body, level),
            [(n + PAD, n), (n + PAD, n), (n, n)],
            [SMEM] * 2 + [VMEM] * (3 + len(aside)),
            (*place, other_map, through, high, *aside),
            "inside",
            flops=1,
            size=1,
        )

    def partner(value, axis, flip):
        return lax.ppermute(value, axis, [(i, i ^ flip) for i in range(counts[axis])])

    own_maps, other_maps = [total], []
    with jax.named_scope("join_0"):
        other, (pi_even, even, phi) = exchange(
            total,
            "inner",
            1,
            lambda: maps(True, (quarter, half, third), loaded, obs, gain, gain_smooth),
        )
        other_maps.append(other)
        own_maps.append(total_call(0, place, own_maps[0], other))
    with jax.named_scope("join_1"):

        def work():
            base_powers = base_work()
            pi_odd, odd = maps(False, (phi,), loaded, obs, gain, base_powers)
            return base_powers, pi_odd, odd

        other, (base_powers, pi_odd, odd) = exchange(own_maps[1], "inner", 3, work)
        other_maps.append(other)
        own_maps.append(total_call(1, place, own_maps[1], other))
    with jax.named_scope("join_2"):

        def work():
            return kernel_call(
                high_powers_body,
                (7, n, n),
                [VMEM],
                (base_powers,),
                "high_powers",
                flops=72 * n**3,
                size=28 * n * n,
            )

        other = partner(own_maps[2], "inner", 4)
        offsets = kernel_call(
            offset_map_body,
            (n + PAD, n),
            [VMEM] * 3,
            (even, odd, base_powers),
            "offset_map",
            scratch=[pltpu.VMEM((4, n + PAD, n), F32)],
            flops=84 * n**3,
            size=36 * n * n,
        )
        far = partner(offsets, "inner", 1)
        other, high, offsets_done = lax.optimization_barrier((other, work(), offsets))
        other_maps.append(other)
        own_maps.append(total_call(2, place, own_maps[2], other))
    with jax.named_scope("join_3"):

        def work():
            through, joined = offsets_join(0, own_maps[0], other_maps[0], offsets, far)
            return through, joined, partner(joined, "inner", 3)

        other = partner(own_maps[3], "inner", 12)
        through, offsets, far = work()
        other, through = lax.optimization_barrier((other, through))
        other_maps.append(other)
        own_maps.append(total_call(3, place, own_maps[3], other))
    with jax.named_scope("join_core"):
        twin = partner(own_maps[4], "outer", 1)
        own_maps.append(total_call(4, place, own_maps[4], twin))
    with jax.named_scope("join_z"):
        chip_map = partner(own_maps[5], "outer", 2)
        inside(0, other_maps[0], through)
        chip_map, aside[:] = lax.optimization_barrier((chip_map, aside))
        total = total_call(5, place, own_maps[5], chip_map)

    group = outer_count // 4
    def mirror(source, dest):
        return [
            (source * group + z * 2 + c, dest * group + (group // 2 - 1 - z) * 2 + c)
            for z in range(group // 2)
            for c in range(2)
        ]

    def ahead(source, dest):
        return [(source * group + k, dest * group + k) for k in range(group)]

    with jax.named_scope("hop_0"):
        y = hop(0, place, first, first, total)
        arrived = lax.ppermute(y, "outer", ahead(0, 1))
        far, _ = lax.optimization_barrier((far, y))
        through, offsets = offsets_join(1, own_maps[1], other_maps[1], offsets, far)
        far = partner(offsets, "inner", 4)
        arrived, through = lax.optimization_barrier((arrived, through))
    with jax.named_scope("hop_1"):
        y = hop(1, place, first, arrived, total)
        near = lax.ppermute(y, "outer", ahead(1, 2))
        farther = lax.ppermute(y, "outer", mirror(1, 3))
        sent_map, _ = lax.optimization_barrier((total, y))
        skipped = lax.ppermute(sent_map, "outer", ahead(2, 3))
        entry_map = kernel_call(
            entry_map_body,
            (n + PAD, n),
            [SMEM] * 2 + [VMEM] * 3,
            (*place, other_maps[3], twin, chip_map),
            "entry_map",
            flops=1,
            size=1,
        )
        inside(1, other_maps[1], through)
        through, offsets = offsets_join(2, own_maps[2], other_maps[2], offsets, far)
        near, farther, offsets, entry_map, aside[:] = lax.optimization_barrier(
            (near, farther, offsets, entry_map, aside)
        )
    with jax.named_scope("offset"):
        entry, value = kernel_call(
            offset_body,
            [(PAD, n), (PAD, n)],
            [SMEM] + [VMEM] * 7,
            (place[1], first, arrived, near, farther, skipped, entry_map, offsets),
            "offset",
            flops=300 * n * n,
            size=12 * n * n,
        )

    def spread(level, value, other):
        return kernel_call(
            functools.partial(spread_body, level),
            (PAD, n),
            [SMEM] * 2 + [VMEM] * 3,
            (*place, value, other, high),
            "spread",
            flops=96 * n * n,
            size=4 * n * n,
        )

    others = []
    with jax.named_scope("spread_x"):
        other = partner(value, "inner", 12)
        inside(2, other_maps[2], through)
        other, aside[:] = lax.optimization_barrier((other, aside))
        others.append(other)
        value = spread(3, value, other)
    with jax.named_scope("spread_core"):
        others.append(partner(value, "outer", 1))
        value = spread(4, value, others[1])
    with jax.named_scope("spread_z0"):
        other = partner(value, "outer", 2)
        ends = kernel_call(
            ends_body,
            [(n, n)] * 5,
            [SMEM] * 2 + [VMEM] * 3,
            (*place, aside[2], base_powers, high),
            "ends",
            flops=60 * n**3,
            size=36 * n * n,
        )
        other, ends = lax.optimization_barrier((other, ends))
        others.append(other)
        value = spread(5, value, other)
    with jax.named_scope("spread_z1"):
        other = partner(value, "outer", 4)
        pred, filt = kernel_call(
            states_body,
            [(steps, n), (steps, n)],
            [VMEM] * 6,
            (entry, aside[0], pi_even, pi_odd, obs, gain),
            "states",
            flops=17 * 96 * n * n,
            size=68 * n * n,
        )
        other, pred = lax.optimization_barrier((other, pred))
        others.append(other)
        value = spread(6, value, other)
    with jax.named_scope("spread_z2"):
        other = partner(value, "outer", 12)
        base = kernel_call(
            local_body,
            (steps, n),
            [VMEM] * 3,
            (pred, filt, base_powers),
            "local",
            scratch=[pltpu.VMEM((2 * steps, n), F32)],
            flops=8 * 96 * n * n,
            size=16 * n * n,
        )
        back = kernel_call(
            gather_body,
            (PAD, n),
            [SMEM] * 2 + [VMEM] * 11,
            (*place, entry, aside[1], base_powers, *others, *ends[:4]),
            "gather",
            flops=600 * n * n,
            size=20 * n * n,
        )
        other, base, back = lax.optimization_barrier((other, base, back))
    with jax.named_scope("backward"):
        smoothed = kernel_call(
            backward_body,
            (steps, n),
            [SMEM] * 2 + [VMEM] * 5,
            (*place, other, ends[4], back, base_powers, base),
            "backward",
            flops=600 * n * n,
            size=24 * n * n,
        )
    return (filt, smoothed)


def solution(mesh):
    return jax.shard_map(
        shards,
        mesh=mesh,
        in_specs=(P(("outer", "inner"), None, None), P(("outer", "inner"), None), P(), P(), P()),
        out_specs=(P(("outer", "inner"), None), P(("outer", "inner"), None)),
        check_vma=False,
    )
```
